128 devices in a mesh: tok: 16 (over x, y), head: 8 (over z, core).
Axes of the slice: x: 4, y: 4, z: 4, core: 2. Of those that a mesh axis runs over, the one named last changes fastest.
Arguments:
- hidden_in: bfloat16 [16384, 2048], P(('tok', 'head')), may hold values from -6 to 6
- attn_gain: float32 [2048], replicated, may hold values from 0.1 to 1.9
- w_qkv: bfloat16 [2048, 2560], P('tok'), may hold values from -0.125 to 0.125
- w_out: bfloat16 [2048, 2048], P('tok'), may hold values from -0.125 to 0.125
- mlp_gain: float32 [2048], replicated, may hold values from 0.1 to 1.9
- w_gate: bfloat16 [2048, 5632], P('tok', 'head'), may hold values from -0.125 to 0.125
- w_up: bfloat16 [2048, 5632], P('tok', 'head'), may hold values from -0.125 to 0.125
- w_down: bfloat16 [5632, 2048], P('head', 'tok'), may hold values from -0.078125 to 0.078125
- cache_kv: bfloat16 [32, 8, 4352, 128], P('tok', 'head'), may hold values from -240 to 240
- cached_len: int32 [32], P('tok'), may hold values from 0 to 8192, as said below
Outputs:
- hidden_out: bfloat16 [16384, 2048], P(('tok', 'head'))
- cache_out: bfloat16 [32, 8, 4352, 128], P('tok', 'head')
The draws below stay inside these ranges and needn't reach their ends.
Inputs may be any that keep to these rules, and one draw needn't show every extreme that they name: `cached_len`: some request has exactly 8192 cached positions.
All inputs are finite; a program needn't handle non-finite values.
Results may differ from the reference program's by a relative error of at most 0.014.
Values may be sent and summed in bfloat16 or wider, within the bound.
No kernel may reach another device: no remote copies, remote signals or barrier semaphores. Data moves between devices by JAX's collectives and lax.ppermute only.
A program may use at most 128 MiB of HBM per device.

```python
import jax
import jax.numpy as jnp
from jax import lax

D = 2048
HEADS = 32
KV_HEADS = 4
HEAD_DIM = 64
FF = 5632
S_NEW = 512
CACHE_MAX = 8192
REQUESTS = 32
TOKENS = 16384
KV_PARTS = 8
POSITIONS = 8704
BLOCK_POS = 4352
QW = 2048
QKV_W = 2560
N_HEAD = 8


def draw_cache_kv(key, part):
    key_one = jax.random.fold_in(jax.random.fold_in(key, 11), 0)
    shape = (REQUESTS, KV_PARTS, BLOCK_POS, 2 * HEAD_DIM)
    base = jnp.clip(jax.random.normal(key_one, shape, jnp.float32), -6.0, 6.0)
    return base.astype(jnp.bfloat16)


def draw_cached_len(key, part):
    key_one, key_two = jax.random.split(jax.random.fold_in(key, 23))
    lengths = jax.random.randint(key_one, (REQUESTS,), 0, CACHE_MAX + 1)
    longest = jax.random.randint(key_two, (), 0, REQUESTS)
    return jnp.where(jnp.arange(REQUESTS) == longest, CACHE_MAX, lengths).astype(jnp.int32)


def levels(stream_key, shape, pieces, low, top_value):
    loudness, own = 1.0, jax.random.fold_in(stream_key, 6)
    for position, parts in pieces:
        steps = jnp.exp(jax.random.uniform(jax.random.fold_in(own, position), (parts,), jnp.float32, low / len(pieces), top_value / len(pieces)))
        loudness = loudness * jnp.repeat(steps, shape[position] // parts).reshape([-1 if axis == position else 1 for axis in range(len(shape))])
    return loudness


def bell_draw(stream_key, dims, scale, most, pieces=(), kind=jnp.bfloat16):
    level = levels(stream_key, dims, pieces, -0.22, 0.18) if pieces else 1.0
    values = jax.random.normal(stream_key, dims, jnp.float32) * scale * level
    return jnp.minimum(jnp.maximum(values, -most), most).astype(kind)


def setup_inputs(seed: int = 0) -> dict:
    arg_keys = jax.random.split(jax.random.key(seed), 11)
    return {
        "hidden_in": bell_draw(arg_keys[0], (TOKENS, D), 1.0, 6.0, ((0, 128),)),
        "attn_gain": jnp.clip(1.0 + 0.18 * jax.random.normal(arg_keys[1], (D,), jnp.float32), 0.1, 1.9),
        "w_qkv": bell_draw(arg_keys[2], (D, QKV_W), D ** -0.5, 0.125, ((0, 16),)),
        "w_out": bell_draw(arg_keys[3], (QW, D), QW ** -0.5, 0.125, ((0, 16),)),
        "mlp_gain": jnp.clip(1.0 + 0.18 * jax.random.normal(arg_keys[4], (D,), jnp.float32), 0.1, 1.9),
        "w_gate": bell_draw(arg_keys[5], (D, FF), D ** -0.5, 0.125, ((0, 16), (1, 8))),
        "w_up": bell_draw(arg_keys[6], (D, FF), D ** -0.5, 0.125, ((0, 16), (1, 8))),
        "w_down": bell_draw(arg_keys[7], (FF, D), FF ** -0.5, 0.078125, ((0, 8), (1, 16))),
        "cache_kv": draw_cache_kv(jax.random.fold_in(arg_keys[10], 71), 0),
        "cached_len": draw_cached_len(jax.random.fold_in(arg_keys[10], 71), 0),
    }


ROPE_BASE = 10000.0

def mean_norm(values, gain):
    widened = values.astype(jnp.float32)
    spread = lax.optimization_barrier(jnp.mean(widened * widened, axis=-1, keepdims=True))
    return (widened * lax.rsqrt(spread + 1e-05) * gain).astype(jnp.bfloat16)

def rotate(values, positions):
    half_dim = values.shape[-1] // 2
    frequency = ROPE_BASE ** (-jnp.arange(half_dim).astype(values.dtype) * 2.0 / values.shape[-1])
    angles = positions[..., None].astype(values.dtype) * frequency
    first_half = values[..., :half_dim]
    second_half = values[..., half_dim:]
    cosine = jnp.cos(angles)
    sine_vals = jnp.sin(angles)
    return jnp.concatenate([first_half * cosine - second_half * sine_vals, second_half * cosine + first_half * sine_vals], axis=-1)

def attend_request(inputs):
    queries, cache_rows, length = inputs
    group = HEADS // KV_HEADS
    query_pos = length + jnp.arange(S_NEW).astype(jnp.int32)
    key_pos = jnp.arange(POSITIONS).astype(jnp.int32)
    allowed = key_pos[None, :] <= query_pos[:, None]

    def one_head(pair):
        head_queries, head_cache = pair
        keys = head_cache[:, :HEAD_DIM].astype(jnp.float32)
        values = head_cache[:, HEAD_DIM:].astype(jnp.float32)
        scores = jnp.einsum('hqd,pd->hqp', head_queries.astype(jnp.float32), keys) * HEAD_DIM ** (-0.5)
        scores = jnp.where(allowed[None], scores, -jnp.inf)
        row_top = lax.optimization_barrier(jnp.max(scores, axis=-1, keepdims=True))
        exps = jnp.exp(scores - row_top)
        row_total = lax.optimization_barrier(jnp.sum(exps, axis=-1))
        weights = lax.optimization_barrier(exps.astype(jnp.bfloat16)).astype(jnp.float32)
        mixed = jnp.einsum('hqp,pd->hqd', weights, values)
        return (mixed / row_total[..., None]).astype(jnp.bfloat16)
    grouped = queries.reshape(S_NEW, KV_HEADS, group, HEAD_DIM).transpose(1, 2, 0, 3)
    result_rows = lax.map(one_head, (grouped, cache_rows))
    return result_rows.transpose(2, 0, 1, 3).reshape(S_NEW, QW)

def reference(hidden_in, attn_gain, w_qkv, w_out, mlp_gain, w_gate, w_up, w_down, cache_kv, cached_len):
    normed = mean_norm(hidden_in, attn_gain)
    projected = jnp.dot(normed, w_qkv, preferred_element_type=jnp.float32)
    token_ids = jnp.arange(TOKENS).astype(jnp.int32)
    positions = cached_len[token_ids // S_NEW] + token_ids % S_NEW
    kv_width = KV_HEADS * HEAD_DIM
    queries = rotate(projected[:, :QW].reshape(TOKENS, HEADS, HEAD_DIM), positions[:, None]).astype(jnp.bfloat16)
    keys_new = rotate(projected[:, QW:QW + kv_width].reshape(TOKENS, KV_HEADS, HEAD_DIM), positions[:, None]).astype(jnp.bfloat16)
    values_new = projected[:, QW + kv_width:].reshape(TOKENS, KV_HEADS, HEAD_DIM).astype(jnp.bfloat16)
    new_rows = jnp.concatenate([keys_new, values_new], axis=-1).reshape(REQUESTS, S_NEW, KV_HEADS, 2 * HEAD_DIM).transpose(0, 2, 1, 3)
    whole_cache = cache_kv.reshape(REQUESTS, KV_HEADS, POSITIONS, 2 * HEAD_DIM)

    def append_one(cache_rows, fresh_rows, length):
        zero_index = jnp.zeros((), jnp.int32)
        return lax.dynamic_update_slice(cache_rows, fresh_rows, (zero_index, length.astype(jnp.int32), zero_index))
    whole_cache = jax.vmap(append_one)(whole_cache, new_rows, cached_len)
    cache_out = whole_cache.reshape(REQUESTS, KV_PARTS, BLOCK_POS, 2 * HEAD_DIM)
    attended = lax.map(attend_request, (queries.reshape(REQUESTS, S_NEW, HEADS, HEAD_DIM), whole_cache, cached_len))
    attended = attended.reshape(TOKENS, QW)
    residual = (hidden_in.astype(jnp.float32) + jnp.dot(attended, w_out, preferred_element_type=jnp.float32)).astype(jnp.bfloat16)
    normed2 = mean_norm(residual, mlp_gain)
    gate_sum = jnp.dot(normed2, w_gate, preferred_element_type=jnp.float32)
    up_sum = jnp.dot(normed2, w_up, preferred_element_type=jnp.float32)
    hidden = (jax.nn.silu(gate_sum) * up_sum).astype(jnp.bfloat16)
    group_units = FF // N_HEAD
    total = residual.astype(jnp.float32)
    for group_index in range(N_HEAD):
        unit_part = jnp.dot(hidden[:, group_index * group_units:(group_index + 1) * group_units], w_down[group_index * group_units:(group_index + 1) * group_units], preferred_element_type=jnp.float32)
        total = total + lax.optimization_barrier(unit_part.astype(jnp.bfloat16)).astype(jnp.float32)
    hidden_out = total.astype(jnp.bfloat16)
    return (hidden_out, cache_out)
```

```python
import jax
import jax.numpy as jnp
from jax import lax
from jax.experimental import pallas as pl
from jax.experimental.pallas import tpu as pltpu
from jax.sharding import PartitionSpec as P

HEADS = 32
KV_HEADS = 4
HEAD_DIM = 64
S_NEW = 512
ROPE_BASE = 10000.0

KEYS = 512
ALIGN = 16
WINDOW = S_NEW + ALIGN
VROWS = HEAD_DIM + 16


def mean_norm(values, gain):
    widened = values.astype(jnp.float32)
    spread = jnp.mean(widened * widened, axis=-1, keepdims=True)
    return (widened * lax.rsqrt(spread + 1e-05) * gain).astype(jnp.bfloat16)


def contract(left_rows, right_rows):
    return jnp.dot(left_rows, right_rows, preferred_element_type=jnp.float32)


def attention_kernel(
    lens_ref, part_ref, x_ref, w_ref, cos_ref, sin_ref, own_hbm, other_hbm,
    out_ref, cache_hbm, kv_ref, qt_ref, new_ref, acc_ref, top_ref, load_sems, store_sems,
):
    req_count, block_pos, lanes = own_hbm.shape
    heads_dev = qt_ref.shape[0]
    half = HEAD_DIM // 2
    own_at = pl.multiple_of(part_ref[0] * block_pos, ALIGN)
    other_at = pl.multiple_of((1 - part_ref[0]) * block_pos, ALIGN)

    def loads(r):
        return (
            pltpu.make_async_copy(
                own_hbm.at[r], kv_ref.at[r, pl.ds(own_at, block_pos)], load_sems.at[r, 0]
            ),
            pltpu.make_async_copy(
                other_hbm.at[r], kv_ref.at[r, pl.ds(other_at, block_pos)], load_sems.at[r, 1]
            ),
        )

    def store(r):
        return pltpu.make_async_copy(
            kv_ref.at[r, pl.ds(own_at, block_pos)], cache_hbm.at[r], store_sems.at[r]
        )

    for r in range(req_count):
        for copy in loads(r):
            copy.start()

    cosine = cos_ref[...]
    sine = sin_ref[...]
    x = x_ref[...]

    def turn(block, scale):
        first = block[:half]
        second = block[half:]
        return jnp.concatenate(
            [(first * cosine - second * sine) * scale, (second * cosine + first * sine) * scale],
            axis=0,
        )

    for pair in range(heads_dev // 2):
        flipped = contract(x, w_ref[:, pair * lanes : (pair + 1) * lanes]).T
        for one in range(2):
            rows = turn(flipped[one * HEAD_DIM : (one + 1) * HEAD_DIM], HEAD_DIM**-0.5)
            qt_ref[2 * pair + one] = jnp.concatenate([rows, jnp.zeros_like(rows)], axis=0).astype(
                jnp.bfloat16
            )
    q_lanes = heads_dev * HEAD_DIM
    flipped = contract(x, w_ref[:, q_lanes : q_lanes + lanes]).T
    fresh = jnp.concatenate([turn(flipped[:HEAD_DIM], 1.0), flipped[HEAD_DIM:]], axis=0)
    new_ref[...] = fresh.T.astype(jnp.bfloat16)

    for r in range(req_count):
        length = lens_ref[r]
        for copy in loads(r):
            copy.wait()
        shift = length % ALIGN
        window_at = pl.multiple_of(length - shift, ALIGN)
        row = lax.broadcasted_iota(jnp.int32, (WINDOW, S_NEW), 0)
        col = lax.broadcasted_iota(jnp.int32, (WINDOW, S_NEW), 1)
        pick = (row - shift == col).astype(jnp.float32).astype(jnp.bfloat16)
        moved = contract(pick, new_ref[r * S_NEW : (r + 1) * S_NEW])
        row = lax.broadcasted_iota(jnp.int32, (WINDOW, lanes), 0)
        inside = (row >= shift) & (row < shift + S_NEW)
        old = kv_ref[r, pl.ds(window_at, WINDOW)].astype(jnp.float32)
        kv_ref[r, pl.ds(window_at, WINDOW)] = jnp.where(inside, moved, old).astype(jnp.bfloat16)
        store(r).start()

    for r in range(req_count):
        length = lens_ref[r]

        def step(index, masked, first):
            at = pl.multiple_of(index * KEYS, KEYS)
            block = kv_ref[r, pl.ds(at, KEYS)]
            lane = lax.broadcasted_iota(jnp.int32, (KEYS, lanes), 1)
            ones = jnp.where(lane < HEAD_DIM, 1.0, block.astype(jnp.float32))
            values = ones.T[HEAD_DIM - 16 :].astype(jnp.bfloat16)
            for h in range(heads_dev):
                scores = contract(block, qt_ref[h, :, r * S_NEW : (r + 1) * S_NEW])
                if masked:
                    key = lax.broadcasted_iota(jnp.int32, scores.shape, 0) + (index * KEYS - length)
                    query = lax.broadcasted_iota(jnp.int32, scores.shape, 1)
                    scores = jnp.where(key <= query, scores, -jnp.inf)
                top = jnp.max(scores, axis=0, keepdims=True)
                if not first:
                    old_top = top_ref[h]
                    top = jnp.maximum(top, old_top)
                exps = jnp.exp(scores - top).astype(jnp.bfloat16)
                product = contract(values, exps)
                if not first:
                    product = product + acc_ref[h] * jnp.exp(old_top - top)
                acc_ref[h] = product
                top_ref[h] = top

        tail = length // KEYS
        step(tail, True, True)

        @pl.when(length % KEYS > 0)
        def _():
            step(tail + 1, True, False)

        def full(index, carry):
            step(index, False, False)
            return carry

        lax.fori_loop(0, tail, full, 0)
        for pair in range(heads_dev // 2):
            sides = [
                acc_ref[h][16:] / acc_ref[h][:1] for h in (2 * pair, 2 * pair + 1)
            ]
            out_ref[r * S_NEW : (r + 1) * S_NEW, pair * lanes : (pair + 1) * lanes] = (
                jnp.concatenate(sides, axis=0).T.astype(jnp.bfloat16)
            )

    for r in range(req_count):
        store(r).wait()


def attention(lens, part, x, w, cosine, sine, own, other, interpret=False):
    req_count, block_pos, lanes = own.shape
    rows = x.shape[0]
    heads_dev = (w.shape[1] - lanes) // HEAD_DIM
    whole = pl.BlockSpec(memory_space=pltpu.VMEM)
    scalar = pl.BlockSpec(memory_space=pltpu.SMEM)
    return pl.pallas_call(
        attention_kernel,
        out_shape=(
            jax.ShapeDtypeStruct((rows, heads_dev * HEAD_DIM), jnp.bfloat16),
            jax.ShapeDtypeStruct(own.shape, jnp.bfloat16),
        ),
        in_specs=[
            scalar, scalar, whole, whole, whole, whole,
            pl.BlockSpec(memory_space=pl.ANY), pl.BlockSpec(memory_space=pl.ANY),
        ],
        out_specs=(whole, pl.BlockSpec(memory_space=pl.ANY)),
        scratch_shapes=[
            pltpu.VMEM((req_count, 2 * block_pos + ALIGN, lanes), jnp.bfloat16),
            pltpu.VMEM((heads_dev, lanes, rows), jnp.bfloat16),
            pltpu.VMEM((rows, lanes), jnp.bfloat16),
            pltpu.VMEM((heads_dev, VROWS, S_NEW), jnp.float32),
            pltpu.VMEM((heads_dev, 1, S_NEW), jnp.float32),
            pltpu.SemaphoreType.DMA((req_count, 2)),
            pltpu.SemaphoreType.DMA((req_count,)),
        ],
        compiler_params=pltpu.CompilerParams(vmem_limit_bytes=48 << 20),
        name="attention",
        interpret=interpret,
    )(lens, part, x, w, cosine, sine, own, other)


def angles_of(cached_len):
    half = HEAD_DIM // 2
    frequency = ROPE_BASE ** (-jnp.arange(half).astype(jnp.float32) * 2.0 / HEAD_DIM)
    positions = (cached_len[:, None] + jnp.arange(S_NEW)[None, :]).reshape(-1)
    angles = frequency[:, None] * positions.astype(jnp.float32)[None, :]
    return jnp.cos(angles), jnp.sin(angles)


def per_device(
    hidden_in, attn_gain, w_qkv, w_out, mlp_gain, w_gate, w_up, w_down, cache_kv, cached_len
):
    head_count = lax.axis_size("head")
    head_index = lax.axis_index("head")
    q_width = HEADS * HEAD_DIM
    kv_width = KV_HEADS * HEAD_DIM
    q_dev = q_width // head_count
    split_count = head_count // KV_HEADS
    part_index = head_index % split_count
    kv_head = head_index // split_count

    own = cache_kv[:, 0]
    other = lax.ppermute(own, "head", [(i, i ^ 1) for i in range(head_count)])
    normed = mean_norm(hidden_in, attn_gain)
    group_x = lax.all_gather(normed, "head", axis=0, tiled=True)
    columns = jnp.concatenate(
        [
            lax.dynamic_slice_in_dim(w_qkv, head_index * q_dev, q_dev, 1),
            lax.dynamic_slice_in_dim(w_qkv, q_width + kv_head * HEAD_DIM, HEAD_DIM, 1),
            lax.dynamic_slice_in_dim(w_qkv, q_width + kv_width + kv_head * HEAD_DIM, HEAD_DIM, 1),
        ],
        axis=1,
    )
    group_w = lax.all_gather(columns, "tok", axis=0, tiled=True)
    cosine, sine = angles_of(cached_len)
    attended, cache_new = attention(
        cached_len, part_index.reshape(1), group_x, group_w, cosine, sine, own, other
    )
    back_rows = lax.all_to_all(attended, "head", split_axis=0, concat_axis=1, tiled=True)
    projected_out = contract(back_rows, lax.all_gather(w_out, "tok", axis=0, tiled=True))
    residual = (hidden_in.astype(jnp.float32) + projected_out).astype(jnp.bfloat16)
    normed2 = mean_norm(residual, mlp_gain)
    gathered2 = lax.all_gather(normed2, "head", axis=0, tiled=True)
    gate_sum = contract(gathered2, lax.all_gather(w_gate, "tok", axis=0, tiled=True))
    up_sum = contract(gathered2, lax.all_gather(w_up, "tok", axis=0, tiled=True))
    hidden = (jax.nn.silu(gate_sum) * up_sum).astype(jnp.bfloat16)
    unit_terms = contract(hidden, lax.all_gather(w_down, "tok", axis=1, tiled=True))
    summed = lax.psum_scatter(
        unit_terms.astype(jnp.bfloat16), "head", scatter_dimension=0, tiled=True
    ).astype(jnp.float32)
    hidden_out = (residual.astype(jnp.float32) + summed).astype(jnp.bfloat16)
    return (hidden_out, cache_new[:, None])


def solution(mesh):
    return jax.shard_map(
        per_device,
        mesh=mesh,
        in_specs=(
            P(("tok", "head"), None),
            P(),
            P("tok", None),
            P("tok", None),
            P(),
            P("tok", "head"),
            P("tok", "head"),
            P("head", "tok"),
            P("tok", "head", None, None),
            P("tok"),
        ),
        out_specs=(P(("tok", "head"), None), P("tok", "head", None, None)),
        check_vma=False,
    )
```

```python
import jax
import jax.numpy as jnp
from jax import lax
from jax.experimental import pallas as pl
from jax.experimental.pallas import tpu as pltpu
from jax.sharding import PartitionSpec as P

HEADS = 32
KV_HEADS = 4
HEAD_DIM = 64
S_NEW = 512
ROPE_BASE = 10000.0

KEYS = 512
ALIGN = 16
WINDOW = S_NEW + ALIGN
VROWS = HEAD_DIM + 16


Z = 4
FF_PAIR = 128


def mean_norm(values, gain):
    widened = values.astype(jnp.float32)
    spread = jnp.mean(widened * widened, axis=-1, keepdims=True)
    return (widened * lax.rsqrt(spread + 1e-05) * gain).astype(jnp.bfloat16)


def contract(left_rows, right_rows):
    return jnp.dot(left_rows, right_rows, preferred_element_type=jnp.float32)


def exchange(array):
    return lax.ppermute(array, "head", [(i, i ^ 1) for i in range(lax.axis_size("head"))])


def along_z(array, distance):
    count = lax.axis_size("head")
    return lax.ppermute(array, "head", [(i, (i + 2 * distance) % count) for i in range(count)])


def along_tok(array, distance, major):
    moves = []
    for i in range(lax.axis_size("tok")):
        x, y = i // Z, i % Z
        moves.append((i, (x + distance) % Z * Z + y if major else x * Z + (y + distance) % Z))
    return lax.ppermute(array, "tok", moves)


def gather_head(array):
    same_core = [array] + [along_z(array, d) for d in range(1, Z)]
    return same_core + [exchange(piece) for piece in same_core]


def sources():
    head_index = lax.axis_index("head")
    z, core = head_index // 2, head_index % 2
    chips = (z - jnp.arange(Z)) % Z * 2
    return jnp.concatenate([chips + core, chips + 1 - core]).astype(jnp.int32)


def attend(length, kv_ref, qt_ref, acc_ref, top_ref, out_ref):
    heads_dev = qt_ref.shape[0]
    lanes = kv_ref.shape[1]

    def step(index, masked, first):
        at = pl.multiple_of(index * KEYS, KEYS)
        block = kv_ref[pl.ds(at, KEYS)]
        lane = lax.broadcasted_iota(jnp.int32, (KEYS, lanes), 1)
        ones = jnp.where(lane < HEAD_DIM, 1.0, block.astype(jnp.float32))
        values = ones.T[HEAD_DIM - 16 :].astype(jnp.bfloat16)
        for h in range(heads_dev):
            scores = contract(block, qt_ref[h])
            if masked:
                key = lax.broadcasted_iota(jnp.int32, scores.shape, 0) + (index * KEYS - length)
                query = lax.broadcasted_iota(jnp.int32, scores.shape, 1)
                scores = jnp.where(key <= query, scores, -jnp.inf)
            top = jnp.max(scores, axis=0, keepdims=True)
            if not first:
                old_top = top_ref[h]
                top = jnp.maximum(top, old_top)
            exps = jnp.exp(scores - top).astype(jnp.bfloat16)
            product = contract(values, exps)
            if not first:
                product = product + acc_ref[h] * jnp.exp(old_top - top)
            acc_ref[h] = product
            top_ref[h] = top

    tail = length // KEYS
    step(tail, True, True)

    @pl.when(length % KEYS > 0)
    def _():
        step(tail + 1, True, False)

    def full(index, carry):
        step(index, False, False)
        return carry

    lax.fori_loop(0, tail, full, 0)
    for pair in range(heads_dev // 2):
        sides = [acc_ref[h][16:] / acc_ref[h][:1] for h in (2 * pair, 2 * pair + 1)]
        out_ref[:, pair * lanes : (pair + 1) * lanes] = (
            jnp.concatenate(sides, axis=0).T.astype(jnp.bfloat16)
        )


def first_kernel(
    lens_ref, part_ref, src_ref, tok_ref, gain_ref, cos_ref, sin_ref, *refs
):
    x_pieces = refs[: 2 * Z]
    w_pieces = refs[2 * Z : 3 * Z]
    own_hbm, other_hbm = refs[3 * Z : 3 * Z + 2]
    out_ref, later_qt_ref, later_kv_hbm, cache_hbm, rows_hbm = refs[3 * Z + 2 : 3 * Z + 7]
    x_ref, w_ref, kv_ref, qt_ref, new_ref, acc_ref, top_ref = refs[3 * Z + 7 : 3 * Z + 14]
    x_sems, w_sems, load_sems, store_sems = refs[3 * Z + 14 :]
    req_count, block_pos, lanes = own_hbm.shape
    heads_dev = qt_ref.shape[0]
    half = HEAD_DIM // 2
    piece_rows = x_pieces[0].shape[0]
    own_at = pl.multiple_of(part_ref[0] * block_pos, ALIGN)
    other_at = pl.multiple_of((1 - part_ref[0]) * block_pos, ALIGN)

    def x_load(i):
        at = pl.multiple_of(src_ref[i] * piece_rows, piece_rows)
        return pltpu.make_async_copy(x_pieces[i], x_ref.at[pl.ds(at, piece_rows)], x_sems.at[i])

    def w_load(i, j):
        rows = w_pieces[0].shape[1]
        at = pl.multiple_of(tok_ref[i * Z + j] * rows, rows)
        return pltpu.make_async_copy(
            w_pieces[i].at[j], w_ref.at[pl.ds(at, rows)], w_sems.at[i * Z + j]
        )

    def loads(r):
        return (
            pltpu.make_async_copy(
                own_hbm.at[r], kv_ref.at[r, pl.ds(own_at, block_pos)], load_sems.at[r, 0]
            ),
            pltpu.make_async_copy(
                other_hbm.at[r], kv_ref.at[r, pl.ds(other_at, block_pos)], load_sems.at[r, 1]
            ),
        )

    def stores(r):
        copies = [
            pltpu.make_async_copy(
                kv_ref.at[r, pl.ds(own_at, block_pos)], cache_hbm.at[r], store_sems.at[r]
            )
        ]
        if r:
            copies.append(pltpu.make_async_copy(kv_ref.at[r], later_kv_hbm, store_sems.at[2]))
        return copies

    for i in range(2 * Z):
        x_load(i).start()
    for i in range(Z):
        for j in range(Z):
            w_load(i, j).start()
    for r in range(req_count):
        for copy in loads(r):
            copy.start()
    for i in range(2 * Z):
        x_load(i).wait()
    keep = pltpu.make_async_copy(x_ref, rows_hbm, store_sems.at[3])
    keep.start()
    for i in range(Z):
        for j in range(Z):
            w_load(i, j).wait()

    q_lanes = heads_dev * HEAD_DIM
    gain = gain_ref[...]
    for r in range(req_count):
        here = slice(r * S_NEW, (r + 1) * S_NEW)
        cosine = cos_ref[:, here]
        sine = sin_ref[:, here]

        def turn(block, scale):
            first = block[:half]
            second = block[half:]
            return jnp.concatenate(
                [
                    (first * cosine - second * sine) * scale,
                    (second * cosine + first * sine) * scale,
                ],
                axis=0,
            )

        normed = mean_norm(x_ref[here], gain)
        projected = contract(normed, w_ref[...])
        for pair in range(heads_dev // 2):
            flipped = projected[:, pair * lanes : (pair + 1) * lanes].T
            for one in range(2):
                rows = turn(flipped[one * HEAD_DIM : (one + 1) * HEAD_DIM], HEAD_DIM**-0.5)
                rows = jnp.concatenate([rows, jnp.zeros_like(rows)], axis=0).astype(jnp.bfloat16)
                if r:
                    later_qt_ref[2 * pair + one] = rows
                else:
                    qt_ref[2 * pair + one] = rows
        flipped = projected[:, q_lanes:].T
        fresh = jnp.concatenate([turn(flipped[:HEAD_DIM], 1.0), flipped[HEAD_DIM:]], axis=0)
        new_ref[r] = fresh.T.astype(jnp.bfloat16)

    for r in range(req_count):
        length = lens_ref[r]
        for copy in loads(r):
            copy.wait()
        shift = length % ALIGN
        window_at = pl.multiple_of(length - shift, ALIGN)
        row = lax.broadcasted_iota(jnp.int32, (WINDOW, S_NEW), 0)
        col = lax.broadcasted_iota(jnp.int32, (WINDOW, S_NEW), 1)
        pick = (row - shift == col).astype(jnp.float32).astype(jnp.bfloat16)
        moved = contract(pick, new_ref[r])
        row = lax.broadcasted_iota(jnp.int32, (WINDOW, lanes), 0)
        inside = (row >= shift) & (row < shift + S_NEW)
        old = kv_ref[r, pl.ds(window_at, WINDOW)].astype(jnp.float32)
        kv_ref[r, pl.ds(window_at, WINDOW)] = jnp.where(inside, moved, old).astype(jnp.bfloat16)
        for copy in stores(r):
            copy.start()

    attend(lens_ref[0], kv_ref.at[0], qt_ref, acc_ref, top_ref, out_ref)
    for r in range(req_count):
        for copy in stores(r):
            copy.wait()
    keep.wait()


def attend_first(lens, part, src, tok_order, gain, cosine, sine, x_pieces, w_pieces, own, other):
    req_count, block_pos, lanes = own.shape
    piece_rows, width = x_pieces[0].shape
    rows = piece_rows * len(x_pieces)
    w_rows = w_pieces[0].shape[0] * w_pieces[0].shape[1] * len(w_pieces)
    w_cols = w_pieces[0].shape[2]
    heads_dev = (w_cols - lanes) // HEAD_DIM
    positions = 2 * block_pos + ALIGN
    whole = pl.BlockSpec(memory_space=pltpu.VMEM)
    scalar = pl.BlockSpec(memory_space=pltpu.SMEM)
    remote = pl.BlockSpec(memory_space=pl.ANY)
    return pl.pallas_call(
        first_kernel,
        out_shape=(
            jax.ShapeDtypeStruct((S_NEW, heads_dev * HEAD_DIM), jnp.bfloat16),
            jax.ShapeDtypeStruct((heads_dev, lanes, S_NEW), jnp.bfloat16),
            jax.ShapeDtypeStruct((positions, lanes), jnp.bfloat16),
            jax.ShapeDtypeStruct(own.shape, jnp.bfloat16),
            jax.ShapeDtypeStruct((rows, width), jnp.bfloat16),
        ),
        in_specs=[scalar] * 4 + [whole] * 3 + [remote] * (len(x_pieces) + len(w_pieces) + 2),
        out_specs=(whole, whole, remote, remote, remote),
        scratch_shapes=[
            pltpu.VMEM((rows, width), jnp.bfloat16),
            pltpu.VMEM((w_rows, w_cols), jnp.bfloat16),
            pltpu.VMEM((req_count, positions, lanes), jnp.bfloat16),
            pltpu.VMEM((heads_dev, lanes, S_NEW), jnp.bfloat16),
            pltpu.VMEM((req_count, S_NEW, lanes), jnp.bfloat16),
            pltpu.VMEM((heads_dev, VROWS, S_NEW), jnp.float32),
            pltpu.VMEM((heads_dev, 1, S_NEW), jnp.float32),
            pltpu.SemaphoreType.DMA((2 * Z,)),
            pltpu.SemaphoreType.DMA((Z * Z,)),
            pltpu.SemaphoreType.DMA((req_count, 2)),
            pltpu.SemaphoreType.DMA((4,)),
        ],
        compiler_params=pltpu.CompilerParams(vmem_limit_bytes=56 << 20),
        cost_estimate=pl.CostEstimate(
            flops=10**10, transcendentals=10**8, bytes_accessed=40 * 10**6
        ),
        name="attend_first",
    )(lens, part, src, tok_order, gain, cosine, sine, *x_pieces, *w_pieces, own, other)


def second_kernel(len_ref, qt_ref, kv_ref, out_ref, acc_ref, top_ref):
    attend(len_ref[1], kv_ref, qt_ref, acc_ref, top_ref, out_ref)


def attend_second(lens, qt, kv):
    heads_dev = qt.shape[0]
    whole = pl.BlockSpec(memory_space=pltpu.VMEM)
    return pl.pallas_call(
        second_kernel,
        out_shape=jax.ShapeDtypeStruct((S_NEW, heads_dev * HEAD_DIM), jnp.bfloat16),
        in_specs=[pl.BlockSpec(memory_space=pltpu.SMEM), whole, whole],
        out_specs=whole,
        scratch_shapes=[
            pltpu.VMEM((heads_dev, VROWS, S_NEW), jnp.float32),
            pltpu.VMEM((heads_dev, 1, S_NEW), jnp.float32),
        ],
        compiler_params=pltpu.CompilerParams(vmem_limit_bytes=40 << 20),
        cost_estimate=pl.CostEstimate(
            flops=10**10, transcendentals=10**8, bytes_accessed=40 * 10**6
        ),
        name="attend_second",
    )(lens, qt, kv)


def out_kernel(src_ref, gain_ref, w_ref, rows_ref, *refs):
    pieces = refs[: 2 * Z]
    residual_ref, normed_ref, att_ref, sems = refs[2 * Z :]
    index = pl.program_id(0)
    tile = w_ref.shape[1]

    @pl.when(index == 0)
    def _():
        copies = [
            pltpu.make_async_copy(pieces[i], att_ref.at[src_ref[i]], sems.at[i])
            for i in range(2 * Z)
        ]
        for copy in copies:
            copy.start()
        for copy in copies:
            copy.wait()

    attended = jnp.concatenate([att_ref[i] for i in range(2 * Z)], axis=1)
    total = rows_ref[...].astype(jnp.float32) + contract(attended, w_ref[...])
    for i in range(residual_ref.shape[1] // tile):

        @pl.when(index == i)
        def _():
            residual_ref[:, i * tile : (i + 1) * tile] = total.astype(jnp.bfloat16)

    @pl.when(index == pl.num_programs(0) - 1)
    def _():
        normed_ref[...] = mean_norm(residual_ref[...], gain_ref[...])


def project_out(src, gain, weights, rows, pieces, request):
    piece_rows, piece_width = pieces[0].shape
    width = rows.shape[1]
    tile = 512
    remote = pl.BlockSpec(memory_space=pl.ANY)
    return pl.pallas_call(
        out_kernel,
        grid=(width // tile,),
        out_shape=(jax.ShapeDtypeStruct((piece_rows, width), jnp.bfloat16),) * 2,
        in_specs=[
            pl.BlockSpec(memory_space=pltpu.SMEM),
            pl.BlockSpec((1, width), lambda i: (0, 0)),
            pl.BlockSpec((width, tile), lambda i: (0, i)),
            pl.BlockSpec((piece_rows, tile), lambda i: (request, i)),
        ]
        + [remote] * len(pieces),
        out_specs=(pl.BlockSpec((piece_rows, width), lambda i: (0, 0)),) * 2,
        scratch_shapes=[
            pltpu.VMEM((2 * Z, piece_rows, piece_width), jnp.bfloat16),
            pltpu.SemaphoreType.DMA((2 * Z,)),
        ],
        compiler_params=pltpu.CompilerParams(vmem_limit_bytes=40 << 20),
        cost_estimate=pl.CostEstimate(
            flops=4 * 10**9, transcendentals=0, bytes_accessed=20 * 10**6
        ),
        name="project_out",
    )(src, gain, weights, rows, *pieces)


def ff_kernel(core_ref, low_hbm, high_hbm, w_hbm, mine_ref, theirs_ref, x_ref, up_ref, down_ref,
              hidden_ref, x_sems, up_sems, down_sem, chunk, col_at, units):
    tiles = up_ref.shape[0]
    width = x_ref.shape[2]
    count = low_hbm.shape[0]
    rows = x_ref.shape[1]
    x_loads = [
        pltpu.make_async_copy(
            part.at[:, pl.ds(chunk * rows, rows)], x_ref.at[pl.ds(i * count, count)], x_sems.at[i]
        )
        for i, part in enumerate((low_hbm, high_hbm))
    ]
    up_loads = []
    for i in range(tiles):
        cols = min(2 * FF_PAIR, 2 * units - 2 * FF_PAIR * i)
        up_loads.append(
            pltpu.make_async_copy(
                w_hbm.at[:, pl.ds(col_at + 2 * FF_PAIR * i, cols)],
                up_ref.at[i, :, pl.ds(0, cols)],
                up_sems.at[i],
            )
        )
    down_load = pltpu.make_async_copy(
        w_hbm.at[:, pl.ds(col_at + 2 * units, units)], down_ref, down_sem
    )
    for copy in (*x_loads, *up_loads, down_load):
        copy.start()
    for copy in x_loads:
        copy.wait()
    x = x_ref[...].reshape(2 * count * rows, width)
    for i in range(tiles):
        size = min(FF_PAIR, units - FF_PAIR * i)
        up_loads[i].wait()
        both = contract(x, up_ref[i, :, : 2 * size])
        hidden_ref[:, i * FF_PAIR : i * FF_PAIR + size] = (
            jax.nn.silu(both[:, :size]) * both[:, size:]
        ).astype(jnp.bfloat16)
    down_load.wait()
    terms = lax.dot_general(
        hidden_ref[...], down_ref[...], (((1,), (1,)), ((), ())),
        preferred_element_type=jnp.float32,
    ).astype(jnp.bfloat16)
    terms = terms.reshape(Z, 2, rows, width)
    for core in range(2):

        @pl.when(core_ref[0] == core)
        def _():
            mine_ref[...] = terms[:, core]
            theirs_ref[...] = terms[:, 1 - core]


def feed_forward(core, low, high, weights, chunk, col_at, units):
    count, group_rows, width = low.shape
    rows = group_rows // 2
    tiles = -(-units // FF_PAIR)
    whole = pl.BlockSpec(memory_space=pltpu.VMEM)
    remote = pl.BlockSpec(memory_space=pl.ANY)

    def kernel(*refs):
        ff_kernel(*refs, chunk, col_at, units)

    return pl.pallas_call(
        kernel,
        out_shape=(jax.ShapeDtypeStruct((Z, rows, width), jnp.bfloat16),) * 2,
        in_specs=[pl.BlockSpec(memory_space=pltpu.SMEM), remote, remote, remote],
        out_specs=(whole, whole),
        scratch_shapes=[
            pltpu.VMEM((2 * count, rows, width), jnp.bfloat16),
            pltpu.VMEM((tiles, width, 2 * FF_PAIR), jnp.bfloat16),
            pltpu.VMEM((width, units), jnp.bfloat16),
            pltpu.VMEM((2 * count * rows, units), jnp.bfloat16),
            pltpu.SemaphoreType.DMA((2,)),
            pltpu.SemaphoreType.DMA((tiles,)),
            pltpu.SemaphoreType.DMA,
        ],
        compiler_params=pltpu.CompilerParams(vmem_limit_bytes=48 << 20),
        cost_estimate=pl.CostEstimate(
            flops=5 * 10**9, transcendentals=10**6, bytes_accessed=16 * 10**6
        ),
        name="feed_forward",
    )(core, low, high, weights)


def angles_of(cached_len):
    half = HEAD_DIM // 2
    frequency = ROPE_BASE ** (-jnp.arange(half).astype(jnp.float32) * 2.0 / HEAD_DIM)
    positions = (cached_len[:, None] + jnp.arange(S_NEW)[None, :]).reshape(-1)
    angles = frequency[:, None] * positions.astype(jnp.float32)[None, :]
    return jnp.cos(angles), jnp.sin(angles)


def beside(gate, up):
    blocks = []
    for at in range(0, gate.shape[1], FF_PAIR):
        blocks += [gate[:, at : at + FF_PAIR], up[:, at : at + FF_PAIR]]
    return jnp.concatenate(blocks, axis=1)


def per_device(
    hidden_in, attn_gain, w_qkv, w_out, mlp_gain, w_gate, w_up, w_down, cache_kv, cached_len
):
    head_count = lax.axis_size("head")
    head_index = lax.axis_index("head")
    tok_index = lax.axis_index("tok")
    q_width = HEADS * HEAD_DIM
    kv_width = KV_HEADS * HEAD_DIM
    q_dev = q_width // head_count
    split_count = head_count // KV_HEADS
    part_index = head_index % split_count
    kv_head = head_index // split_count
    units = w_gate.shape[1]
    row_count, width = hidden_in.shape

    x_pieces = gather_head(hidden_in)
    columns = jnp.concatenate(
        [
            lax.dynamic_slice_in_dim(w_qkv, head_index * q_dev, q_dev, 1),
            lax.dynamic_slice_in_dim(w_qkv, q_width + kv_head * HEAD_DIM, HEAD_DIM, 1),
            lax.dynamic_slice_in_dim(w_qkv, q_width + kv_width + kv_head * HEAD_DIM, HEAD_DIM, 1),
        ],
        axis=1,
    )
    column = jnp.stack([columns] + [along_tok(columns, d, False) for d in range(1, Z)])
    w_pieces = [column] + [along_tok(column, d, True) for d in range(1, Z)]
    steps = jnp.arange(Z)
    tok_order = (
        ((tok_index // Z - steps) % Z * Z)[:, None] + ((tok_index % Z - steps) % Z)[None, :]
    ).reshape(-1).astype(jnp.int32)
    own = cache_kv[:, 0]
    other = exchange(own)
    weights = lax.all_gather(
        jnp.concatenate([w_out, beside(w_gate, w_up), w_down.T], axis=1),
        "tok", axis=0, tiled=True,
    )
    cosine, sine = angles_of(cached_len)
    src = sources()
    att_0, qt_1, kv_1, cache_new, rows = attend_first(
        cached_len, part_index.reshape(1), src, tok_order, attn_gain[None], cosine, sine,
        x_pieces, w_pieces, own, other,
    )
    pieces_0 = gather_head(att_0)
    att_1 = attend_second(cached_len, qt_1, kv_1)
    pieces_1 = gather_head(att_1)
    gain = mlp_gain[None]
    residual_0, normed_0 = project_out(src, gain, weights, rows, pieces_0, 0)
    residual_1, normed_1 = project_out(src, gain, weights, rows, pieces_1, 1)
    half_count = head_count // 2
    low = normed_0.reshape(half_count, row_count, width)
    high = normed_1.reshape(half_count, row_count, width)
    residual = lax.dynamic_index_in_dim(
        jnp.concatenate([residual_0, residual_1]).reshape(head_count, row_count, width),
        head_index, 0, keepdims=False,
    )
    z = head_index // 2
    core = (head_index % 2).reshape(1)
    outs = []
    for chunk in range(2):
        mine, theirs = feed_forward(core, low, high, weights, chunk, w_out.shape[1], units)
        pair = (mine.astype(jnp.float32) + exchange(theirs).astype(jnp.float32)).astype(
            jnp.bfloat16
        )
        rows_here = row_count // 2
        total = residual[chunk * rows_here : (chunk + 1) * rows_here].astype(jnp.float32)
        total = total + lax.dynamic_index_in_dim(pair, z, 0, keepdims=False).astype(jnp.float32)
        for d in range(1, Z):
            sent = lax.dynamic_index_in_dim(pair, (z + d) % Z, 0, keepdims=False)
            total = total + along_z(sent, d).astype(jnp.float32)
        outs.append(total.astype(jnp.bfloat16))
    return (jnp.concatenate(outs), cache_new[:, None])


def solution(mesh):
    return jax.shard_map(
        per_device,
        mesh=mesh,
        in_specs=(
            P(("tok", "head"), None),
            P(),
            P("tok", None),
            P("tok", None),
            P(),
            P("tok", "head"),
            P("tok", "head"),
            P("head", "tok"),
            P("tok", "head", None, None),
            P("tok"),
        ),
        out_specs=(P(("tok", "head"), None), P("tok", "head", None, None)),
        check_vma=False,
    )
```

```python
import jax
import jax.numpy as jnp
from jax import lax
from jax.experimental import pallas as pl
from jax.experimental.pallas import tpu as pltpu
from jax.sharding import PartitionSpec as P

HEADS = 32
KV_HEADS = 4
HEAD_DIM = 64
S_NEW = 512
ROPE_BASE = 10000.0

KEYS = 512
ALIGN = 16
WINDOW = S_NEW + ALIGN
VROWS = HEAD_DIM + 16


Z = 4
FF_PAIR = 128


def mean_norm(values, gain):
    widened = values.astype(jnp.float32)
    spread = jnp.mean(widened * widened, axis=-1, keepdims=True)
    return (widened * lax.rsqrt(spread + 1e-05) * gain).astype(jnp.bfloat16)


def contract(left_rows, right_rows):
    return jnp.dot(left_rows, right_rows, preferred_element_type=jnp.float32)


def exchange(array):
    return lax.ppermute(array, "head", [(i, i ^ 1) for i in range(lax.axis_size("head"))])


def along_z(array, distance):
    count = lax.axis_size("head")
    return lax.ppermute(array, "head", [(i, (i + 2 * distance) % count) for i in range(count)])


def gather_head(array):
    same_core = [array] + [along_z(array, d) for d in range(1, Z)]
    return same_core, exchange(jnp.stack(same_core))


def sources():
    head_index = lax.axis_index("head")
    z, core = head_index // 2, head_index % 2
    chips = (z - jnp.arange(Z)) % Z * 2
    return jnp.concatenate([chips + core, chips + 1 - core]).astype(jnp.int32)


def attend(length, kv_ref, qt_ref, acc_ref, top_ref, out_ref):
    lanes = kv_ref.shape[1]
    acc_ref[...] = jnp.zeros(acc_ref.shape, jnp.float32)
    top_ref[...] = jnp.full(top_ref.shape, -1e30, jnp.float32)

    def step(index, masked):
        at = pl.multiple_of(index * KEYS, KEYS)
        block = kv_ref[pl.ds(at, KEYS)]
        lane = lax.broadcasted_iota(jnp.int32, (KEYS, lanes), 1)
        ones = jnp.where(lane < HEAD_DIM, 1.0, block.astype(jnp.float32))
        values = ones.T[HEAD_DIM - 16 :].astype(jnp.bfloat16)
        scores = contract(block, qt_ref[...])
        if masked:
            key = lax.broadcasted_iota(jnp.int32, scores.shape, 0) + (index * KEYS - length)
            query = lax.broadcasted_iota(jnp.int32, scores.shape, 1) % S_NEW
            scores = jnp.where(key <= query, scores, -jnp.inf)
        old_top = top_ref[...]
        top = jnp.maximum(jnp.max(scores, axis=0, keepdims=True), old_top)
        exps = jnp.exp(scores - top).astype(jnp.bfloat16)
        acc_ref[...] = contract(values, exps) + acc_ref[...] * jnp.exp(old_top - top)
        top_ref[...] = top

    def last(index, carry):
        step(index, True)
        return carry

    def full(index, carry):
        step(index, False)
        return carry

    tail = length // KEYS
    lax.fori_loop(tail, (length + S_NEW + KEYS - 1) // KEYS, last, 0)
    lax.fori_loop(0, tail, full, 0)
    for pair in range(qt_ref.shape[1] // (2 * S_NEW)):
        sides = []
        for h in (2 * pair, 2 * pair + 1):
            here = slice(h * S_NEW, (h + 1) * S_NEW)
            sides.append(acc_ref[16:, here] / acc_ref[:1, here])
        out_ref[:, pair * lanes : (pair + 1) * lanes] = (
            jnp.concatenate(sides, axis=0).T.astype(jnp.bfloat16)
        )


def first_kernel(
    lens_ref, part_ref, src_ref, gain_ref, cos_ref, sin_ref, w_ref, x_0, x_1, x_2, x_3, x_others,
    own_hbm, other_hbm, out_ref, later_qt_ref, later_kv_hbm, cache_hbm, rows_hbm, x_ref, kv_ref,
    qt_ref, new_ref, acc_ref, top_ref, x_sems, load_sems, store_sems,
):
    req_count, block_pos, lanes = own_hbm.shape
    heads_dev = qt_ref.shape[1] // S_NEW
    half = HEAD_DIM // 2
    x_pieces = [x_0, x_1, x_2, x_3] + [x_others.at[i] for i in range(Z)]
    piece_rows = x_0.shape[0]
    own_at = pl.multiple_of(part_ref[0] * block_pos, ALIGN)
    other_at = pl.multiple_of((1 - part_ref[0]) * block_pos, ALIGN)

    def x_load(i):
        at = pl.multiple_of(src_ref[i] * piece_rows, piece_rows)
        return pltpu.make_async_copy(x_pieces[i], x_ref.at[pl.ds(at, piece_rows)], x_sems.at[i])

    def loads(r):
        return (
            pltpu.make_async_copy(
                own_hbm.at[r], kv_ref.at[r, pl.ds(own_at, block_pos)], load_sems.at[r, 0]
            ),
            pltpu.make_async_copy(
                other_hbm.at[r], kv_ref.at[r, pl.ds(other_at, block_pos)], load_sems.at[r, 1]
            ),
        )

    def stores(r):
        copies = [
            pltpu.make_async_copy(
                kv_ref.at[r, pl.ds(own_at, block_pos)], cache_hbm.at[r], store_sems.at[r]
            )
        ]
        if r:
            copies.append(pltpu.make_async_copy(kv_ref.at[r], later_kv_hbm, store_sems.at[2]))
        return copies

    for i in range(2 * Z):
        x_load(i).start()
    for r in range(req_count):
        for copy in loads(r):
            copy.start()
    for i in range(2 * Z):
        x_load(i).wait()
    keep = pltpu.make_async_copy(x_ref, rows_hbm, store_sems.at[3])
    keep.start()

    q_lanes = heads_dev * HEAD_DIM
    gain = gain_ref[...]
    for r in range(req_count):
        here = slice(r * S_NEW, (r + 1) * S_NEW)
        cosine = cos_ref[:, here]
        sine = sin_ref[:, here]

        def turn(block, scale):
            first = block[:half]
            second = block[half:]
            return jnp.concatenate(
                [
                    (first * cosine - second * sine) * scale,
                    (second * cosine + first * sine) * scale,
                ],
                axis=0,
            )

        normed = mean_norm(x_ref[here], gain)
        projected = contract(normed, w_ref[...])
        for pair in range(heads_dev // 2):
            flipped = projected[:, pair * lanes : (pair + 1) * lanes].T
            for one in range(2):
                rows = turn(flipped[one * HEAD_DIM : (one + 1) * HEAD_DIM], HEAD_DIM**-0.5)
                rows = jnp.concatenate([rows, jnp.zeros_like(rows)], axis=0).astype(jnp.bfloat16)
                at = (2 * pair + one) * S_NEW
                (later_qt_ref if r else qt_ref)[:, at : at + S_NEW] = rows
        flipped = projected[:, q_lanes:].T
        fresh = jnp.concatenate([turn(flipped[:HEAD_DIM], 1.0), flipped[HEAD_DIM:]], axis=0)
        new_ref[r] = fresh.T.astype(jnp.bfloat16)

    for r in range(req_count):
        length = lens_ref[r]
        for copy in loads(r):
            copy.wait()
        shift = length % ALIGN
        window_at = pl.multiple_of(length - shift, ALIGN)
        row = lax.broadcasted_iota(jnp.int32, (WINDOW, S_NEW), 0)
        col = lax.broadcasted_iota(jnp.int32, (WINDOW, S_NEW), 1)
        pick = (row - shift == col).astype(jnp.float32).astype(jnp.bfloat16)
        moved = contract(pick, new_ref[r])
        row = lax.broadcasted_iota(jnp.int32, (WINDOW, lanes), 0)
        inside = (row >= shift) & (row < shift + S_NEW)
        old = kv_ref[r, pl.ds(window_at, WINDOW)].astype(jnp.float32)
        kv_ref[r, pl.ds(window_at, WINDOW)] = jnp.where(inside, moved, old).astype(jnp.bfloat16)
        for copy in stores(r):
            copy.start()

    attend(lens_ref[0], kv_ref.at[0], qt_ref, acc_ref, top_ref, out_ref)
    for r in range(req_count):
        for copy in stores(r):
            copy.wait()
    keep.wait()


def attend_first(lens, part, src, gain, cosine, sine, w, x_same, x_others, own, other):
    req_count, block_pos, lanes = own.shape
    piece_rows, width = x_same[0].shape
    rows = piece_rows * 2 * Z
    heads_dev = (w.shape[1] - lanes) // HEAD_DIM
    positions = 2 * block_pos + ALIGN
    whole = pl.BlockSpec(memory_space=pltpu.VMEM)
    scalar = pl.BlockSpec(memory_space=pltpu.SMEM)
    remote = pl.BlockSpec(memory_space=pl.ANY)
    return pl.pallas_call(
        first_kernel,
        out_shape=(
            jax.ShapeDtypeStruct((S_NEW, heads_dev * HEAD_DIM), jnp.bfloat16),
            jax.ShapeDtypeStruct((lanes, heads_dev * S_NEW), jnp.bfloat16),
            jax.ShapeDtypeStruct((positions, lanes), jnp.bfloat16),
            jax.ShapeDtypeStruct(own.shape, jnp.bfloat16),
            jax.ShapeDtypeStruct((rows, width), jnp.bfloat16),
        ),
        in_specs=[scalar] * 3 + [whole] * 4 + [remote] * (Z + 3),
        out_specs=(whole, whole, remote, remote, remote),
        scratch_shapes=[
            pltpu.VMEM((rows, width), jnp.bfloat16),
            pltpu.VMEM((req_count, positions, lanes), jnp.bfloat16),
            pltpu.VMEM((lanes, heads_dev * S_NEW), jnp.bfloat16),
            pltpu.VMEM((req_count, S_NEW, lanes), jnp.bfloat16),
            pltpu.VMEM((VROWS, heads_dev * S_NEW), jnp.float32),
            pltpu.VMEM((1, heads_dev * S_NEW), jnp.float32),
            pltpu.SemaphoreType.DMA((2 * Z,)),
            pltpu.SemaphoreType.DMA((req_count, 2)),
            pltpu.SemaphoreType.DMA((4,)),
        ],
        compiler_params=pltpu.CompilerParams(vmem_limit_bytes=50 << 20),
        cost_estimate=pl.CostEstimate(
            flops=4 * 10**10, transcendentals=10**8, bytes_accessed=100 * 10**6
        ),
        name="attend_first",
    )(lens, part, src, gain, cosine, sine, w, *x_same, x_others, own, other)


def second_kernel(len_ref, qt_ref, kv_ref, out_ref, acc_ref, top_ref):
    attend(len_ref[1], kv_ref, qt_ref, acc_ref, top_ref, out_ref)


def attend_second(lens, qt, kv):
    columns = qt.shape[1]
    whole = pl.BlockSpec(memory_space=pltpu.VMEM)
    return pl.pallas_call(
        second_kernel,
        out_shape=jax.ShapeDtypeStruct((S_NEW, columns // S_NEW * HEAD_DIM), jnp.bfloat16),
        in_specs=[pl.BlockSpec(memory_space=pltpu.SMEM), whole, whole],
        out_specs=whole,
        scratch_shapes=[
            pltpu.VMEM((VROWS, columns), jnp.float32),
            pltpu.VMEM((1, columns), jnp.float32),
        ],
        compiler_params=pltpu.CompilerParams(vmem_limit_bytes=40 << 20),
        cost_estimate=pl.CostEstimate(
            flops=4 * 10**10, transcendentals=10**8, bytes_accessed=100 * 10**6
        ),
        name="attend_second",
    )(lens, qt, kv)


def out_kernel(
    src_ref, gain_ref, rows_ref, w_0, w_1, w_2, w_3, w_others, a_0, a_1, a_2, a_3, a_others,
    residual_ref, normed_ref, att_ref, w_ref, sum_ref, att_sems, w_sems,
):
    weights = [w_0, w_1, w_2, w_3] + [w_others.at[i] for i in range(Z)]
    pieces = [a_0, a_1, a_2, a_3] + [a_others.at[i] for i in range(Z)]
    att_loads = [
        pltpu.make_async_copy(pieces[i], att_ref.at[src_ref[i]], att_sems.at[i])
        for i in range(2 * Z)
    ]
    w_loads = [
        pltpu.make_async_copy(weights[i], w_ref.at[i], w_sems.at[i]) for i in range(2 * Z)
    ]
    for copy in (*att_loads, *w_loads):
        copy.start()
    for copy in att_loads:
        copy.wait()
    attended = jnp.concatenate([att_ref[i] for i in range(2 * Z)], axis=1)
    for i in range(2 * Z):
        w_loads[i].wait()
        sum_ref[src_ref[i]] = contract(attended, w_ref[i])
    total = jnp.concatenate([sum_ref[i] for i in range(2 * Z)], axis=1)
    residual_ref[...] = (rows_ref[...].astype(jnp.float32) + total).astype(jnp.bfloat16)
    normed_ref[...] = mean_norm(residual_ref[...], gain_ref[...])


def project_out(src, gain, weights, rows, pieces, request):
    piece_rows, piece_width = pieces[0][0].shape
    width = rows.shape[1]
    cols = weights[0][0].shape[1]
    remote = pl.BlockSpec(memory_space=pl.ANY)
    return pl.pallas_call(
        out_kernel,
        grid=(1,),
        out_shape=(jax.ShapeDtypeStruct((piece_rows, width), jnp.bfloat16),) * 2,
        in_specs=[
            pl.BlockSpec(memory_space=pltpu.SMEM),
            pl.BlockSpec((1, width), lambda i: (0, 0)),
            pl.BlockSpec((piece_rows, width), lambda i: (request, 0)),
        ]
        + [remote] * (2 * Z + 2),
        out_specs=(pl.BlockSpec((piece_rows, width), lambda i: (0, 0)),) * 2,
        scratch_shapes=[
            pltpu.VMEM((2 * Z, piece_rows, piece_width), jnp.bfloat16),
            pltpu.VMEM((2 * Z, width, cols), jnp.bfloat16),
            pltpu.VMEM((2 * Z, piece_rows, cols), jnp.float32),
            pltpu.SemaphoreType.DMA((2 * Z,)),
            pltpu.SemaphoreType.DMA((2 * Z,)),
        ],
        compiler_params=pltpu.CompilerParams(vmem_limit_bytes=48 << 20),
        cost_estimate=pl.CostEstimate(
            flops=4 * 10**9, transcendentals=0, bytes_accessed=16 * 10**6
        ),
        name="project_out",
    )(src, gain, rows, *weights[0], weights[1], *pieces[0], pieces[1])


def ff_kernel(place_ref, low_hbm, high_hbm, w_hbm, mine_ref, theirs_ref, x_ref, up_ref, down_ref,
              hidden_ref, x_sems, up_sems, down_sem):
    tiles, shards, depth, lanes = up_ref.shape
    units = down_ref.shape[1]
    width = x_ref.shape[2]
    count = low_hbm.shape[0]
    rows = x_ref.shape[1]
    row_at = pl.multiple_of(place_ref[1] * rows, rows)
    x_loads = [
        pltpu.make_async_copy(
            part.at[:, pl.ds(row_at, rows)], x_ref.at[pl.ds(i * count, count)], x_sems.at[i]
        )
        for i, part in enumerate((low_hbm, high_hbm))
    ]
    up_loads = [
        pltpu.make_async_copy(
            w_hbm.at[:, pl.ds(depth * i, depth)], up_ref.at[i], up_sems.at[i]
        )
        for i in range(tiles)
    ]
    down_load = pltpu.make_async_copy(w_hbm.at[:, pl.ds(depth * tiles, units)], down_ref, down_sem)
    for copy in (*x_loads, *up_loads, down_load):
        copy.start()
    for copy in x_loads:
        copy.wait()
    x = x_ref[...].reshape(2 * count * rows, width)
    for i in range(0, tiles, 2):
        blocks = []
        for j in range(i, min(i + 2, tiles)):
            up_loads[j].wait()
            blocks.append(up_ref[j].reshape(width, lanes))
        both = contract(x, jnp.concatenate(blocks, axis=1))
        size = both.shape[1] // 2
        hidden_ref[:, i * lanes // 2 : i * lanes // 2 + size] = (
            jax.nn.silu(both[:, :size]) * both[:, size:]
        ).astype(jnp.bfloat16)
    down_load.wait()
    hidden = hidden_ref[...]
    for i in range(0, shards, 2):
        terms = contract(hidden, jnp.concatenate([down_ref[i], down_ref[i + 1]], axis=1))
        terms = terms.astype(jnp.bfloat16).reshape(Z, 2, rows, 2 * lanes)
        here = slice(i * lanes, (i + 2) * lanes)
        for core in range(2):

            @pl.when(place_ref[0] == core)
            def _():
                mine_ref[:, :, here] = terms[:, core]
                theirs_ref[:, :, here] = terms[:, 1 - core]


def feed_forward(place, low, high, weights, units):
    count, group_rows, width = low.shape
    rows = group_rows // 2
    shards, height, lanes = weights.shape
    depth = width // shards
    tiles = (height - units) // depth
    whole = pl.BlockSpec(memory_space=pltpu.VMEM)
    remote = pl.BlockSpec(memory_space=pl.ANY)
    return pl.pallas_call(
        ff_kernel,
        out_shape=(jax.ShapeDtypeStruct((Z, rows, width), jnp.bfloat16),) * 2,
        in_specs=[pl.BlockSpec(memory_space=pltpu.SMEM), remote, remote, remote],
        out_specs=(whole, whole),
        scratch_shapes=[
            pltpu.VMEM((2 * count, rows, width), jnp.bfloat16),
            pltpu.VMEM((tiles, shards, depth, lanes), jnp.bfloat16),
            pltpu.VMEM((shards, units, lanes), jnp.bfloat16),
            pltpu.VMEM((2 * count * rows, units), jnp.bfloat16),
            pltpu.SemaphoreType.DMA((2,)),
            pltpu.SemaphoreType.DMA((tiles,)),
            pltpu.SemaphoreType.DMA,
        ],
        compiler_params=pltpu.CompilerParams(vmem_limit_bytes=48 << 20),
        cost_estimate=pl.CostEstimate(
            flops=5 * 10**9, transcendentals=10**6, bytes_accessed=16 * 10**6
        ),
        name="feed_forward",
    )(place, low, high, weights)


def angles_of(cached_len):
    half = HEAD_DIM // 2
    frequency = ROPE_BASE ** (-jnp.arange(half).astype(jnp.float32) * 2.0 / HEAD_DIM)
    positions = (cached_len[:, None] + jnp.arange(S_NEW)[None, :]).reshape(-1)
    angles = frequency[:, None] * positions.astype(jnp.float32)[None, :]
    return jnp.cos(angles), jnp.sin(angles)


def beside(gate, up):
    blocks = []
    count = gate.shape[1] // FF_PAIR
    for i in range(count):
        here = slice(i * FF_PAIR, (i + 1) * FF_PAIR)
        blocks += [gate[:, here], up[:, here]]
    blocks.append(jnp.concatenate([gate[:, count * FF_PAIR :], up[:, count * FF_PAIR :]], axis=1))
    return jnp.concatenate(blocks, axis=0)


def per_device(
    hidden_in, attn_gain, w_qkv, w_out, mlp_gain, w_gate, w_up, w_down, cache_kv, cached_len
):
    head_count = lax.axis_size("head")
    head_index = lax.axis_index("head")
    q_width = HEADS * HEAD_DIM
    kv_width = KV_HEADS * HEAD_DIM
    q_dev = q_width // head_count
    split_count = head_count // KV_HEADS
    part_index = head_index % split_count
    kv_head = head_index // split_count
    units = w_gate.shape[1]
    row_count, width = hidden_in.shape

    src = sources()
    own = cache_kv[:, 0]
    other = exchange(own)
    x_same = [hidden_in] + [along_z(hidden_in, d) for d in range(1, Z)]
    columns = jnp.concatenate(
        [
            lax.dynamic_slice_in_dim(w_qkv, head_index * q_dev, q_dev, 1),
            lax.dynamic_slice_in_dim(w_qkv, q_width + kv_head * HEAD_DIM, HEAD_DIM, 1),
            lax.dynamic_slice_in_dim(w_qkv, q_width + kv_width + kv_head * HEAD_DIM, HEAD_DIM, 1),
        ],
        axis=1,
    )
    group_w = lax.all_to_all(
        jnp.broadcast_to(columns[None], (lax.axis_size("tok"), *columns.shape)), "tok", 0, 0, tiled=True
    ).reshape(width, columns.shape[1])
    out_cols = width // head_count
    out_part = lax.all_gather(
        lax.dynamic_slice_in_dim(w_out, head_index * out_cols, out_cols, 1),
        "tok", axis=0, tiled=True,
    )
    ff_part, group_w, other, *x_same = lax.optimization_barrier(
        (jnp.concatenate([beside(w_gate, w_up), w_down], axis=0), group_w, other, *x_same)
    )
    x_others = exchange(jnp.stack(x_same))
    ff_weights = lax.all_gather(ff_part, "tok", axis=0)
    cosine, sine = angles_of(cached_len)
    att_0, qt_1, kv_1, cache_new, rows = attend_first(
        cached_len, part_index.reshape(1), src, attn_gain[None], cosine, sine, group_w,
        x_same, x_others, own, other,
    )
    out_same = [out_part] + [along_z(out_part, d) for d in range(1, Z)]
    qt_1, *out_same = lax.optimization_barrier((qt_1, *out_same))
    out_pieces = (out_same, exchange(jnp.stack(out_same)))
    pieces_0 = gather_head(att_0)
    att_1 = attend_second(cached_len, qt_1, kv_1)
    pieces_1 = gather_head(att_1)
    gain = mlp_gain[None]
    residual_0, normed_0 = project_out(src, gain, out_pieces, rows, pieces_0, 0)
    rows, residual_0 = lax.optimization_barrier((rows, residual_0))
    residual_1, normed_1 = project_out(src, gain, out_pieces, rows, pieces_1, 1)
    half_count = head_count // 2
    low = normed_0.reshape(half_count, row_count, width)
    high = normed_1.reshape(half_count, row_count, width)
    z = head_index // 2
    core = head_index % 2
    own_0 = lax.dynamic_index_in_dim(
        residual_0.reshape(half_count, row_count, width), head_index % half_count, 0, keepdims=False
    )
    own_1 = lax.dynamic_index_in_dim(
        residual_1.reshape(half_count, row_count, width), head_index % half_count, 0, keepdims=False
    )
    residual = jnp.where(head_index < half_count, own_0, own_1)
    outs = []
    for chunk in range(2):
        place = jnp.stack([core, jnp.int32(chunk)]).astype(jnp.int32)
        mine, theirs = feed_forward(place, low, high, ff_weights, units)
        pair = (mine.astype(jnp.float32) + exchange(theirs).astype(jnp.float32)).astype(
            jnp.bfloat16
        )
        rows_here = row_count // 2
        total = residual[chunk * rows_here : (chunk + 1) * rows_here].astype(jnp.float32)
        total = total + lax.dynamic_index_in_dim(pair, z, 0, keepdims=False).astype(jnp.float32)
        for d in range(1, Z):
            sent = lax.dynamic_index_in_dim(pair, (z + d) % Z, 0, keepdims=False)
            total = total + along_z(sent, d).astype(jnp.float32)
        outs.append(total.astype(jnp.bfloat16))
    return (jnp.concatenate(outs), cache_new[:, None])


def solution(mesh):
    return jax.shard_map(
        per_device,
        mesh=mesh,
        in_specs=(
            P(("tok", "head"), None),
            P(),
            P("tok", None),
            P("tok", None),
            P(),
            P("tok", "head"),
            P("tok", "head"),
            P("head", "tok"),
            P("tok", "head", None, None),
            P("tok"),
        ),
        out_specs=(P(("tok", "head"), None), P("tok", "head", None, None)),
        check_vma=False,
    )
```

```python
import jax
import jax.numpy as jnp
from jax import lax
from jax.experimental import pallas as pl
from jax.experimental.pallas import tpu as pltpu
from jax.sharding import PartitionSpec as P

HEADS = 32
KV_HEADS = 4
HEAD_DIM = 64
S_NEW = 512
ROPE_BASE = 10000.0

KEYS = 512
ALIGN = 16
WINDOW = S_NEW + ALIGN
VROWS = HEAD_DIM + 16


Z = 4
FF_PAIR = 128


def mean_norm(values, gain):
    widened = values.astype(jnp.float32)
    spread = jnp.mean(widened * widened, axis=-1, keepdims=True)
    return (widened * lax.rsqrt(spread + 1e-05) * gain).astype(jnp.bfloat16)


def contract(left_rows, right_rows):
    return jnp.dot(left_rows, right_rows, preferred_element_type=jnp.float32)


def exchange(array):
    return lax.ppermute(array, "head", [(i, i ^ 1) for i in range(lax.axis_size("head"))])


def along_z(array, distance):
    count = lax.axis_size("head")
    return lax.ppermute(array, "head", [(i, (i + 2 * distance) % count) for i in range(count)])


def gather_head(array):
    same_core = [array] + [along_z(array, d) for d in range(1, Z)]
    return same_core, exchange(jnp.stack(same_core))


def sources():
    head_index = lax.axis_index("head")
    z, core = head_index // 2, head_index % 2
    chips = (z - jnp.arange(Z)) % Z * 2
    return jnp.concatenate([chips + core, chips + 1 - core]).astype(jnp.int32)


def attend(length, kv_ref, qt_ref, acc_ref, top_ref, out_ref):
    lanes = kv_ref.shape[1]
    acc_ref[...] = jnp.zeros(acc_ref.shape, jnp.float32)
    top_ref[...] = jnp.full(top_ref.shape, -1e30, jnp.float32)

    def step(index, masked):
        at = pl.multiple_of(index * KEYS, KEYS)
        block = kv_ref[pl.ds(at, KEYS)]
        lane = lax.broadcasted_iota(jnp.int32, (KEYS, lanes), 1)
        ones = jnp.where(lane < HEAD_DIM, 1.0, block.astype(jnp.float32))
        values = ones.T[HEAD_DIM - 16 :].astype(jnp.bfloat16)
        scores = contract(block, qt_ref[...])
        if masked:
            key = lax.broadcasted_iota(jnp.int32, scores.shape, 0) + (index * KEYS - length)
            query = lax.broadcasted_iota(jnp.int32, scores.shape, 1) % S_NEW
            scores = jnp.where(key <= query, scores, -jnp.inf)
        old_top = top_ref[...]
        top = jnp.maximum(jnp.max(scores, axis=0, keepdims=True), old_top)
        exps = jnp.exp(scores - top).astype(jnp.bfloat16)
        acc_ref[...] = contract(values, exps) + acc_ref[...] * jnp.exp(old_top - top)
        top_ref[...] = top

    def last(index, carry):
        step(index, True)
        return carry

    def full(index, carry):
        step(index, False)
        return carry

    tail = length // KEYS
    lax.fori_loop(tail, (length + S_NEW + KEYS - 1) // KEYS, last, 0)
    lax.fori_loop(0, tail, full, 0)
    for pair in range(qt_ref.shape[1] // (2 * S_NEW)):
        sides = []
        for h in (2 * pair, 2 * pair + 1):
            here = slice(h * S_NEW, (h + 1) * S_NEW)
            sides.append(acc_ref[16:, here] / acc_ref[:1, here])
        out_ref[:, pair * lanes : (pair + 1) * lanes] = (
            jnp.concatenate(sides, axis=0).T.astype(jnp.bfloat16)
        )


def prepare_kernel(
    lens_ref, part_ref, src_ref, gain_ref, cos_ref, sin_ref, w_ref, x_0, x_1, x_2, x_3, x_others,
    own_hbm, other_hbm, qt_0, qt_1, kv_0, kv_1, cache_hbm, rows_hbm, x_ref, kv_ref, new_ref,
    x_sems, load_sems, store_sems,
):
    req_count, block_pos, lanes = own_hbm.shape
    heads_dev = qt_0.shape[1] // S_NEW
    half = HEAD_DIM // 2
    x_pieces = [x_0, x_1, x_2, x_3] + [x_others.at[i] for i in range(Z)]
    piece_rows = x_0.shape[0]
    own_at = pl.multiple_of(part_ref[0] * block_pos, ALIGN)
    other_at = pl.multiple_of((1 - part_ref[0]) * block_pos, ALIGN)

    def x_load(i):
        at = pl.multiple_of(src_ref[i] * piece_rows, piece_rows)
        return pltpu.make_async_copy(x_pieces[i], x_ref.at[pl.ds(at, piece_rows)], x_sems.at[i])

    def loads(r):
        return (
            pltpu.make_async_copy(
                own_hbm.at[r], kv_ref.at[r, pl.ds(own_at, block_pos)], load_sems.at[r, 0]
            ),
            pltpu.make_async_copy(
                other_hbm.at[r], kv_ref.at[r, pl.ds(other_at, block_pos)], load_sems.at[r, 1]
            ),
        )

    def stores(r):
        return (
            pltpu.make_async_copy(
                kv_ref.at[r, pl.ds(own_at, block_pos)], cache_hbm.at[r], store_sems.at[r, 0]
            ),
            pltpu.make_async_copy(kv_ref.at[r], (kv_0, kv_1)[r], store_sems.at[r, 1]),
        )

    for i in range(2 * Z):
        x_load(i).start()
    for r in range(req_count):
        for copy in loads(r):
            copy.start()
    for i in range(2 * Z):
        x_load(i).wait()
    keep = pltpu.make_async_copy(x_ref, rows_hbm, store_sems.at[req_count, 0])
    keep.start()

    q_lanes = heads_dev * HEAD_DIM
    gain = gain_ref[...]
    for r in range(req_count):
        here = slice(r * S_NEW, (r + 1) * S_NEW)
        cosine = cos_ref[:, here]
        sine = sin_ref[:, here]

        def turn(block, scale):
            first = block[:half]
            second = block[half:]
            return jnp.concatenate(
                [
                    (first * cosine - second * sine) * scale,
                    (second * cosine + first * sine) * scale,
                ],
                axis=0,
            )

        normed = mean_norm(x_ref[here], gain)
        projected = contract(normed, w_ref[...])
        for pair in range(heads_dev // 2):
            flipped = projected[:, pair * lanes : (pair + 1) * lanes].T
            for one in range(2):
                rows = turn(flipped[one * HEAD_DIM : (one + 1) * HEAD_DIM], HEAD_DIM**-0.5)
                rows = jnp.concatenate([rows, jnp.zeros_like(rows)], axis=0).astype(jnp.bfloat16)
                at = (2 * pair + one) * S_NEW
                (qt_0, qt_1)[r][:, at : at + S_NEW] = rows
        flipped = projected[:, q_lanes:].T
        fresh = jnp.concatenate([turn(flipped[:HEAD_DIM], 1.0), flipped[HEAD_DIM:]], axis=0)
        new_ref[r] = fresh.T.astype(jnp.bfloat16)

    for r in range(req_count):
        length = lens_ref[r]
        for copy in loads(r):
            copy.wait()
        shift = length % ALIGN
        window_at = pl.multiple_of(length - shift, ALIGN)
        row = lax.broadcasted_iota(jnp.int32, (WINDOW, S_NEW), 0)
        col = lax.broadcasted_iota(jnp.int32, (WINDOW, S_NEW), 1)
        pick = (row - shift == col).astype(jnp.float32).astype(jnp.bfloat16)
        moved = contract(pick, new_ref[r])
        row = lax.broadcasted_iota(jnp.int32, (WINDOW, lanes), 0)
        inside = (row >= shift) & (row < shift + S_NEW)
        old = kv_ref[r, pl.ds(window_at, WINDOW)].astype(jnp.float32)
        kv_ref[r, pl.ds(window_at, WINDOW)] = jnp.where(inside, moved, old).astype(jnp.bfloat16)
        for copy in stores(r):
            copy.start()

    for r in range(req_count):
        for copy in stores(r):
            copy.wait()
    keep.wait()


def prepare(lens, part, src, gain, cosine, sine, w, x_same, x_others, own, other):
    req_count, block_pos, lanes = own.shape
    piece_rows, width = x_same[0].shape
    rows = piece_rows * 2 * Z
    heads_dev = (w.shape[1] - lanes) // HEAD_DIM
    positions = 2 * block_pos + ALIGN
    whole = pl.BlockSpec(memory_space=pltpu.VMEM)
    scalar = pl.BlockSpec(memory_space=pltpu.SMEM)
    remote = pl.BlockSpec(memory_space=pl.ANY)
    return pl.pallas_call(
        prepare_kernel,
        out_shape=(
            jax.ShapeDtypeStruct((lanes, heads_dev * S_NEW), jnp.bfloat16),
            jax.ShapeDtypeStruct((lanes, heads_dev * S_NEW), jnp.bfloat16),
            jax.ShapeDtypeStruct((positions, lanes), jnp.bfloat16),
            jax.ShapeDtypeStruct((positions, lanes), jnp.bfloat16),
            jax.ShapeDtypeStruct(own.shape, jnp.bfloat16),
            jax.ShapeDtypeStruct((rows, width), jnp.bfloat16),
        ),
        in_specs=[scalar] * 3 + [whole] * 4 + [remote] * (Z + 3),
        out_specs=(whole, whole, remote, remote, remote, remote),
        scratch_shapes=[
            pltpu.VMEM((rows, width), jnp.bfloat16),
            pltpu.VMEM((req_count, positions, lanes), jnp.bfloat16),
            pltpu.VMEM((req_count, S_NEW, lanes), jnp.bfloat16),
            pltpu.SemaphoreType.DMA((2 * Z,)),
            pltpu.SemaphoreType.DMA((req_count, 2)),
            pltpu.SemaphoreType.DMA((req_count + 1, 2)),
        ],
        compiler_params=pltpu.CompilerParams(vmem_limit_bytes=32 << 20),
        cost_estimate=pl.CostEstimate(
            flops=4 * 10**9, transcendentals=10**6, bytes_accessed=20 * 10**6
        ),
        name="prepare",
    )(lens, part, src, gain, cosine, sine, w, *x_same, x_others, own, other)


def attention_kernel(len_ref, qt_ref, kv_ref, out_ref, acc_ref, top_ref):
    attend(len_ref[0], kv_ref, qt_ref, acc_ref, top_ref, out_ref)


def attention(length, qt, kv):
    columns = qt.shape[1]
    whole = pl.BlockSpec(memory_space=pltpu.VMEM)
    return pl.pallas_call(
        attention_kernel,
        out_shape=jax.ShapeDtypeStruct((S_NEW, columns // S_NEW * HEAD_DIM), jnp.bfloat16),
        in_specs=[pl.BlockSpec(memory_space=pltpu.SMEM), whole, whole],
        out_specs=whole,
        scratch_shapes=[
            pltpu.VMEM((VROWS, columns), jnp.float32),
            pltpu.VMEM((1, columns), jnp.float32),
        ],
        compiler_params=pltpu.CompilerParams(vmem_limit_bytes=20 << 20),
        cost_estimate=pl.CostEstimate(
            flops=4 * 10**10, transcendentals=10**8, bytes_accessed=100 * 10**6
        ),
        name="attention",
    )(length, qt, kv)


def out_kernel(
    src_ref, gain_ref, rows_ref, w_0, w_1, w_2, w_3, w_others, a_0, a_1, a_2, a_3, a_others,
    residual_ref, normed_ref, att_ref, sum_ref,
):
    for i, piece in enumerate((a_0, a_1, a_2, a_3)):
        att_ref[src_ref[i]] = piece[...]
        att_ref[src_ref[Z + i]] = a_others[i]
    attended = jnp.concatenate([att_ref[i] for i in range(2 * Z)], axis=1)
    for i, weights in enumerate((w_0, w_1, w_2, w_3)):
        sum_ref[src_ref[i]] = contract(attended, weights[...])
        sum_ref[src_ref[Z + i]] = contract(attended, w_others[i])
    total = jnp.concatenate([sum_ref[i] for i in range(2 * Z)], axis=1)
    residual_ref[...] = (rows_ref[...].astype(jnp.float32) + total).astype(jnp.bfloat16)
    normed_ref[...] = mean_norm(residual_ref[...], gain_ref[...])


def project_out(src, gain, weights, rows, pieces, request):
    piece_rows, piece_width = pieces[0][0].shape
    width = rows.shape[1]
    cols = weights[0][0].shape[1]
    whole = pl.BlockSpec(memory_space=pltpu.VMEM)
    return pl.pallas_call(
        out_kernel,
        grid=(1,),
        out_shape=(jax.ShapeDtypeStruct((piece_rows, width), jnp.bfloat16),) * 2,
        in_specs=[
            pl.BlockSpec(memory_space=pltpu.SMEM),
            pl.BlockSpec((1, width), lambda i: (0, 0)),
            pl.BlockSpec((piece_rows, width), lambda i: (request, 0)),
        ]
        + [whole] * (2 * Z + 2),
        out_specs=(whole,) * 2,
        scratch_shapes=[
            pltpu.VMEM((2 * Z, piece_rows, piece_width), jnp.bfloat16),
            pltpu.VMEM((2 * Z, piece_rows, cols), jnp.float32),
        ],
        compiler_params=pltpu.CompilerParams(vmem_limit_bytes=20 << 20),
        cost_estimate=pl.CostEstimate(
            flops=4 * 10**9, transcendentals=0, bytes_accessed=16 * 10**6
        ),
        name="project_out",
    )(src, gain, rows, *weights[0], weights[1], *pieces[0], pieces[1])


def ff_kernel(
    place_ref, low_hbm, high_hbm, w_ref, mine_ref, theirs_ref, x_ref, hidden_ref, x_sems
):
    shards, height, lanes = w_ref.shape
    width = x_ref.shape[3]
    depth = width // shards
    units = hidden_ref.shape[1]
    tiles = (height - units) // depth
    rows = x_ref.shape[2]
    count = low_hbm.shape[0]
    row_at = pl.multiple_of(place_ref[1] * rows, rows)
    x_loads = []
    for i in range(2 * count):
        side = lax.rem(place_ref[0] + i % 2, 2)
        x_loads.append(
            pltpu.make_async_copy(
                (low_hbm, high_hbm)[i // count].at[i % count, pl.ds(row_at, rows)],
                x_ref.at[side, i // 2],
                x_sems.at[i],
            )
        )
    for copy in x_loads:
        copy.start()
    for copy in x_loads:
        copy.wait()
    x = x_ref[...].reshape(2 * Z * rows, width)
    for i in range(0, tiles, 2):
        blocks = [
            w_ref[:, depth * j : depth * (j + 1)].reshape(width, lanes)
            for j in range(i, min(i + 2, tiles))
        ]
        both = contract(x, jnp.concatenate(blocks, axis=1))
        size = both.shape[1] // 2
        hidden_ref[:, i * lanes // 2 : i * lanes // 2 + size] = (
            jax.nn.silu(both[:, :size]) * both[:, size:]
        ).astype(jnp.bfloat16)
    hidden = hidden_ref[...]
    for i in range(0, shards, 2):
        down = jnp.concatenate([w_ref[i, depth * tiles :], w_ref[i + 1, depth * tiles :]], axis=1)
        terms = contract(hidden, down).astype(jnp.bfloat16).reshape(2, Z, rows, 2 * lanes)
        mine_ref[:, :, i * lanes : (i + 2) * lanes] = terms[0]
        theirs_ref[:, :, i * lanes : (i + 2) * lanes] = terms[1]


def feed_forward(place, low, high, weights, units):
    count, group_rows, width = low.shape
    rows = group_rows // 2
    whole = pl.BlockSpec(memory_space=pltpu.VMEM)
    remote = pl.BlockSpec(memory_space=pl.ANY)
    return pl.pallas_call(
        ff_kernel,
        out_shape=(jax.ShapeDtypeStruct((Z, rows, width), jnp.bfloat16),) * 2,
        in_specs=[pl.BlockSpec(memory_space=pltpu.SMEM), remote, remote, whole],
        out_specs=(whole, whole),
        scratch_shapes=[
            pltpu.VMEM((2, Z, rows, width), jnp.bfloat16),
            pltpu.VMEM((2 * count * rows, units), jnp.bfloat16),
            pltpu.SemaphoreType.DMA((2 * count,)),
        ],
        compiler_params=pltpu.CompilerParams(vmem_limit_bytes=20 << 20),
        cost_estimate=pl.CostEstimate(
            flops=5 * 10**9, transcendentals=10**6, bytes_accessed=16 * 10**6
        ),
        name="feed_forward",
    )(place, low, high, weights)


def angles_of(cached_len):
    half = HEAD_DIM // 2
    frequency = ROPE_BASE ** (-jnp.arange(half).astype(jnp.float32) * 2.0 / HEAD_DIM)
    positions = (cached_len[:, None] + jnp.arange(S_NEW)[None, :]).reshape(-1)
    angles = frequency[:, None] * positions.astype(jnp.float32)[None, :]
    return jnp.cos(angles), jnp.sin(angles)


def beside(gate, up):
    blocks = []
    count = gate.shape[1] // FF_PAIR
    for i in range(count):
        here = slice(i * FF_PAIR, (i + 1) * FF_PAIR)
        blocks += [gate[:, here], up[:, here]]
    blocks.append(jnp.concatenate([gate[:, count * FF_PAIR :], up[:, count * FF_PAIR :]], axis=1))
    return jnp.concatenate(blocks, axis=0)


def per_device(
    hidden_in, attn_gain, w_qkv, w_out, mlp_gain, w_gate, w_up, w_down, cache_kv, cached_len
):
    head_count = lax.axis_size("head")
    head_index = lax.axis_index("head")
    q_width = HEADS * HEAD_DIM
    kv_width = KV_HEADS * HEAD_DIM
    q_dev = q_width // head_count
    split_count = head_count // KV_HEADS
    part_index = head_index % split_count
    kv_head = head_index // split_count
    units = w_gate.shape[1]
    row_count, width = hidden_in.shape

    src = sources()
    own = cache_kv[:, 0]
    other = exchange(own)
    columns = jnp.concatenate(
        [
            lax.dynamic_slice_in_dim(w_qkv, head_index * q_dev, q_dev, 1),
            lax.dynamic_slice_in_dim(w_qkv, q_width + kv_head * HEAD_DIM, HEAD_DIM, 1),
            lax.dynamic_slice_in_dim(w_qkv, q_width + kv_width + kv_head * HEAD_DIM, HEAD_DIM, 1),
        ],
        axis=1,
    )
    spread = jnp.broadcast_to(columns[None], (lax.axis_size("tok"), *columns.shape))
    spread, x_own = lax.optimization_barrier((spread, hidden_in))
    group_w = lax.all_to_all(spread, "tok", 0, 0, tiled=True).reshape(width, columns.shape[1])
    x_same = [x_own] + [along_z(x_own, d) for d in range(1, Z)]
    out_cols = width // head_count
    out_part = lax.all_gather(
        lax.dynamic_slice_in_dim(w_out, head_index * out_cols, out_cols, 1),
        "tok", axis=0, tiled=True,
    )
    ff_part, group_w, other, *x_same = lax.optimization_barrier(
        (jnp.concatenate([beside(w_gate, w_up), w_down], axis=0), group_w, other, *x_same)
    )
    x_others = exchange(jnp.stack(x_same))
    ff_weights = lax.all_gather(ff_part, "tok", axis=0)
    cosine, sine = angles_of(cached_len)
    qt_0, qt_1, kv_0, kv_1, cache_new, rows = prepare(
        cached_len, part_index.reshape(1), src, attn_gain[None], cosine, sine, group_w,
        x_same, x_others, own, other,
    )
    out_part, qt_0 = lax.optimization_barrier((out_part, qt_0))
    att_0 = attention(cached_len[:1], qt_0, kv_0)
    out_same = [out_part] + [along_z(out_part, d) for d in range(1, Z)]
    qt_1, *out_same = lax.optimization_barrier((qt_1, *out_same))
    out_pieces = (out_same, exchange(jnp.stack(out_same)))
    pieces_0 = gather_head(att_0)
    att_1 = attention(cached_len[1:], qt_1, kv_1)
    pieces_1 = gather_head(att_1)
    gain = mlp_gain[None]
    residual_0, normed_0 = project_out(src, gain, out_pieces, rows, pieces_0, 0)
    rows, residual_0, ff_weights = lax.optimization_barrier((rows, residual_0, ff_weights))
    residual_1, normed_1 = project_out(src, gain, out_pieces, rows, pieces_1, 1)
    half_count = head_count // 2
    low = normed_0.reshape(half_count, row_count, width)
    high = normed_1.reshape(half_count, row_count, width)
    z = head_index // 2
    core = head_index % 2
    own_0 = lax.dynamic_index_in_dim(
        residual_0.reshape(half_count, row_count, width), head_index % half_count, 0, keepdims=False
    )
    own_1 = lax.dynamic_index_in_dim(
        residual_1.reshape(half_count, row_count, width), head_index % half_count, 0, keepdims=False
    )
    residual = jnp.where(head_index < half_count, own_0, own_1)
    outs = []
    for chunk in range(2):
        place = jnp.stack([core, jnp.int32(chunk)]).astype(jnp.int32)
        mine, theirs = feed_forward(place, low, high, ff_weights, units)
        pair = (mine.astype(jnp.float32) + exchange(theirs).astype(jnp.float32)).astype(
            jnp.bfloat16
        )
        rows_here = row_count // 2
        total = residual[chunk * rows_here : (chunk + 1) * rows_here].astype(jnp.float32)
        total = total + lax.dynamic_index_in_dim(pair, z, 0, keepdims=False).astype(jnp.float32)
        for d in range(1, Z):
            sent = lax.dynamic_index_in_dim(pair, (z + d) % Z, 0, keepdims=False)
            total = total + along_z(sent, d).astype(jnp.float32)
        outs.append(total.astype(jnp.bfloat16))
    return (jnp.concatenate(outs), cache_new[:, None])


def solution(mesh):
    return jax.shard_map(
        per_device,
        mesh=mesh,
        in_specs=(
            P(("tok", "head"), None),
            P(),
            P("tok", None),
            P("tok", None),
            P(),
            P("tok", "head"),
            P("tok", "head"),
            P("head", "tok"),
            P("tok", "head", None, None),
            P("tok"),
        ),
        out_specs=(P(("tok", "head"), None), P("tok", "head", None, None)),
        check_vma=False,
    )
```

```python
import jax
import jax.numpy as jnp
from jax import lax
from jax.experimental import pallas as pl
from jax.experimental.pallas import tpu as pltpu
from jax.sharding import PartitionSpec as P

HEADS = 32
KV_HEADS = 4
HEAD_DIM = 64
S_NEW = 512
ROPE_BASE = 10000.0

KEYS = 512
ALIGN = 16
WINDOW = S_NEW + ALIGN
VROWS = HEAD_DIM + 16


Z = 4
FF_PAIR = 128


def mean_norm(values, gain):
    widened = values.astype(jnp.float32)
    spread = jnp.mean(widened * widened, axis=-1, keepdims=True)
    return (widened * lax.rsqrt(spread + 1e-05) * gain).astype(jnp.bfloat16)


def contract(left_rows, right_rows):
    return jnp.dot(left_rows, right_rows, preferred_element_type=jnp.float32)


def exchange(array):
    return lax.ppermute(array, "head", [(i, i ^ 1) for i in range(lax.axis_size("head"))])


def along_z(array, distance):
    count = lax.axis_size("head")
    return lax.ppermute(array, "head", [(i, (i + 2 * distance) % count) for i in range(count)])


def gather_head(array):
    same_core = jnp.stack([array] + [along_z(array, d) for d in range(1, Z)])
    return same_core, exchange(same_core)


def along_z_to(array, distance, chips):
    count = lax.axis_size("head")
    moves = [(i, (i + 2 * distance) % count) for i in range(count)]
    return lax.ppermute(array, "head", [m for m in moves if m[1] // 2 in chips])


def sources():
    head_index = lax.axis_index("head")
    z, core = head_index // 2, head_index % 2
    chips = (z - jnp.arange(Z)) % Z * 2
    return jnp.concatenate([chips + core, chips + 1 - core]).astype(jnp.int32)


def attend(length, kv_ref, qt_ref, acc_ref, top_ref, out_ref):
    lanes = kv_ref.shape[1]
    acc_ref[...] = jnp.zeros(acc_ref.shape, jnp.float32)
    top_ref[...] = jnp.full(top_ref.shape, -1e30, jnp.float32)

    def step(index, masked, here):
        at = pl.multiple_of(index * KEYS, KEYS)
        block = kv_ref[pl.ds(at, KEYS)]
        lane = lax.broadcasted_iota(jnp.int32, (KEYS, lanes), 1)
        ones = jnp.where(lane < HEAD_DIM, 1.0, block.astype(jnp.float32))
        values = ones.T[HEAD_DIM - 16 :].astype(jnp.bfloat16)
        scores = contract(block, qt_ref[:, here])
        if masked:
            key = lax.broadcasted_iota(jnp.int32, scores.shape, 0) + (index * KEYS - length)
            query = lax.broadcasted_iota(jnp.int32, scores.shape, 1)
            scores = jnp.where(key <= query, scores, -jnp.inf)
        old_top = top_ref[:, here]
        top = jnp.maximum(jnp.max(scores, axis=0, keepdims=True), old_top)
        exps = jnp.exp(scores - top).astype(jnp.bfloat16)
        acc_ref[:, here] = contract(values, exps) + acc_ref[:, here] * jnp.exp(old_top - top)
        top_ref[:, here] = top

    def last(index, carry):
        def one_head(h, inner):
            step(index, True, pl.ds(pl.multiple_of(h * S_NEW, S_NEW), S_NEW))
            return inner

        return lax.fori_loop(0, qt_ref.shape[1] // S_NEW, one_head, carry)

    def full(index, carry):
        step(index, False, slice(None))
        return carry

    tail = length // KEYS
    lax.fori_loop(tail, (length + S_NEW + KEYS - 1) // KEYS, last, 0)
    lax.fori_loop(0, tail, full, 0)
    for pair in range(qt_ref.shape[1] // (2 * S_NEW)):
        sides = []
        for h in (2 * pair, 2 * pair + 1):
            here = slice(h * S_NEW, (h + 1) * S_NEW)
            sides.append(acc_ref[16:, here] / acc_ref[:1, here])
        out_ref[:, pair * lanes : (pair + 1) * lanes] = (
            jnp.concatenate(sides, axis=0).T.astype(jnp.bfloat16)
        )


def prepare_kernel(
    lens_ref, part_ref, src_ref, gain_ref, cos_ref, sin_ref, w_ref, x_0, x_1, x_2, x_3, x_others,
    own_hbm, other_hbm, qt_0, qt_1, kv_0, kv_1, cache_hbm, rows_hbm, x_ref, kv_ref, new_ref,
    qt_ref, x_sems, load_sems, store_sems,
):
    req_count, block_pos, lanes = own_hbm.shape
    heads_dev = qt_0.shape[1] // S_NEW
    half = HEAD_DIM // 2
    x_pieces = [x_0, x_1, x_2, x_3] + [x_others.at[i] for i in range(Z)]
    piece_rows = x_0.shape[0]
    own_at = pl.multiple_of(part_ref[0] * block_pos, ALIGN)
    other_at = pl.multiple_of((1 - part_ref[0]) * block_pos, ALIGN)

    def x_load(i):
        at = pl.multiple_of(src_ref[i] * piece_rows, piece_rows)
        return pltpu.make_async_copy(x_pieces[i], x_ref.at[pl.ds(at, piece_rows)], x_sems.at[i])

    def loads(r):
        return (
            pltpu.make_async_copy(
                own_hbm.at[r], kv_ref.at[r, pl.ds(own_at, block_pos)], load_sems.at[r, 0]
            ),
            pltpu.make_async_copy(
                other_hbm.at[r], kv_ref.at[r, pl.ds(other_at, block_pos)], load_sems.at[r, 1]
            ),
        )

    def stores(r):
        return (
            pltpu.make_async_copy(
                kv_ref.at[r, pl.ds(own_at, block_pos)], cache_hbm.at[r], store_sems.at[r, 0]
            ),
            pltpu.make_async_copy(kv_ref.at[r], (kv_0, kv_1)[r], store_sems.at[r, 1]),
            pltpu.make_async_copy(qt_ref.at[r], (qt_0, qt_1)[r], store_sems.at[r, 2]),
        )

    for i in range(2 * Z):
        x_load(i).start()
    for r in range(req_count):
        for copy in loads(r):
            copy.start()
    for i in range(2 * Z):
        x_load(i).wait()
    keep = pltpu.make_async_copy(x_ref, rows_hbm, store_sems.at[req_count, 0])
    keep.start()

    q_lanes = heads_dev * HEAD_DIM
    gain = gain_ref[...]
    for r in range(req_count):
        here = slice(r * S_NEW, (r + 1) * S_NEW)
        cosine = cos_ref[:, here]
        sine = sin_ref[:, here]

        def turn(block, scale):
            first = block[:half]
            second = block[half:]
            return jnp.concatenate(
                [
                    (first * cosine - second * sine) * scale,
                    (second * cosine + first * sine) * scale,
                ],
                axis=0,
            )

        normed = mean_norm(x_ref[here], gain)
        projected = contract(normed, w_ref[...])
        for pair in range(heads_dev // 2):
            flipped = projected[:, pair * lanes : (pair + 1) * lanes].T
            for one in range(2):
                rows = turn(flipped[one * HEAD_DIM : (one + 1) * HEAD_DIM], HEAD_DIM**-0.5)
                rows = jnp.concatenate([rows, jnp.zeros_like(rows)], axis=0).astype(jnp.bfloat16)
                at = (2 * pair + one) * S_NEW
                qt_ref[r, :, at : at + S_NEW] = rows
        flipped = projected[:, q_lanes:].T
        fresh = jnp.concatenate([turn(flipped[:HEAD_DIM], 1.0), flipped[HEAD_DIM:]], axis=0)
        new_ref[r] = fresh.T.astype(jnp.bfloat16)

    for r in range(req_count):
        length = lens_ref[r]
        for copy in loads(r):
            copy.wait()
        shift = length % ALIGN
        window_at = pl.multiple_of(length - shift, ALIGN)
        row = lax.broadcasted_iota(jnp.int32, (WINDOW, S_NEW), 0)
        col = lax.broadcasted_iota(jnp.int32, (WINDOW, S_NEW), 1)
        pick = (row - shift == col).astype(jnp.float32).astype(jnp.bfloat16)
        moved = contract(pick, new_ref[r])
        row = lax.broadcasted_iota(jnp.int32, (WINDOW, lanes), 0)
        inside = (row >= shift) & (row < shift + S_NEW)
        old = kv_ref[r, pl.ds(window_at, WINDOW)].astype(jnp.float32)
        kv_ref[r, pl.ds(window_at, WINDOW)] = jnp.where(inside, moved, old).astype(jnp.bfloat16)
        for copy in stores(r):
            copy.start()

    for r in range(req_count):
        for copy in stores(r):
            copy.wait()
    keep.wait()


def prepare(lens, part, src, gain, cosine, sine, w, x_same, x_others, own, other):
    req_count, block_pos, lanes = own.shape
    piece_rows, width = x_same[0].shape
    rows = piece_rows * 2 * Z
    heads_dev = (w.shape[1] - lanes) // HEAD_DIM
    positions = 2 * block_pos + ALIGN
    whole = pl.BlockSpec(memory_space=pltpu.VMEM)
    scalar = pl.BlockSpec(memory_space=pltpu.SMEM)
    remote = pl.BlockSpec(memory_space=pl.ANY)
    return pl.pallas_call(
        prepare_kernel,
        out_shape=(
            jax.ShapeDtypeStruct((lanes, heads_dev * S_NEW), jnp.bfloat16),
            jax.ShapeDtypeStruct((lanes, heads_dev * S_NEW), jnp.bfloat16),
            jax.ShapeDtypeStruct((positions, lanes), jnp.bfloat16),
            jax.ShapeDtypeStruct((positions, lanes), jnp.bfloat16),
            jax.ShapeDtypeStruct(own.shape, jnp.bfloat16),
            jax.ShapeDtypeStruct((rows, width), jnp.bfloat16),
        ),
        in_specs=[scalar] * 3 + [whole] * 4 + [remote] * (Z + 3),
        out_specs=(pl.BlockSpec(memory_space=pltpu.HBM),) * 6,
        scratch_shapes=[
            pltpu.VMEM((rows, width), jnp.bfloat16),
            pltpu.VMEM((req_count, positions, lanes), jnp.bfloat16),
            pltpu.VMEM((req_count, S_NEW, lanes), jnp.bfloat16),
            pltpu.VMEM((req_count, lanes, heads_dev * S_NEW), jnp.bfloat16),
            pltpu.SemaphoreType.DMA((2 * Z,)),
            pltpu.SemaphoreType.DMA((req_count, 2)),
            pltpu.SemaphoreType.DMA((req_count + 1, 3)),
        ],
        compiler_params=pltpu.CompilerParams(vmem_limit_bytes=24 << 20),
        cost_estimate=pl.CostEstimate(
            flops=4 * 10**9, transcendentals=10**6, bytes_accessed=20 * 10**6
        ),
        name="prepare",
    )(lens, part, src, gain, cosine, sine, w, *x_same, x_others, own, other)


def attention_kernel(len_ref, qt_hbm, kv_hbm, out_ref, qt_ref, kv_ref, acc_ref, top_ref, sems):
    loads = (
        pltpu.make_async_copy(qt_hbm, qt_ref, sems.at[0]),
        pltpu.make_async_copy(kv_hbm, kv_ref, sems.at[1]),
    )
    for copy in loads:
        copy.start()
    for copy in loads:
        copy.wait()
    attend(len_ref[0], kv_ref, qt_ref, acc_ref, top_ref, out_ref)


def attention(length, qt, kv):
    columns = qt.shape[1]
    remote = pl.BlockSpec(memory_space=pltpu.HBM)
    return pl.pallas_call(
        attention_kernel,
        out_shape=jax.ShapeDtypeStruct((S_NEW, columns // S_NEW * HEAD_DIM), jnp.bfloat16),
        in_specs=[pl.BlockSpec(memory_space=pltpu.SMEM), remote, remote],
        out_specs=pl.BlockSpec(memory_space=pltpu.VMEM),
        scratch_shapes=[
            pltpu.VMEM(qt.shape, jnp.bfloat16),
            pltpu.VMEM(kv.shape, jnp.bfloat16),
            pltpu.VMEM((VROWS, columns), jnp.float32),
            pltpu.VMEM((1, columns), jnp.float32),
            pltpu.SemaphoreType.DMA((2,)),
        ],
        compiler_params=pltpu.CompilerParams(vmem_limit_bytes=20 << 20),
        cost_estimate=pl.CostEstimate(
            flops=4 * 10**10, transcendentals=10**8, bytes_accessed=100 * 10**6
        ),
        name="attention",
    )(length, qt, kv)


def finish_kernel(
    src_ref, place_ref, gain_ref, rows_hbm, w_same, w_others, a_same, a_others, ff_ref,
    own_ref, mine_ref, theirs_ref, att_ref, sum_ref, rows_ref, residual_ref, x_ref, hidden_ref,
    row_sem, request,
):
    full_rows, width = rows_ref.shape
    load = pltpu.make_async_copy(
        rows_hbm.at[pl.ds(request * full_rows, full_rows)], rows_ref, row_sem
    )
    load.start()
    for i in range(Z):
        att_ref[src_ref[i]] = a_same[i]
        att_ref[src_ref[Z + i]] = a_others[i]

    def columns(i, carry):
        attended = jnp.concatenate([att_ref[j] for j in range(2 * Z)], axis=1)
        sum_ref[src_ref[i]] = contract(attended, w_same[i])
        sum_ref[src_ref[Z + i]] = contract(attended, w_others[i])
        return carry

    lax.fori_loop(0, Z, columns, 0)
    load.wait()
    total = jnp.concatenate([sum_ref[i] for i in range(2 * Z)], axis=1)
    residual_ref[...] = (rows_ref[...].astype(jnp.float32) + total).astype(jnp.bfloat16)
    sides, chips, rows, _ = x_ref.shape
    own_ref[...] = residual_ref[pl.ds(pl.multiple_of(place_ref[1] * rows, rows), rows)]
    for i in range(sides * chips):
        side = lax.rem(place_ref[0] + i % 2, 2)
        x_ref[side, i // 2] = mean_norm(residual_ref[i * rows : (i + 1) * rows], gain_ref[...])

    shards, height, lanes = ff_ref.shape
    depth = width // shards
    tiles = hidden_ref.shape[0]
    start = (2 * tiles - 1) * depth

    def up(i, blocks):
        x = x_ref[...].reshape(full_rows, width)
        loaded = [
            ff_ref[:, pl.ds(pl.multiple_of((2 * i + j) * depth, depth), depth)].reshape(
                width, lanes
            )
            for j in range(blocks)
        ]
        both = contract(x, jnp.concatenate(loaded, axis=1) if blocks > 1 else loaded[0])
        size = both.shape[1] // 2
        hidden_ref[i, :, :size] = (jax.nn.silu(both[:, :size]) * both[:, size:]).astype(
            jnp.bfloat16
        )

    def up_pair(i, carry):
        up(i, 2)
        return carry

    lax.fori_loop(0, tiles - 1, up_pair, 0)
    up(tiles - 1, 1)
    for i in range(0, shards, 2):
        hidden = jnp.concatenate([hidden_ref[j] for j in range(tiles)], axis=1)
        hidden = hidden[:, : height - start]
        down = jnp.concatenate([ff_ref[i, start:], ff_ref[i + 1, start:]], axis=1)
        terms = contract(hidden, down).astype(jnp.bfloat16).reshape(sides, chips, rows, 2 * lanes)
        mine_ref[:, :, i * lanes : (i + 2) * lanes] = terms[0]
        theirs_ref[:, :, i * lanes : (i + 2) * lanes] = terms[1]


def finish(src, place, gain, rows, weights, pieces, ff_weights, units, piece_rows, request):
    width = rows.shape[1]
    piece_width = pieces[0].shape[2]
    chips = S_NEW // (2 * piece_rows)
    tiles = -(-units // FF_PAIR)
    scalar = pl.BlockSpec(memory_space=pltpu.SMEM)
    whole = pl.BlockSpec(memory_space=pltpu.VMEM)

    def kernel(*refs):
        finish_kernel(*refs, request)

    return pl.pallas_call(
        kernel,
        out_shape=(jax.ShapeDtypeStruct((piece_rows, width), jnp.bfloat16),)
        + (jax.ShapeDtypeStruct((chips, piece_rows, width), jnp.bfloat16),) * 2,
        in_specs=[scalar, scalar, whole, pl.BlockSpec(memory_space=pltpu.HBM)] + [whole] * 5,
        out_specs=(whole,) * 3,
        scratch_shapes=[
            pltpu.VMEM((2 * Z, S_NEW, piece_width), jnp.bfloat16),
            pltpu.VMEM((2 * Z, S_NEW, weights[0].shape[2]), jnp.float32),
            pltpu.VMEM((S_NEW, width), jnp.bfloat16),
            pltpu.VMEM((S_NEW, width), jnp.bfloat16),
            pltpu.VMEM((2, chips, piece_rows, width), jnp.bfloat16),
            pltpu.VMEM((tiles, S_NEW, FF_PAIR), jnp.bfloat16),
            pltpu.SemaphoreType.DMA,
        ],
        compiler_params=pltpu.CompilerParams(vmem_limit_bytes=27 << 20),
        cost_estimate=pl.CostEstimate(
            flops=9 * 10**9, transcendentals=10**6, bytes_accessed=30 * 10**6
        ),
        name="finish",
    )(src, place, gain, rows, *weights, *pieces, ff_weights)


def angles_of(cached_len):
    half = HEAD_DIM // 2
    frequency = ROPE_BASE ** (-jnp.arange(half).astype(jnp.float32) * 2.0 / HEAD_DIM)
    positions = (cached_len[:, None] + jnp.arange(S_NEW)[None, :]).reshape(-1)
    angles = frequency[:, None] * positions.astype(jnp.float32)[None, :]
    return jnp.cos(angles), jnp.sin(angles)


def beside(gate, up):
    blocks = []
    count = gate.shape[1] // FF_PAIR
    for i in range(count):
        here = slice(i * FF_PAIR, (i + 1) * FF_PAIR)
        blocks += [gate[:, here], up[:, here]]
    blocks.append(jnp.concatenate([gate[:, count * FF_PAIR :], up[:, count * FF_PAIR :]], axis=1))
    return jnp.concatenate(blocks, axis=0)


def per_device(
    hidden_in, attn_gain, w_qkv, w_out, mlp_gain, w_gate, w_up, w_down, cache_kv, cached_len
):
    head_count = lax.axis_size("head")
    head_index = lax.axis_index("head")
    q_width = HEADS * HEAD_DIM
    kv_width = KV_HEADS * HEAD_DIM
    q_dev = q_width // head_count
    split_count = head_count // KV_HEADS
    part_index = head_index % split_count
    kv_head = head_index // split_count
    units = w_gate.shape[1]
    row_count, width = hidden_in.shape

    src = sources()
    own = cache_kv[:, 0]
    other = exchange(own)
    columns = jnp.concatenate(
        [
            lax.dynamic_slice_in_dim(w_qkv, head_index * q_dev, q_dev, 1),
            lax.dynamic_slice_in_dim(w_qkv, q_width + kv_head * HEAD_DIM, HEAD_DIM, 1),
            lax.dynamic_slice_in_dim(w_qkv, q_width + kv_width + kv_head * HEAD_DIM, HEAD_DIM, 1),
        ],
        axis=1,
    )
    spread = jnp.broadcast_to(columns[None], (lax.axis_size("tok"), *columns.shape))
    spread, x_own = lax.optimization_barrier((spread, hidden_in))
    group_w = lax.all_to_all(spread, "tok", 0, 0, tiled=True).reshape(width, columns.shape[1])
    x_same = [x_own] + [along_z(x_own, d) for d in range(1, Z)]
    out_cols = width // head_count
    out_part = lax.all_gather(
        lax.dynamic_slice_in_dim(w_out, head_index * out_cols, out_cols, 1),
        "tok", axis=0, tiled=True,
    )
    ff_part, group_w, other, *x_same = lax.optimization_barrier(
        (jnp.concatenate([beside(w_gate, w_up), w_down], axis=0), group_w, other, *x_same)
    )
    x_others = exchange(jnp.stack(x_same))
    ff_weights = lax.all_gather(ff_part, "tok", axis=0)
    cosine, sine = angles_of(cached_len)
    qt_0, qt_1, kv_0, kv_1, cache_new, rows = prepare(
        cached_len, part_index.reshape(1), src, attn_gain[None], cosine, sine, group_w,
        x_same, x_others, own, other,
    )
    out_part, qt_0 = lax.optimization_barrier((out_part, qt_0))
    att_0 = attention(cached_len[:1], qt_0, kv_0)
    out_far = [along_z(out_part, d) for d in range(1, Z)]
    att_0, out_part, *out_far = lax.optimization_barrier((att_0, out_part, *out_far))
    out_same = jnp.stack([out_part] + out_far)
    out_pieces = (out_same, exchange(out_same))
    far_0 = [along_z(att_0, d) for d in range(1, Z)]
    att_1 = attention(cached_len[1:], qt_1, kv_1)
    att_1, att_0, *far_0 = lax.optimization_barrier((att_1, att_0, *far_0))
    same_0 = jnp.stack([att_0] + far_0)
    pieces_0 = (same_0, exchange(same_0))
    near_1 = [along_z(att_1, d) for d in range(1, Z)]
    gain = mlp_gain[None]
    z = head_index // 2
    half_z = Z // 2
    half_count = head_count // 2

    place = jnp.stack([head_index % 2, head_index % half_count]).astype(jnp.int32)

    def after_attention(request, pieces):
        return finish(
            src, place, gain, rows, out_pieces, pieces, ff_weights, units, row_count, request
        )

    def sums(request, mine, theirs):
        pair = (mine.astype(jnp.float32) + exchange(theirs).astype(jnp.float32)).astype(
            jnp.bfloat16
        )
        chips = range(request * half_z, (request + 1) * half_z)
        own = lax.dynamic_index_in_dim(pair, z % half_z, 0, keepdims=False)
        moved = [
            along_z_to(
                lax.dynamic_index_in_dim(pair, (z + d) % half_z, 0, keepdims=False), d, chips
            )
            for d in range(1, Z)
        ]
        return own, moved

    residual_0, mine_0, theirs_0 = after_attention(0, pieces_0)
    att_1, mine_0, *near_1 = lax.optimization_barrier((att_1, mine_0, *near_1))
    same_1 = jnp.stack([att_1] + near_1)
    pieces_1 = (same_1, exchange(same_1))
    own_0, moved_0 = sums(0, mine_0, theirs_0)
    residual_1, mine_1, theirs_1 = after_attention(1, pieces_1)
    own_1, moved_1 = sums(1, mine_1, theirs_1)
    low = z < half_z
    total = jnp.where(low, residual_0, residual_1).astype(jnp.float32)
    total = total + jnp.where(low, own_0, own_1).astype(jnp.float32)
    for term_0, term_1 in zip(moved_0, moved_1):
        total = total + (term_0.astype(jnp.float32) + term_1.astype(jnp.float32))
    hidden_out = total.astype(jnp.bfloat16)
    return (hidden_out, cache_new[:, None])


def solution(mesh):
    return jax.shard_map(
        per_device,
        mesh=mesh,
        in_specs=(
            P(("tok", "head"), None),
            P(),
            P("tok", None),
            P("tok", None),
            P(),
            P("tok", "head"),
            P("tok", "head"),
            P("head", "tok"),
            P("tok", "head", None, None),
            P("tok"),
        ),
        out_specs=(P(("tok", "head"), None), P("tok", "head", None, None)),
        check_vma=False,
    )
```

```python
import jax
import jax.numpy as jnp
from jax import lax
from jax.experimental import pallas as pl
from jax.experimental.pallas import tpu as pltpu
from jax.sharding import PartitionSpec as P

HEADS = 32
KV_HEADS = 4
HEAD_DIM = 64
S_NEW = 512
ROPE_BASE = 10000.0

KEYS = 512
ALIGN = 16
WINDOW = S_NEW + ALIGN
VROWS = HEAD_DIM + 16


Z = 4
FF_PAIR = 128


def mean_norm(values, gain):
    widened = values.astype(jnp.float32)
    spread = jnp.mean(widened * widened, axis=-1, keepdims=True)
    return (widened * lax.rsqrt(spread + 1e-05) * gain).astype(jnp.bfloat16)


def contract(left_rows, right_rows):
    return jnp.dot(left_rows, right_rows, preferred_element_type=jnp.float32)


def in_hbm(array):
    return pltpu.with_memory_space_constraint(array, pltpu.HBM)


def exchange(array):
    return lax.ppermute(array, "head", [(i, i ^ 1) for i in range(lax.axis_size("head"))])


def along_z(array, distance):
    count = lax.axis_size("head")
    return lax.ppermute(array, "head", [(i, (i + 2 * distance) % count) for i in range(count)])


def gather_head(array):
    same_core = jnp.stack([array] + [along_z(array, d) for d in range(1, Z)])
    return same_core, exchange(same_core)


def sources():
    head_index = lax.axis_index("head")
    z, core = head_index // 2, head_index % 2
    chips = (z - jnp.arange(Z)) % Z * 2
    return jnp.concatenate([chips + core, chips + 1 - core]).astype(jnp.int32)


def attend(length, kv_ref, qt_ref, acc_ref, top_ref, out_ref):
    lanes = kv_ref.shape[1]
    acc_ref[...] = jnp.zeros(acc_ref.shape, jnp.float32)
    top_ref[...] = jnp.full(top_ref.shape, -1e30, jnp.float32)

    def step(index, masked, here):
        at = pl.multiple_of(index * KEYS, KEYS)
        block = kv_ref[pl.ds(at, KEYS)]
        lane = lax.broadcasted_iota(jnp.int32, (KEYS, lanes), 1)
        ones = jnp.where(lane < HEAD_DIM, 1.0, block.astype(jnp.float32))
        values = ones.T[HEAD_DIM - 16 :].astype(jnp.bfloat16)
        scores = contract(block, qt_ref[:, here])
        if masked:
            key = lax.broadcasted_iota(jnp.int32, scores.shape, 0) + (index * KEYS - length)
            query = lax.broadcasted_iota(jnp.int32, scores.shape, 1)
            scores = jnp.where(key <= query, scores, -jnp.inf)
        old_top = top_ref[:, here]
        top = jnp.maximum(jnp.max(scores, axis=0, keepdims=True), old_top)
        exps = jnp.exp(scores - top).astype(jnp.bfloat16)
        acc_ref[:, here] = contract(values, exps) + acc_ref[:, here] * jnp.exp(old_top - top)
        top_ref[:, here] = top

    def last(index, carry):
        def one_head(h, inner):
            step(index, True, pl.ds(pl.multiple_of(h * S_NEW, S_NEW), S_NEW))
            return inner

        return lax.fori_loop(0, qt_ref.shape[1] // S_NEW, one_head, carry)

    def full(index, carry):
        step(index, False, slice(None))
        return carry

    tail = length // KEYS
    lax.fori_loop(tail, (length + S_NEW + KEYS - 1) // KEYS, last, 0)
    lax.fori_loop(0, tail, full, 0)
    for pair in range(qt_ref.shape[1] // (2 * S_NEW)):
        sides = []
        for h in (2 * pair, 2 * pair + 1):
            here = slice(h * S_NEW, (h + 1) * S_NEW)
            sides.append(acc_ref[16:, here] / acc_ref[:1, here])
        out_ref[:, pair * lanes : (pair + 1) * lanes] = (
            jnp.concatenate(sides, axis=0).T.astype(jnp.bfloat16)
        )


def prepare_kernel(
    lens_ref, part_ref, src_ref, gain_ref, cos_ref, sin_ref, w_ref, x_0, x_1, x_2, x_3, x_others,
    own_hbm, other_hbm, qt_0, qt_1, kv_0, kv_1, cache_hbm, rows_hbm, x_ref, kv_ref, new_ref,
    qt_ref, x_sems, load_sems, store_sems,
):
    req_count, block_pos, lanes = own_hbm.shape
    heads_dev = qt_0.shape[1] // S_NEW
    half = HEAD_DIM // 2
    x_pieces = [x_0, x_1, x_2, x_3] + [x_others.at[i] for i in range(Z)]
    piece_rows = x_0.shape[0]
    own_at = pl.multiple_of(part_ref[0] * block_pos, ALIGN)
    other_at = pl.multiple_of((1 - part_ref[0]) * block_pos, ALIGN)

    def x_load(i):
        at = pl.multiple_of(src_ref[i] * piece_rows, piece_rows)
        return pltpu.make_async_copy(x_pieces[i], x_ref.at[pl.ds(at, piece_rows)], x_sems.at[i])

    def loads(r):
        return (
            pltpu.make_async_copy(
                own_hbm.at[r], kv_ref.at[r, pl.ds(own_at, block_pos)], load_sems.at[r, 0]
            ),
            pltpu.make_async_copy(
                other_hbm.at[r], kv_ref.at[r, pl.ds(other_at, block_pos)], load_sems.at[r, 1]
            ),
        )

    def stores(r):
        return (
            pltpu.make_async_copy(
                kv_ref.at[r, pl.ds(own_at, block_pos)], cache_hbm.at[r], store_sems.at[r, 0]
            ),
            pltpu.make_async_copy(kv_ref.at[r], (kv_0, kv_1)[r], store_sems.at[r, 1]),
            pltpu.make_async_copy(qt_ref.at[r], (qt_0, qt_1)[r], store_sems.at[r, 2]),
        )

    for i in range(2 * Z):
        x_load(i).start()
    for r in range(req_count):
        for copy in loads(r):
            copy.start()
    for i in range(2 * Z):
        x_load(i).wait()
    keep = pltpu.make_async_copy(x_ref, rows_hbm, store_sems.at[req_count, 0])
    keep.start()

    q_lanes = heads_dev * HEAD_DIM
    gain = gain_ref[...]
    def project(r, carry):
        here = pl.ds(pl.multiple_of(r * S_NEW, S_NEW), S_NEW)
        cosine = cos_ref[:, here]
        sine = sin_ref[:, here]

        def turn(block, scale):
            first = block[:half]
            second = block[half:]
            return jnp.concatenate(
                [
                    (first * cosine - second * sine) * scale,
                    (second * cosine + first * sine) * scale,
                ],
                axis=0,
            )

        normed = mean_norm(x_ref[here], gain)
        projected = contract(normed, w_ref[...])
        for pair in range(heads_dev // 2):
            flipped = projected[:, pair * lanes : (pair + 1) * lanes].T
            for one in range(2):
                rows = turn(flipped[one * HEAD_DIM : (one + 1) * HEAD_DIM], HEAD_DIM**-0.5)
                rows = jnp.concatenate([rows, jnp.zeros_like(rows)], axis=0).astype(jnp.bfloat16)
                at = (2 * pair + one) * S_NEW
                qt_ref[r, :, at : at + S_NEW] = rows
        flipped = projected[:, q_lanes:].T
        fresh = jnp.concatenate([turn(flipped[:HEAD_DIM], 1.0), flipped[HEAD_DIM:]], axis=0)
        new_ref[r] = fresh.T.astype(jnp.bfloat16)
        return carry

    lax.fori_loop(0, req_count, project, 0)

    for r in range(req_count):
        length = lens_ref[r]
        for copy in loads(r):
            copy.wait()
        shift = length % ALIGN
        window_at = pl.multiple_of(length - shift, ALIGN)
        row = lax.broadcasted_iota(jnp.int32, (WINDOW, S_NEW), 0)
        col = lax.broadcasted_iota(jnp.int32, (WINDOW, S_NEW), 1)
        pick = (row - shift == col).astype(jnp.float32).astype(jnp.bfloat16)
        moved = contract(pick, new_ref[r])
        row = lax.broadcasted_iota(jnp.int32, (WINDOW, lanes), 0)
        inside = (row >= shift) & (row < shift + S_NEW)
        old = kv_ref[r, pl.ds(window_at, WINDOW)].astype(jnp.float32)
        kv_ref[r, pl.ds(window_at, WINDOW)] = jnp.where(inside, moved, old).astype(jnp.bfloat16)
        for copy in stores(r):
            copy.start()

    for r in range(req_count):
        for copy in stores(r):
            copy.wait()
    keep.wait()


def prepare(lens, part, src, gain, cosine, sine, w, x_same, x_others, own, other):
    req_count, block_pos, lanes = own.shape
    piece_rows, width = x_same[0].shape
    rows = piece_rows * 2 * Z
    heads_dev = (w.shape[1] - lanes) // HEAD_DIM
    positions = 2 * block_pos + ALIGN
    whole = pl.BlockSpec(memory_space=pltpu.VMEM)
    scalar = pl.BlockSpec(memory_space=pltpu.SMEM)
    remote = pl.BlockSpec(memory_space=pl.ANY)
    return pl.pallas_call(
        prepare_kernel,
        out_shape=(
            pltpu.HBM((lanes, heads_dev * S_NEW), jnp.bfloat16),
            pltpu.HBM((lanes, heads_dev * S_NEW), jnp.bfloat16),
            pltpu.HBM((positions, lanes), jnp.bfloat16),
            pltpu.HBM((positions, lanes), jnp.bfloat16),
            pltpu.HBM(own.shape, jnp.bfloat16),
            pltpu.HBM((rows, width), jnp.bfloat16),
        ),
        in_specs=[scalar] * 3 + [whole] * 4 + [remote] * (Z + 3),
        out_specs=(pl.BlockSpec(memory_space=pltpu.HBM),) * 6,
        scratch_shapes=[
            pltpu.VMEM((rows, width), jnp.bfloat16),
            pltpu.VMEM((req_count, positions, lanes), jnp.bfloat16),
            pltpu.VMEM((req_count, S_NEW, lanes), jnp.bfloat16),
            pltpu.VMEM((req_count, lanes, heads_dev * S_NEW), jnp.bfloat16),
            pltpu.SemaphoreType.DMA((2 * Z,)),
            pltpu.SemaphoreType.DMA((req_count, 2)),
            pltpu.SemaphoreType.DMA((req_count + 1, 3)),
        ],
        compiler_params=pltpu.CompilerParams(vmem_limit_bytes=24 << 20),
        cost_estimate=pl.CostEstimate(
            flops=4 * 10**9, transcendentals=10**6, bytes_accessed=20 * 10**6
        ),
        name="prepare",
    )(lens, part, src, gain, cosine, sine, w, *x_same, x_others, in_hbm(own), other)


def attention_kernel(len_ref, qt_hbm, kv_hbm, out_ref, qt_ref, kv_ref, acc_ref, top_ref, sems):
    loads = (
        pltpu.make_async_copy(qt_hbm, qt_ref, sems.at[0]),
        pltpu.make_async_copy(kv_hbm, kv_ref, sems.at[1]),
    )
    for copy in loads:
        copy.start()
    for copy in loads:
        copy.wait()
    attend(len_ref[0], kv_ref, qt_ref, acc_ref, top_ref, out_ref)


def attention(length, qt, kv):
    columns = qt.shape[1]
    remote = pl.BlockSpec(memory_space=pltpu.HBM)
    return pl.pallas_call(
        attention_kernel,
        out_shape=jax.ShapeDtypeStruct((S_NEW, columns // S_NEW * HEAD_DIM), jnp.bfloat16),
        in_specs=[pl.BlockSpec(memory_space=pltpu.SMEM), remote, remote],
        out_specs=pl.BlockSpec(memory_space=pltpu.VMEM),
        scratch_shapes=[
            pltpu.VMEM(qt.shape, jnp.bfloat16),
            pltpu.VMEM(kv.shape, jnp.bfloat16),
            pltpu.VMEM((VROWS, columns), jnp.float32),
            pltpu.VMEM((1, columns), jnp.float32),
            pltpu.SemaphoreType.DMA((2,)),
        ],
        compiler_params=pltpu.CompilerParams(vmem_limit_bytes=20 << 20),
        cost_estimate=pl.CostEstimate(
            flops=4 * 10**10, transcendentals=10**8, bytes_accessed=100 * 10**6
        ),
        name="attention",
    )(length, in_hbm(qt), in_hbm(kv))


def out_kernel(
    src_ref, request_ref, gain_ref, rows_hbm, w_same, w_others, a_same, a_others, residual_hbm,
    normed_hbm, att_ref, sum_ref, rows_ref, normed_ref, row_sem, out_sems,
):
    full_rows = rows_ref.shape[0]
    at = pl.multiple_of(request_ref[0] * full_rows, full_rows)
    load = pltpu.make_async_copy(rows_hbm.at[pl.ds(at, full_rows)], rows_ref, row_sem)
    load.start()
    for i in range(Z):
        att_ref[src_ref[i]] = a_same[i]
        att_ref[src_ref[Z + i]] = a_others[i]

    def columns(i, carry):
        attended = jnp.concatenate([att_ref[j] for j in range(2 * Z)], axis=1)
        sum_ref[src_ref[i]] = contract(attended, w_same[i])
        sum_ref[src_ref[Z + i]] = contract(attended, w_others[i])
        return carry

    lax.fori_loop(0, Z, columns, 0)
    load.wait()
    total = jnp.concatenate([sum_ref[i] for i in range(2 * Z)], axis=1)
    rows_ref[...] = (rows_ref[...].astype(jnp.float32) + total).astype(jnp.bfloat16)
    keep = pltpu.make_async_copy(rows_ref, residual_hbm, out_sems.at[0])
    keep.start()
    normed_ref[...] = mean_norm(rows_ref[...], gain_ref[...])
    give = pltpu.make_async_copy(normed_ref, normed_hbm, out_sems.at[1])
    give.start()
    keep.wait()
    give.wait()


def project_out(src, gain, weights, rows, pieces, request):
    piece_rows, piece_width = pieces[0].shape[1:]
    width = rows.shape[1]
    cols = weights[0].shape[2]
    scalar = pl.BlockSpec(memory_space=pltpu.SMEM)
    whole = pl.BlockSpec(memory_space=pltpu.VMEM)
    return pl.pallas_call(
        out_kernel,
        out_shape=(pltpu.HBM((piece_rows, width), jnp.bfloat16),) * 2,
        in_specs=[scalar, scalar, whole, pl.BlockSpec(memory_space=pltpu.HBM)] + [whole] * 4,
        out_specs=(pl.BlockSpec(memory_space=pltpu.HBM),) * 2,
        scratch_shapes=[
            pltpu.VMEM((2 * Z, piece_rows, piece_width), jnp.bfloat16),
            pltpu.VMEM((2 * Z, piece_rows, cols), jnp.float32),
            pltpu.VMEM((piece_rows, width), jnp.bfloat16),
            pltpu.VMEM((piece_rows, width), jnp.bfloat16),
            pltpu.SemaphoreType.DMA,
            pltpu.SemaphoreType.DMA((2,)),
        ],
        compiler_params=pltpu.CompilerParams(vmem_limit_bytes=20 << 20),
        cost_estimate=pl.CostEstimate(
            flops=4 * 10**9, transcendentals=0, bytes_accessed=16 * 10**6
        ),
        name="project_out",
    )(src, jnp.full((1,), request, jnp.int32), gain, in_hbm(rows), *weights, *pieces)


def ff_kernel(
    place_ref, low_hbm, high_hbm, w_ref, mine_ref, theirs_ref, x_ref, hidden_ref, x_sems
):
    shards, height, lanes = w_ref.shape
    width = x_ref.shape[3]
    depth = width // shards
    units = hidden_ref.shape[1]
    tiles = (height - units) // depth
    rows = x_ref.shape[2]
    count = low_hbm.shape[0]
    row_at = pl.multiple_of(place_ref[1] * rows, rows)
    x_loads = []
    for i in range(2 * count):
        side = lax.rem(place_ref[0] + i % 2, 2)
        x_loads.append(
            pltpu.make_async_copy(
                (low_hbm, high_hbm)[i // count].at[i % count, pl.ds(row_at, rows)],
                x_ref.at[side, i // 2],
                x_sems.at[i],
            )
        )
    for copy in x_loads:
        copy.start()
    for copy in x_loads:
        copy.wait()
    x = x_ref[...].reshape(2 * Z * rows, width)
    for i in range(0, tiles, 2):
        blocks = [
            w_ref[:, depth * j : depth * (j + 1)].reshape(width, lanes)
            for j in range(i, min(i + 2, tiles))
        ]
        both = contract(x, jnp.concatenate(blocks, axis=1))
        size = both.shape[1] // 2
        hidden_ref[:, i * lanes // 2 : i * lanes // 2 + size] = (
            jax.nn.silu(both[:, :size]) * both[:, size:]
        ).astype(jnp.bfloat16)
    hidden = hidden_ref[...]
    for i in range(0, shards, 2):
        down = jnp.concatenate([w_ref[i, depth * tiles :], w_ref[i + 1, depth * tiles :]], axis=1)
        terms = contract(hidden, down).astype(jnp.bfloat16).reshape(2, Z, rows, 2 * lanes)
        mine_ref[:, :, i * lanes : (i + 2) * lanes] = terms[0]
        theirs_ref[:, :, i * lanes : (i + 2) * lanes] = terms[1]


def feed_forward(place, low, high, weights, units):
    count, group_rows, width = low.shape
    rows = group_rows // 2
    whole = pl.BlockSpec(memory_space=pltpu.VMEM)
    remote = pl.BlockSpec(memory_space=pl.ANY)
    return pl.pallas_call(
        ff_kernel,
        out_shape=(jax.ShapeDtypeStruct((Z, rows, width), jnp.bfloat16),) * 2,
        in_specs=[pl.BlockSpec(memory_space=pltpu.SMEM), remote, remote, whole],
        out_specs=(whole, whole),
        scratch_shapes=[
            pltpu.VMEM((2, Z, rows, width), jnp.bfloat16),
            pltpu.VMEM((2 * count * rows, units), jnp.bfloat16),
            pltpu.SemaphoreType.DMA((2 * count,)),
        ],
        compiler_params=pltpu.CompilerParams(vmem_limit_bytes=20 << 20),
        cost_estimate=pl.CostEstimate(
            flops=5 * 10**9, transcendentals=10**6, bytes_accessed=16 * 10**6
        ),
        name="feed_forward",
    )(place, in_hbm(low), in_hbm(high), weights)


def angles_of(cached_len):
    half = HEAD_DIM // 2
    frequency = ROPE_BASE ** (-jnp.arange(half).astype(jnp.float32) * 2.0 / HEAD_DIM)
    positions = (cached_len[:, None] + jnp.arange(S_NEW)[None, :]).reshape(-1)
    angles = frequency[:, None] * positions.astype(jnp.float32)[None, :]
    return jnp.cos(angles), jnp.sin(angles)


def beside(gate, up):
    blocks = []
    count = gate.shape[1] // FF_PAIR
    for i in range(count):
        here = slice(i * FF_PAIR, (i + 1) * FF_PAIR)
        blocks += [gate[:, here], up[:, here]]
    blocks.append(jnp.concatenate([gate[:, count * FF_PAIR :], up[:, count * FF_PAIR :]], axis=1))
    return jnp.concatenate(blocks, axis=0)


def per_device(
    hidden_in, attn_gain, w_qkv, w_out, mlp_gain, w_gate, w_up, w_down, cache_kv, cached_len
):
    head_count = lax.axis_size("head")
    head_index = lax.axis_index("head")
    q_width = HEADS * HEAD_DIM
    kv_width = KV_HEADS * HEAD_DIM
    q_dev = q_width // head_count
    split_count = head_count // KV_HEADS
    part_index = head_index % split_count
    kv_head = head_index // split_count
    units = w_gate.shape[1]
    half_z = Z // 2
    row_count, width = hidden_in.shape

    src = sources()
    own = cache_kv[:, 0]
    other = exchange(own)
    columns = jnp.concatenate(
        [
            lax.dynamic_slice_in_dim(w_qkv, head_index * q_dev, q_dev, 1),
            lax.dynamic_slice_in_dim(w_qkv, q_width + kv_head * HEAD_DIM, HEAD_DIM, 1),
            lax.dynamic_slice_in_dim(w_qkv, q_width + kv_width + kv_head * HEAD_DIM, HEAD_DIM, 1),
        ],
        axis=1,
    )
    spread = jnp.broadcast_to(columns[None], (lax.axis_size("tok"), *columns.shape))
    spread, x_own = lax.optimization_barrier((spread, hidden_in))
    group_w = lax.all_to_all(spread, "tok", 0, 0, tiled=True).reshape(width, columns.shape[1])
    x_same = [x_own] + [along_z(x_own, d) for d in range(1, Z)]
    x_others = exchange(jnp.stack(x_same))
    out_cols = width // head_count
    out_pair = lax.all_gather(
        jnp.concatenate(
            [
                lax.dynamic_slice_in_dim(w_out, block * out_cols, out_cols, 1)
                for block in (head_index, (head_index + half_z * 2) % head_count)
            ],
            axis=1,
        ),
        "tok", axis=0, tiled=True,
    )
    ff_part, group_w, other, *_ = lax.optimization_barrier(
        (jnp.concatenate([beside(w_gate, w_up), w_down], axis=0), group_w, other, *x_same)
    )
    ff_weights = lax.all_gather(ff_part, "tok", axis=0)
    cosine, sine = angles_of(cached_len)
    qt_0, qt_1, kv_0, kv_1, cache_new, rows = prepare(
        cached_len, part_index.reshape(1), src, attn_gain[None], cosine, sine, group_w,
        x_same, x_others, own, other,
    )
    out_pair, qt_0 = lax.optimization_barrier((out_pair, qt_0))
    att_0 = attention(cached_len[:1], qt_0, kv_0)
    out_part = out_pair[:, :out_cols]
    out_far = [along_z(out_part, 1), along_z(out_part, Z - 1)]
    att_0, out_part, out_pair, *out_far = lax.optimization_barrier(
        (att_0, out_part, out_pair, *out_far)
    )
    out_same = jnp.stack([out_part, out_far[0], out_pair[:, out_cols:], out_far[1]])
    out_pieces = (out_same, exchange(out_same))
    far_0 = [along_z(att_0, d) for d in range(1, Z)]
    att_1 = attention(cached_len[1:], qt_1, kv_1)
    att_1, att_0, *far_0 = lax.optimization_barrier((att_1, att_0, *far_0))
    same_0 = jnp.stack([att_0] + far_0)
    pieces_0 = (same_0, exchange(same_0))
    far_1 = [along_z(att_1, d) for d in range(1, Z)]
    gain = mlp_gain[None]
    residual_0, normed_0 = project_out(src, gain, out_pieces, rows, pieces_0, 0)
    att_1, residual_0, ff_weights, *far_1 = lax.optimization_barrier(
        (att_1, residual_0, ff_weights, *far_1)
    )
    same_1 = jnp.stack([att_1] + far_1)
    pieces_1 = (same_1, exchange(same_1))
    residual_1, normed_1 = project_out(src, gain, out_pieces, rows, pieces_1, 1)
    half_count = head_count // 2
    low = normed_0.reshape(half_count, row_count, width)
    high = normed_1.reshape(half_count, row_count, width)
    z = head_index // 2
    core = head_index % 2
    own_0 = lax.dynamic_index_in_dim(
        residual_0.reshape(half_count, row_count, width), head_index % half_count, 0, keepdims=False
    )
    own_1 = lax.dynamic_index_in_dim(
        residual_1.reshape(half_count, row_count, width), head_index % half_count, 0, keepdims=False
    )
    residual = jnp.where(head_index < half_count, own_0, own_1)
    outs = []
    for chunk in range(2):
        place = jnp.stack([core, jnp.int32(chunk)]).astype(jnp.int32)
        mine, theirs = feed_forward(place, low, high, ff_weights, units)
        pair = (mine.astype(jnp.float32) + exchange(theirs).astype(jnp.float32)).astype(
            jnp.bfloat16
        )
        rows_here = row_count // 2
        total = residual[chunk * rows_here : (chunk + 1) * rows_here].astype(jnp.float32)
        total = total + lax.dynamic_index_in_dim(pair, z, 0, keepdims=False).astype(jnp.float32)
        for d in range(1, Z):
            sent = lax.dynamic_index_in_dim(pair, (z + d) % Z, 0, keepdims=False)
            total = total + along_z(sent, d).astype(jnp.float32)
        outs.append(total.astype(jnp.bfloat16))
    return (jnp.concatenate(outs), cache_new[:, None])


def solution(mesh):
    return jax.shard_map(
        per_device,
        mesh=mesh,
        in_specs=(
            P(("tok", "head"), None),
            P(),
            P("tok", None),
            P("tok", None),
            P(),
            P("tok", "head"),
            P("tok", "head"),
            P("head", "tok"),
            P("tok", "head", None, None),
            P("tok"),
        ),
        out_specs=(P(("tok", "head"), None), P("tok", "head", None, None)),
        check_vma=False,
    )
```

```python
import jax
import jax.numpy as jnp
from jax import lax
from jax.experimental import pallas as pl
from jax.experimental.pallas import tpu as pltpu
from jax.sharding import PartitionSpec as P

HEADS = 32
KV_HEADS = 4
HEAD_DIM = 64
S_NEW = 512
ROPE_BASE = 10000.0

KEYS = 512
ALIGN = 16
WINDOW = S_NEW + ALIGN
LOG2_E = 1.4426950408889634
VROWS = HEAD_DIM + 16


Z = 4
FF_PAIR = 128


def mean_norm(values, gain):
    widened = values.astype(jnp.float32)
    spread = jnp.mean(widened * widened, axis=-1, keepdims=True)
    return (widened * lax.rsqrt(spread + 1e-05) * gain).astype(jnp.bfloat16)


def contract(left_rows, right_rows):
    return jnp.dot(left_rows, right_rows, preferred_element_type=jnp.float32)


def in_hbm(array):
    return pltpu.with_memory_space_constraint(array, pltpu.HBM)


def exchange(array):
    return lax.ppermute(array, "head", [(i, i ^ 1) for i in range(lax.axis_size("head"))])


def along_z(array, distance):
    count = lax.axis_size("head")
    return lax.ppermute(array, "head", [(i, (i + 2 * distance) % count) for i in range(count)])


def gather_head(array):
    same_core = jnp.stack([array] + [along_z(array, d) for d in range(1, Z)])
    return same_core, exchange(same_core)


def sources():
    head_index = lax.axis_index("head")
    z, core = head_index // 2, head_index % 2
    chips = (z - jnp.arange(Z)) % Z * 2
    return jnp.concatenate([chips + core, chips + 1 - core]).astype(jnp.int32)


def attend(length, kv_ref, qt_ref, acc_ref, top_ref, out_ref):
    lanes = kv_ref.shape[1]
    acc_ref[...] = jnp.zeros(acc_ref.shape, jnp.float32)
    top_ref[...] = jnp.full(top_ref.shape, -1e30, jnp.float32)

    def step(index, masked, here):
        at = pl.multiple_of(index * KEYS, KEYS)
        block = kv_ref[pl.ds(at, KEYS)].astype(jnp.float32)
        on_key = lax.broadcasted_iota(jnp.int32, (KEYS, lanes), 1) < HEAD_DIM
        values = jnp.where(on_key, 1.0, block).T[HEAD_DIM - 16 :].astype(jnp.bfloat16)
        keys = jnp.where(on_key, block, pltpu.roll(block, HEAD_DIM, 1)).astype(jnp.bfloat16)
        scores = contract(keys, qt_ref[:, here])
        if masked:
            key = lax.broadcasted_iota(jnp.int32, scores.shape, 0) + (index * KEYS - length)
            query = lax.broadcasted_iota(jnp.int32, scores.shape, 1)
            scores = jnp.where(key <= query, scores, -jnp.inf)
        old_top = top_ref[:, here]
        top = jnp.maximum(jnp.max(scores, axis=0, keepdims=True), old_top)
        exps = jnp.exp2(scores - top).astype(jnp.bfloat16)
        acc_ref[:, here] = contract(values, exps) + acc_ref[:, here] * jnp.exp2(old_top - top)
        top_ref[:, here] = top

    def last(index, carry):
        def one_head(h, inner):
            step(index, True, pl.ds(pl.multiple_of(h * S_NEW, S_NEW), S_NEW))
            return inner

        return lax.fori_loop(0, qt_ref.shape[1] // S_NEW, one_head, carry)

    def full(index, carry):
        step(index, False, slice(None))
        return carry

    tail = length // KEYS
    lax.fori_loop(tail, (length + S_NEW + KEYS - 1) // KEYS, last, 0)
    lax.fori_loop(0, tail, full, 0)
    for pair in range(qt_ref.shape[1] // (2 * S_NEW)):
        sides = []
        for h in (2 * pair, 2 * pair + 1):
            here = slice(h * S_NEW, (h + 1) * S_NEW)
            sides.append(acc_ref[16:, here] / acc_ref[:1, here])
        out_ref[:, pair * lanes : (pair + 1) * lanes] = (
            jnp.concatenate(sides, axis=0).T.astype(jnp.bfloat16)
        )


def prepare_kernel(
    lens_ref, part_ref, src_ref, gain_ref, cos_ref, sin_ref, w_ref, x_0, x_1, x_2, x_3, x_others,
    own_hbm, other_hbm, qt_0, qt_1, kv_0, kv_1, cache_hbm, rows_hbm, x_ref, kv_ref, new_ref,
    qt_ref, x_sems, load_sems, store_sems,
):
    req_count, block_pos, lanes = own_hbm.shape
    heads_dev = qt_0.shape[1] // S_NEW
    half = HEAD_DIM // 2
    x_pieces = [x_0, x_1, x_2, x_3] + [x_others.at[i] for i in range(Z)]
    piece_rows = x_0.shape[0]
    own_at = pl.multiple_of(part_ref[0] * block_pos, ALIGN)
    other_at = pl.multiple_of((1 - part_ref[0]) * block_pos, ALIGN)

    def x_load(i):
        at = pl.multiple_of(src_ref[i] * piece_rows, piece_rows)
        return pltpu.make_async_copy(x_pieces[i], x_ref.at[pl.ds(at, piece_rows)], x_sems.at[i])

    def loads(r):
        return (
            pltpu.make_async_copy(
                own_hbm.at[r], kv_ref.at[r, pl.ds(own_at, block_pos)], load_sems.at[r, 0]
            ),
            pltpu.make_async_copy(
                other_hbm.at[r], kv_ref.at[r, pl.ds(other_at, block_pos)], load_sems.at[r, 1]
            ),
        )

    def stores(r):
        return (
            pltpu.make_async_copy(
                kv_ref.at[r, pl.ds(own_at, block_pos)], cache_hbm.at[r], store_sems.at[r, 0]
            ),
            pltpu.make_async_copy(kv_ref.at[r], (kv_0, kv_1)[r], store_sems.at[r, 1]),
            pltpu.make_async_copy(qt_ref.at[r], (qt_0, qt_1)[r], store_sems.at[r, 2]),
        )

    for i in range(2 * Z):
        x_load(i).start()
    for r in range(req_count):
        for copy in loads(r):
            copy.start()
    for i in range(2 * Z):
        x_load(i).wait()
    keep = pltpu.make_async_copy(x_ref, rows_hbm, store_sems.at[req_count, 0])
    keep.start()

    q_lanes = heads_dev * HEAD_DIM
    gain = gain_ref[...]
    def project(r, carry):
        here = pl.ds(pl.multiple_of(r * S_NEW, S_NEW), S_NEW)
        cosine = cos_ref[:, here]
        sine = sin_ref[:, here]

        def turn(block, scale):
            first = block[:half]
            second = block[half:]
            return jnp.concatenate(
                [
                    (first * cosine - second * sine) * scale,
                    (second * cosine + first * sine) * scale,
                ],
                axis=0,
            )

        normed = mean_norm(x_ref[here], gain)
        projected = contract(normed, w_ref[...])
        for pair in range(heads_dev // 2):
            flipped = projected[:, pair * lanes : (pair + 1) * lanes].T
            for one in range(2):
                rows = turn(flipped[one * HEAD_DIM : (one + 1) * HEAD_DIM], HEAD_DIM**-0.5)
                rows = rows.astype(jnp.bfloat16).astype(jnp.float32) * LOG2_E
                upper = rows.astype(jnp.bfloat16)
                lower = (rows - upper.astype(jnp.float32)).astype(jnp.bfloat16)
                at = (2 * pair + one) * S_NEW
                qt_ref[r, :HEAD_DIM, at : at + S_NEW] = upper
                qt_ref[r, HEAD_DIM:, at : at + S_NEW] = lower
        flipped = projected[:, q_lanes:].T
        fresh = jnp.concatenate([turn(flipped[:HEAD_DIM], 1.0), flipped[HEAD_DIM:]], axis=0)
        new_ref[r] = fresh.T.astype(jnp.bfloat16)
        return carry

    lax.fori_loop(0, req_count, project, 0)

    for r in range(req_count):
        length = lens_ref[r]
        for copy in loads(r):
            copy.wait()
        shift = length % ALIGN
        window_at = pl.multiple_of(length - shift, ALIGN)
        row = lax.broadcasted_iota(jnp.int32, (WINDOW, S_NEW), 0)
        col = lax.broadcasted_iota(jnp.int32, (WINDOW, S_NEW), 1)
        pick = (row - shift == col).astype(jnp.float32).astype(jnp.bfloat16)
        moved = contract(pick, new_ref[r])
        row = lax.broadcasted_iota(jnp.int32, (WINDOW, lanes), 0)
        inside = (row >= shift) & (row < shift + S_NEW)
        old = kv_ref[r, pl.ds(window_at, WINDOW)].astype(jnp.float32)
        kv_ref[r, pl.ds(window_at, WINDOW)] = jnp.where(inside, moved, old).astype(jnp.bfloat16)
        for copy in stores(r):
            copy.start()

    for r in range(req_count):
        for copy in stores(r):
            copy.wait()
    keep.wait()


def prepare(lens, part, src, gain, cosine, sine, w, x_same, x_others, own, other):
    req_count, block_pos, lanes = own.shape
    piece_rows, width = x_same[0].shape
    rows = piece_rows * 2 * Z
    heads_dev = (w.shape[1] - lanes) // HEAD_DIM
    positions = 2 * block_pos + ALIGN
    whole = pl.BlockSpec(memory_space=pltpu.VMEM)
    scalar = pl.BlockSpec(memory_space=pltpu.SMEM)
    remote = pl.BlockSpec(memory_space=pl.ANY)
    return pl.pallas_call(
        prepare_kernel,
        out_shape=(
            pltpu.HBM((lanes, heads_dev * S_NEW), jnp.bfloat16),
            pltpu.HBM((lanes, heads_dev * S_NEW), jnp.bfloat16),
            pltpu.HBM((positions, lanes), jnp.bfloat16),
            pltpu.HBM((positions, lanes), jnp.bfloat16),
            pltpu.HBM(own.shape, jnp.bfloat16),
            pltpu.HBM((rows, width), jnp.bfloat16),
        ),
        in_specs=[scalar] * 3 + [whole] * 4 + [remote] * (Z + 3),
        out_specs=(pl.BlockSpec(memory_space=pltpu.HBM),) * 6,
        scratch_shapes=[
            pltpu.VMEM((rows, width), jnp.bfloat16),
            pltpu.VMEM((req_count, positions, lanes), jnp.bfloat16),
            pltpu.VMEM((req_count, S_NEW, lanes), jnp.bfloat16),
            pltpu.VMEM((req_count, lanes, heads_dev * S_NEW), jnp.bfloat16),
            pltpu.SemaphoreType.DMA((2 * Z,)),
            pltpu.SemaphoreType.DMA((req_count, 2)),
            pltpu.SemaphoreType.DMA((req_count + 1, 3)),
        ],
        compiler_params=pltpu.CompilerParams(vmem_limit_bytes=24 << 20),
        cost_estimate=pl.CostEstimate(
            flops=4 * 10**9, transcendentals=10**6, bytes_accessed=20 * 10**6
        ),
        name="prepare",
    )(lens, part, src, gain, cosine, sine, w, *x_same, x_others, in_hbm(own), other)


def attention_kernel(len_ref, qt_hbm, kv_hbm, out_ref, qt_ref, kv_ref, acc_ref, top_ref, sems):
    loads = (
        pltpu.make_async_copy(qt_hbm, qt_ref, sems.at[0]),
        pltpu.make_async_copy(kv_hbm, kv_ref, sems.at[1]),
    )
    for copy in loads:
        copy.start()
    for copy in loads:
        copy.wait()
    attend(len_ref[0], kv_ref, qt_ref, acc_ref, top_ref, out_ref)


def attention(length, qt, kv):
    columns = qt.shape[1]
    remote = pl.BlockSpec(memory_space=pltpu.HBM)
    return pl.pallas_call(
        attention_kernel,
        out_shape=jax.ShapeDtypeStruct((S_NEW, columns // S_NEW * HEAD_DIM), jnp.bfloat16),
        in_specs=[pl.BlockSpec(memory_space=pltpu.SMEM), remote, remote],
        out_specs=pl.BlockSpec(memory_space=pltpu.VMEM),
        scratch_shapes=[
            pltpu.VMEM(qt.shape, jnp.bfloat16),
            pltpu.VMEM(kv.shape, jnp.bfloat16),
            pltpu.VMEM((VROWS, columns), jnp.float32),
            pltpu.VMEM((1, columns), jnp.float32),
            pltpu.SemaphoreType.DMA((2,)),
        ],
        compiler_params=pltpu.CompilerParams(vmem_limit_bytes=20 << 20),
        cost_estimate=pl.CostEstimate(
            flops=4 * 10**10, transcendentals=10**8, bytes_accessed=100 * 10**6
        ),
        name="attention",
    )(length, in_hbm(qt), in_hbm(kv))


def out_kernel(
    src_ref, request_ref, gain_ref, rows_hbm, w_same, w_others, a_same, a_others, residual_hbm,
    normed_hbm, att_ref, sum_ref, rows_ref, normed_ref, row_sem, out_sems,
):
    full_rows = rows_ref.shape[0]
    at = pl.multiple_of(request_ref[0] * full_rows, full_rows)
    load = pltpu.make_async_copy(rows_hbm.at[pl.ds(at, full_rows)], rows_ref, row_sem)
    load.start()
    for i in range(Z):
        att_ref[src_ref[i]] = a_same[i]
        att_ref[src_ref[Z + i]] = a_others[i]

    def columns(i, carry):
        attended = jnp.concatenate([att_ref[j] for j in range(2 * Z)], axis=1)
        sum_ref[src_ref[i]] = contract(attended, w_same[i])
        sum_ref[src_ref[Z + i]] = contract(attended, w_others[i])
        return carry

    lax.fori_loop(0, Z, columns, 0)
    load.wait()
    total = jnp.concatenate([sum_ref[i] for i in range(2 * Z)], axis=1)
    rows_ref[...] = (rows_ref[...].astype(jnp.float32) + total).astype(jnp.bfloat16)
    keep = pltpu.make_async_copy(rows_ref, residual_hbm, out_sems.at[0])
    keep.start()
    normed_ref[...] = mean_norm(rows_ref[...], gain_ref[...])
    give = pltpu.make_async_copy(normed_ref, normed_hbm, out_sems.at[1])
    give.start()
    keep.wait()
    give.wait()


def project_out(src, gain, weights, rows, pieces, request):
    piece_rows, piece_width = pieces[0].shape[1:]
    width = rows.shape[1]
    cols = weights[0].shape[2]
    scalar = pl.BlockSpec(memory_space=pltpu.SMEM)
    whole = pl.BlockSpec(memory_space=pltpu.VMEM)
    return pl.pallas_call(
        out_kernel,
        out_shape=(pltpu.HBM((piece_rows, width), jnp.bfloat16),) * 2,
        in_specs=[scalar, scalar, whole, pl.BlockSpec(memory_space=pltpu.HBM)] + [whole] * 4,
        out_specs=(pl.BlockSpec(memory_space=pltpu.HBM),) * 2,
        scratch_shapes=[
            pltpu.VMEM((2 * Z, piece_rows, piece_width), jnp.bfloat16),
            pltpu.VMEM((2 * Z, piece_rows, cols), jnp.float32),
            pltpu.VMEM((piece_rows, width), jnp.bfloat16),
            pltpu.VMEM((piece_rows, width), jnp.bfloat16),
            pltpu.SemaphoreType.DMA,
            pltpu.SemaphoreType.DMA((2,)),
        ],
        compiler_params=pltpu.CompilerParams(vmem_limit_bytes=20 << 20),
        cost_estimate=pl.CostEstimate(
            flops=4 * 10**9, transcendentals=0, bytes_accessed=16 * 10**6
        ),
        name="project_out",
    )(src, jnp.full((1,), request, jnp.int32), gain, in_hbm(rows), *weights, *pieces)


def ff_kernel(
    place_ref, low_hbm, high_hbm, w_ref, mine_ref, theirs_ref, x_ref, hidden_ref, x_sems
):
    shards, height, lanes = w_ref.shape
    width = x_ref.shape[3]
    units = hidden_ref.shape[1]
    rows = x_ref.shape[2]
    count = low_hbm.shape[0]
    row_at = pl.multiple_of(place_ref[1] * rows, rows)
    x_loads = []
    for i in range(2 * count):
        side = lax.rem(place_ref[0] + i % 2, 2)
        x_loads.append(
            pltpu.make_async_copy(
                (low_hbm, high_hbm)[i // count].at[i % count, pl.ds(row_at, rows)],
                x_ref.at[side, i // 2],
                x_sems.at[i],
            )
        )
    for copy in x_loads:
        copy.start()
    for copy in x_loads:
        copy.wait()
    x = x_ref[...].reshape(2 * Z * rows, width)
    for i in range(0, units, FF_PAIR):
        size = min(FF_PAIR, units - i)
        both = lax.dot_general(
            x,
            jnp.concatenate(
                [
                    jnp.concatenate([w_ref[j, at : at + size] for j in range(shards)], axis=1)
                    for at in (i, units + i)
                ],
                axis=0,
            ),
            (((1,), (1,)), ((), ())),
            preferred_element_type=jnp.float32,
        )
        hidden_ref[:, i : i + size] = (jax.nn.silu(both[:, :size]) * both[:, size:]).astype(
            jnp.bfloat16
        )
    hidden = hidden_ref[...]
    for i in range(0, shards, 2):
        down = jnp.concatenate([w_ref[i, 2 * units :], w_ref[i + 1, 2 * units :]], axis=1)
        terms = contract(hidden, down).astype(jnp.bfloat16).reshape(2, Z, rows, 2 * lanes)
        mine_ref[:, :, i * lanes : (i + 2) * lanes] = terms[0]
        theirs_ref[:, :, i * lanes : (i + 2) * lanes] = terms[1]


def feed_forward(place, low, high, weights, units):
    count, group_rows, width = low.shape
    rows = group_rows // 2
    whole = pl.BlockSpec(memory_space=pltpu.VMEM)
    remote = pl.BlockSpec(memory_space=pl.ANY)
    return pl.pallas_call(
        ff_kernel,
        out_shape=(jax.ShapeDtypeStruct((Z, rows, width), jnp.bfloat16),) * 2,
        in_specs=[pl.BlockSpec(memory_space=pltpu.SMEM), remote, remote, whole],
        out_specs=(whole, whole),
        scratch_shapes=[
            pltpu.VMEM((2, Z, rows, width), jnp.bfloat16),
            pltpu.VMEM((2 * count * rows, units), jnp.bfloat16),
            pltpu.SemaphoreType.DMA((2 * count,)),
        ],
        compiler_params=pltpu.CompilerParams(vmem_limit_bytes=20 << 20),
        cost_estimate=pl.CostEstimate(
            flops=5 * 10**9, transcendentals=10**6, bytes_accessed=16 * 10**6
        ),
        name="feed_forward",
    )(place, in_hbm(low), in_hbm(high), weights)


def angles_of(cached_len):
    half = HEAD_DIM // 2
    frequency = ROPE_BASE ** (-jnp.arange(half).astype(jnp.float32) * 2.0 / HEAD_DIM)
    positions = (cached_len[:, None] + jnp.arange(S_NEW)[None, :]).reshape(-1)
    angles = frequency[:, None] * positions.astype(jnp.float32)[None, :]
    return jnp.cos(angles), jnp.sin(angles)


def per_device(
    hidden_in, attn_gain, w_qkv, w_out, mlp_gain, w_gate, w_up, w_down, cache_kv, cached_len
):
    head_count = lax.axis_size("head")
    head_index = lax.axis_index("head")
    q_width = HEADS * HEAD_DIM
    kv_width = KV_HEADS * HEAD_DIM
    q_dev = q_width // head_count
    split_count = head_count // KV_HEADS
    part_index = head_index % split_count
    kv_head = head_index // split_count
    units = w_gate.shape[1]
    half_z = Z // 2
    row_count, width = hidden_in.shape

    src = sources()
    own = cache_kv[:, 0]
    other = exchange(own)
    columns = jnp.concatenate(
        [
            lax.dynamic_slice_in_dim(w_qkv, head_index * q_dev, q_dev, 1),
            lax.dynamic_slice_in_dim(w_qkv, q_width + kv_head * HEAD_DIM, HEAD_DIM, 1),
            lax.dynamic_slice_in_dim(w_qkv, q_width + kv_width + kv_head * HEAD_DIM, HEAD_DIM, 1),
        ],
        axis=1,
    )
    spread = jnp.broadcast_to(columns[None], (lax.axis_size("tok"), *columns.shape))
    spread, x_own = lax.optimization_barrier((spread, hidden_in))
    group_w = lax.all_to_all(spread, "tok", 0, 0, tiled=True).reshape(width, columns.shape[1])
    x_same = [x_own] + [along_z(x_own, d) for d in range(1, Z)]
    out_cols = width // head_count
    out_own = jnp.concatenate(
        [
            lax.dynamic_slice_in_dim(w_out, block * out_cols, out_cols, 1)
            for block in (head_index, (head_index + half_z * 2) % head_count)
        ],
        axis=1,
    )
    out_own, group_w, other, *x_same = lax.optimization_barrier((out_own, group_w, other, *x_same))
    x_others = exchange(jnp.stack(x_same))
    out_pair = lax.all_to_all(
        jnp.broadcast_to(out_own[None], (lax.axis_size("tok"), *out_own.shape)), "tok", 0, 0,
        tiled=True,
    ).reshape(width, out_own.shape[1])
    ff_part = jnp.concatenate([w_gate.T, w_up.T, w_down], axis=0)
    cosine, sine = angles_of(cached_len)
    qt_0, qt_1, kv_0, kv_1, cache_new, rows = prepare(
        cached_len, part_index.reshape(1), src, attn_gain[None], cosine, sine, group_w,
        x_same, x_others, own, other,
    )
    ff_part, out_pair, qt_0 = lax.optimization_barrier((ff_part, out_pair, qt_0))
    ff_weights = lax.all_gather(ff_part, "tok", axis=0)
    att_0 = attention(cached_len[:1], qt_0, kv_0)
    out_part = out_pair[:, :out_cols]
    out_far = [along_z(out_part, 1), along_z(out_part, Z - 1)]
    att_0, out_part, out_pair, *out_far = lax.optimization_barrier(
        (att_0, out_part, out_pair, *out_far)
    )
    out_same = jnp.stack([out_part, out_far[0], out_pair[:, out_cols:], out_far[1]])
    out_pieces = (out_same, exchange(out_same))
    far_0 = [along_z(att_0, d) for d in range(1, Z)]
    att_1 = attention(cached_len[1:], qt_1, kv_1)
    att_1, att_0, *far_0 = lax.optimization_barrier((att_1, att_0, *far_0))
    same_0 = jnp.stack([att_0] + far_0)
    pieces_0 = (same_0, exchange(same_0))
    far_1 = [along_z(att_1, d) for d in range(1, Z)]
    gain = mlp_gain[None]
    residual_0, normed_0 = project_out(src, gain, out_pieces, rows, pieces_0, 0)
    att_1, residual_0, ff_weights, *far_1 = lax.optimization_barrier(
        (att_1, residual_0, ff_weights, *far_1)
    )
    same_1 = jnp.stack([att_1] + far_1)
    pieces_1 = (same_1, exchange(same_1))
    residual_1, normed_1 = project_out(src, gain, out_pieces, rows, pieces_1, 1)
    half_count = head_count // 2
    low = normed_0.reshape(half_count, row_count, width)
    high = normed_1.reshape(half_count, row_count, width)
    z = head_index // 2
    core = head_index % 2
    own_0 = lax.dynamic_index_in_dim(
        residual_0.reshape(half_count, row_count, width), head_index % half_count, 0, keepdims=False
    )
    own_1 = lax.dynamic_index_in_dim(
        residual_1.reshape(half_count, row_count, width), head_index % half_count, 0, keepdims=False
    )
    residual = jnp.where(head_index < half_count, own_0, own_1)
    outs = []
    for chunk in range(2):
        place = jnp.stack([core, jnp.int32(chunk)]).astype(jnp.int32)
        mine, theirs = feed_forward(place, low, high, ff_weights, units)
        pair = (mine.astype(jnp.float32) + exchange(theirs).astype(jnp.float32)).astype(
            jnp.bfloat16
        )
        rows_here = row_count // 2
        total = residual[chunk * rows_here : (chunk + 1) * rows_here].astype(jnp.float32)
        total = total + lax.dynamic_index_in_dim(pair, z, 0, keepdims=False).astype(jnp.float32)
        for d in range(1, Z):
            sent = lax.dynamic_index_in_dim(pair, (z + d) % Z, 0, keepdims=False)
            total = total + along_z(sent, d).astype(jnp.float32)
        outs.append(total.astype(jnp.bfloat16))
    return (jnp.concatenate(outs), cache_new[:, None])


def solution(mesh):
    return jax.shard_map(
        per_device,
        mesh=mesh,
        in_specs=(
            P(("tok", "head"), None),
            P(),
            P("tok", None),
            P("tok", None),
            P(),
            P("tok", "head"),
            P("tok", "head"),
            P("head", "tok"),
            P("tok", "head", None, None),
            P("tok"),
        ),
        out_specs=(P(("tok", "head"), None), P("tok", "head", None, None)),
        check_vma=False,
    )
```

```python
import jax
import jax.numpy as jnp
from jax import lax
from jax.experimental import pallas as pl
from jax.experimental.pallas import tpu as pltpu
from jax.sharding import PartitionSpec as P

HEADS = 32
KV_HEADS = 4
HEAD_DIM = 64
S_NEW = 512
ROPE_BASE = 10000.0

KEYS = 512
ALIGN = 16
WINDOW = S_NEW + ALIGN
LOG2_E = 1.4426950408889634
VROWS = HEAD_DIM + 16


Z = 4
FF_PAIR = 128


def mean_norm(values, gain):
    widened = values.astype(jnp.float32)
    spread = jnp.mean(widened * widened, axis=-1, keepdims=True)
    return (widened * lax.rsqrt(spread + 1e-05) * gain).astype(jnp.bfloat16)


def contract(left_rows, right_rows):
    return jnp.dot(left_rows, right_rows, preferred_element_type=jnp.float32)


def in_hbm(array):
    return pltpu.with_memory_space_constraint(array, pltpu.HBM)


def exchange(array):
    return lax.ppermute(array, "head", [(i, i ^ 1) for i in range(lax.axis_size("head"))])


def along_z(array, distance):
    count = lax.axis_size("head")
    return lax.ppermute(array, "head", [(i, (i + 2 * distance) % count) for i in range(count)])


def gather_head(array):
    same_core = jnp.stack([array] + [along_z(array, d) for d in range(1, Z)])
    return same_core, exchange(same_core)


def sources():
    head_index = lax.axis_index("head")
    z, core = head_index // 2, head_index % 2
    chips = (z - jnp.arange(Z)) % Z * 2
    return jnp.concatenate([chips + core, chips + 1 - core]).astype(jnp.int32)


def attend(length, kv_ref, qt_ref, acc_ref, top_ref, out_ref):
    lanes = kv_ref.shape[1]
    acc_ref[...] = jnp.zeros(acc_ref.shape, jnp.float32)
    top_ref[...] = jnp.full(top_ref.shape, -1e30, jnp.float32)

    def step(index, masked, here):
        at = pl.multiple_of(index * KEYS, KEYS)
        block = kv_ref[pl.ds(at, KEYS)].astype(jnp.float32)
        on_key = lax.broadcasted_iota(jnp.int32, (KEYS, lanes), 1) < HEAD_DIM
        values = jnp.where(on_key, 1.0, block).T[HEAD_DIM - 16 :].astype(jnp.bfloat16)
        keys = jnp.where(on_key, block, pltpu.roll(block, HEAD_DIM, 1)).astype(jnp.bfloat16)
        scores = contract(keys, qt_ref[:, here])
        if masked:
            key = lax.broadcasted_iota(jnp.int32, scores.shape, 0) + (index * KEYS - length)
            query = lax.broadcasted_iota(jnp.int32, scores.shape, 1)
            scores = jnp.where(key <= query, scores, -jnp.inf)
        old_top = top_ref[:, here]
        top = jnp.maximum(jnp.max(scores, axis=0, keepdims=True), old_top)
        exps = jnp.exp2(scores - top).astype(jnp.bfloat16)
        acc_ref[:, here] = contract(values, exps) + acc_ref[:, here] * jnp.exp2(old_top - top)
        top_ref[:, here] = top

    def last(index, carry):
        def one_head(h, inner):
            step(index, True, pl.ds(pl.multiple_of(h * S_NEW, S_NEW), S_NEW))
            return inner

        return lax.fori_loop(0, qt_ref.shape[1] // S_NEW, one_head, carry)

    def full(index, carry):
        step(index, False, slice(None))
        return carry

    tail = length // KEYS
    lax.fori_loop(tail, (length + S_NEW + KEYS - 1) // KEYS, last, 0)
    lax.fori_loop(0, tail, full, 0)
    for pair in range(qt_ref.shape[1] // (2 * S_NEW)):
        sides = []
        for h in (2 * pair, 2 * pair + 1):
            here = slice(h * S_NEW, (h + 1) * S_NEW)
            sides.append(acc_ref[16:, here] / acc_ref[:1, here])
        out_ref[:, pair * lanes : (pair + 1) * lanes] = (
            jnp.concatenate(sides, axis=0).T.astype(jnp.bfloat16)
        )


def prepare_kernel(
    lens_ref, part_ref, src_ref, gain_ref, cos_ref, sin_ref, w_ref, x_0, x_1, x_2, x_3, x_others,
    own_hbm, other_hbm, qt_0, qt_1, kv_0, kv_1, cache_hbm, rows_hbm, x_ref, kv_ref, new_ref,
    qt_ref, x_sems, load_sems, store_sems,
):
    req_count, block_pos, lanes = own_hbm.shape
    heads_dev = qt_0.shape[1] // S_NEW
    half = HEAD_DIM // 2
    x_pieces = [x_0, x_1, x_2, x_3] + [x_others.at[i] for i in range(Z)]
    piece_rows = x_0.shape[0]
    own_at = pl.multiple_of(part_ref[0] * block_pos, ALIGN)
    other_at = pl.multiple_of((1 - part_ref[0]) * block_pos, ALIGN)

    def x_load(i):
        at = pl.multiple_of(src_ref[i] * piece_rows, piece_rows)
        return pltpu.make_async_copy(x_pieces[i], x_ref.at[pl.ds(at, piece_rows)], x_sems.at[i])

    def loads(r):
        return (
            pltpu.make_async_copy(
                own_hbm.at[r], kv_ref.at[r, pl.ds(own_at, block_pos)], load_sems.at[r, 0]
            ),
            pltpu.make_async_copy(
                other_hbm.at[r], kv_ref.at[r, pl.ds(other_at, block_pos)], load_sems.at[r, 1]
            ),
        )

    def stores(r):
        return (
            pltpu.make_async_copy(
                kv_ref.at[r, pl.ds(own_at, block_pos)], cache_hbm.at[r], store_sems.at[r, 0]
            ),
            pltpu.make_async_copy(kv_ref.at[r], (kv_0, kv_1)[r], store_sems.at[r, 1]),
            pltpu.make_async_copy(qt_ref.at[r], (qt_0, qt_1)[r], store_sems.at[r, 2]),
        )

    for i in range(2 * Z):
        x_load(i).start()
    for r in range(req_count):
        for copy in loads(r):
            copy.start()
    for i in range(2 * Z):
        x_load(i).wait()
    keep = pltpu.make_async_copy(x_ref, rows_hbm, store_sems.at[req_count, 0])
    keep.start()

    q_lanes = heads_dev * HEAD_DIM
    gain = gain_ref[...]
    def project(r, carry):
        here = pl.ds(pl.multiple_of(r * S_NEW, S_NEW), S_NEW)
        cosine = cos_ref[:, here]
        sine = sin_ref[:, here]

        def turn(block, scale):
            first = block[:half]
            second = block[half:]
            return jnp.concatenate(
                [
                    (first * cosine - second * sine) * scale,
                    (second * cosine + first * sine) * scale,
                ],
                axis=0,
            )

        normed = mean_norm(x_ref[here], gain)
        projected = contract(normed, w_ref[...])
        for pair in range(heads_dev // 2):
            flipped = projected[:, pair * lanes : (pair + 1) * lanes].T
            for one in range(2):
                rows = turn(flipped[one * HEAD_DIM : (one + 1) * HEAD_DIM], HEAD_DIM**-0.5)
                rows = rows.astype(jnp.bfloat16).astype(jnp.float32) * LOG2_E
                upper = rows.astype(jnp.bfloat16)
                lower = (rows - upper.astype(jnp.float32)).astype(jnp.bfloat16)
                at = (2 * pair + one) * S_NEW
                qt_ref[r, :HEAD_DIM, at : at + S_NEW] = upper
                qt_ref[r, HEAD_DIM:, at : at + S_NEW] = lower
        flipped = projected[:, q_lanes:].T
        fresh = jnp.concatenate([turn(flipped[:HEAD_DIM], 1.0), flipped[HEAD_DIM:]], axis=0)
        new_ref[r] = fresh.T.astype(jnp.bfloat16)
        return carry

    lax.fori_loop(0, req_count, project, 0)

    for r in range(req_count):
        length = lens_ref[r]
        for copy in loads(r):
            copy.wait()
        shift = length % ALIGN
        window_at = pl.multiple_of(length - shift, ALIGN)
        row = lax.broadcasted_iota(jnp.int32, (WINDOW, S_NEW), 0)
        col = lax.broadcasted_iota(jnp.int32, (WINDOW, S_NEW), 1)
        pick = (row - shift == col).astype(jnp.float32).astype(jnp.bfloat16)
        moved = contract(pick, new_ref[r])
        row = lax.broadcasted_iota(jnp.int32, (WINDOW, lanes), 0)
        inside = (row >= shift) & (row < shift + S_NEW)
        old = kv_ref[r, pl.ds(window_at, WINDOW)].astype(jnp.float32)
        kv_ref[r, pl.ds(window_at, WINDOW)] = jnp.where(inside, moved, old).astype(jnp.bfloat16)
        for copy in stores(r):
            copy.start()

    for r in range(req_count):
        for copy in stores(r):
            copy.wait()
    keep.wait()


def prepare(lens, part, src, gain, cosine, sine, w, x_same, x_others, own, other):
    req_count, block_pos, lanes = own.shape
    piece_rows, width = x_same[0].shape
    rows = piece_rows * 2 * Z
    heads_dev = (w.shape[1] - lanes) // HEAD_DIM
    positions = 2 * block_pos + ALIGN
    whole = pl.BlockSpec(memory_space=pltpu.VMEM)
    scalar = pl.BlockSpec(memory_space=pltpu.SMEM)
    remote = pl.BlockSpec(memory_space=pl.ANY)
    return pl.pallas_call(
        prepare_kernel,
        out_shape=(
            pltpu.HBM((lanes, heads_dev * S_NEW), jnp.bfloat16),
            pltpu.HBM((lanes, heads_dev * S_NEW), jnp.bfloat16),
            pltpu.HBM((positions, lanes), jnp.bfloat16),
            pltpu.HBM((positions, lanes), jnp.bfloat16),
            pltpu.HBM(own.shape, jnp.bfloat16),
            pltpu.HBM((rows, width), jnp.bfloat16),
        ),
        in_specs=[scalar] * 3 + [whole] * 4 + [remote] * (Z + 3),
        out_specs=(pl.BlockSpec(memory_space=pltpu.HBM),) * 6,
        scratch_shapes=[
            pltpu.VMEM((rows, width), jnp.bfloat16),
            pltpu.VMEM((req_count, positions, lanes), jnp.bfloat16),
            pltpu.VMEM((req_count, S_NEW, lanes), jnp.bfloat16),
            pltpu.VMEM((req_count, lanes, heads_dev * S_NEW), jnp.bfloat16),
            pltpu.SemaphoreType.DMA((2 * Z,)),
            pltpu.SemaphoreType.DMA((req_count, 2)),
            pltpu.SemaphoreType.DMA((req_count + 1, 3)),
        ],
        compiler_params=pltpu.CompilerParams(vmem_limit_bytes=22 << 20),
        cost_estimate=pl.CostEstimate(
            flops=4 * 10**9, transcendentals=10**6, bytes_accessed=20 * 10**6
        ),
        name="prepare",
    )(lens, part, src, gain, cosine, sine, w, *x_same, x_others, in_hbm(own), other)


def attention_kernel(len_ref, qt_hbm, kv_hbm, out_ref, qt_ref, kv_ref, acc_ref, top_ref, sems):
    loads = (
        pltpu.make_async_copy(qt_hbm, qt_ref, sems.at[0]),
        pltpu.make_async_copy(kv_hbm, kv_ref, sems.at[1]),
    )
    for copy in loads:
        copy.start()
    for copy in loads:
        copy.wait()
    attend(len_ref[0], kv_ref, qt_ref, acc_ref, top_ref, out_ref)


def attention(length, qt, kv):
    columns = qt.shape[1]
    remote = pl.BlockSpec(memory_space=pltpu.HBM)
    return pl.pallas_call(
        attention_kernel,
        out_shape=jax.ShapeDtypeStruct((S_NEW, columns // S_NEW * HEAD_DIM), jnp.bfloat16),
        in_specs=[pl.BlockSpec(memory_space=pltpu.SMEM), remote, remote],
        out_specs=pl.BlockSpec(memory_space=pltpu.VMEM),
        scratch_shapes=[
            pltpu.VMEM(qt.shape, jnp.bfloat16),
            pltpu.VMEM(kv.shape, jnp.bfloat16),
            pltpu.VMEM((VROWS, columns), jnp.float32),
            pltpu.VMEM((1, columns), jnp.float32),
            pltpu.SemaphoreType.DMA((2,)),
        ],
        compiler_params=pltpu.CompilerParams(vmem_limit_bytes=16 << 20),
        cost_estimate=pl.CostEstimate(
            flops=4 * 10**10, transcendentals=10**8, bytes_accessed=100 * 10**6
        ),
        name="attention",
    )(length, in_hbm(qt), in_hbm(kv))


def out_kernel(
    src_ref, request_ref, gain_ref, rows_hbm, w_same, w_others, a_same, a_others, residual_hbm,
    normed_hbm, att_ref, w_ref, sum_ref, rows_ref, normed_ref, row_sem, out_sems, w_sems,
):
    def w_load(side, i):
        source = (w_same, w_others)[side]
        return pltpu.make_async_copy(source.at[i], w_ref.at[side, i], w_sems.at[side, i])

    full_rows = rows_ref.shape[0]
    at = pl.multiple_of(request_ref[0] * full_rows, full_rows)
    load = pltpu.make_async_copy(rows_hbm.at[pl.ds(at, full_rows)], rows_ref, row_sem)
    for i in range(Z):
        w_load(0, i).start()
        w_load(1, i).start()
    load.start()
    for i in range(Z):
        att_ref[src_ref[i]] = a_same[i]
        att_ref[src_ref[Z + i]] = a_others[i]

    def columns(i, carry):
        attended = jnp.concatenate([att_ref[j] for j in range(2 * Z)], axis=1)
        w_load(0, i).wait()
        w_load(1, i).wait()
        sum_ref[src_ref[i]] = contract(attended, w_ref[0, i])
        sum_ref[src_ref[Z + i]] = contract(attended, w_ref[1, i])
        return carry

    lax.fori_loop(0, Z, columns, 0)
    load.wait()
    total = jnp.concatenate([sum_ref[i] for i in range(2 * Z)], axis=1)
    rows_ref[...] = (rows_ref[...].astype(jnp.float32) + total).astype(jnp.bfloat16)
    keep = pltpu.make_async_copy(rows_ref, residual_hbm, out_sems.at[0])
    keep.start()
    normed_ref[...] = mean_norm(rows_ref[...], gain_ref[...])
    give = pltpu.make_async_copy(normed_ref, normed_hbm, out_sems.at[1])
    give.start()
    keep.wait()
    give.wait()


def project_out(src, gain, weights, rows, pieces, request):
    piece_rows, piece_width = pieces[0].shape[1:]
    width = rows.shape[1]
    cols = weights[0].shape[2]
    scalar = pl.BlockSpec(memory_space=pltpu.SMEM)
    whole = pl.BlockSpec(memory_space=pltpu.VMEM)
    remote = pl.BlockSpec(memory_space=pltpu.HBM)
    return pl.pallas_call(
        out_kernel,
        out_shape=(pltpu.HBM((piece_rows, width), jnp.bfloat16),) * 2,
        in_specs=[scalar, scalar, whole] + [remote] * 3 + [whole] * 2,
        out_specs=(pl.BlockSpec(memory_space=pltpu.HBM),) * 2,
        scratch_shapes=[
            pltpu.VMEM((2 * Z, piece_rows, piece_width), jnp.bfloat16),
            pltpu.VMEM((2, Z, width, cols), jnp.bfloat16),
            pltpu.VMEM((2 * Z, piece_rows, cols), jnp.float32),
            pltpu.VMEM((piece_rows, width), jnp.bfloat16),
            pltpu.VMEM((piece_rows, width), jnp.bfloat16),
            pltpu.SemaphoreType.DMA,
            pltpu.SemaphoreType.DMA((2,)),
            pltpu.SemaphoreType.DMA((2, Z)),
        ],
        compiler_params=pltpu.CompilerParams(vmem_limit_bytes=27 << 20),
        cost_estimate=pl.CostEstimate(
            flops=4 * 10**9, transcendentals=0, bytes_accessed=16 * 10**6
        ),
        name="project_out",
    )(src, jnp.full((1,), request, jnp.int32), gain, in_hbm(rows), *map(in_hbm, weights), *pieces)


def ff_kernel(
    place_ref, low_hbm, high_hbm, w_ref, mine_ref, theirs_ref, x_ref, hidden_ref, x_sems
):
    shards, height, lanes = w_ref.shape
    width = x_ref.shape[3]
    units = hidden_ref.shape[1]
    rows = x_ref.shape[2]
    count = low_hbm.shape[0]
    row_at = pl.multiple_of(place_ref[1] * rows, rows)
    x_loads = []
    for i in range(2 * count):
        side = lax.rem(place_ref[0] + i % 2, 2)
        x_loads.append(
            pltpu.make_async_copy(
                (low_hbm, high_hbm)[i // count].at[i % count, pl.ds(row_at, rows)],
                x_ref.at[side, i // 2],
                x_sems.at[i],
            )
        )
    for copy in x_loads:
        copy.start()
    for copy in x_loads:
        copy.wait()
    x = x_ref[...].reshape(2 * Z * rows, width)
    for i in range(0, units, FF_PAIR):
        size = min(FF_PAIR, units - i)
        both = lax.dot_general(
            x,
            jnp.concatenate(
                [
                    jnp.concatenate([w_ref[j, at : at + size] for j in range(shards)], axis=1)
                    for at in (i, units + i)
                ],
                axis=0,
            ),
            (((1,), (1,)), ((), ())),
            preferred_element_type=jnp.float32,
        )
        hidden_ref[:, i : i + size] = (jax.nn.silu(both[:, :size]) * both[:, size:]).astype(
            jnp.bfloat16
        )
    hidden = hidden_ref[...]
    for i in range(0, shards, 2):
        down = jnp.concatenate([w_ref[i, 2 * units :], w_ref[i + 1, 2 * units :]], axis=1)
        terms = contract(hidden, down).astype(jnp.bfloat16).reshape(2, Z, rows, 2 * lanes)
        mine_ref[:, :, i * lanes : (i + 2) * lanes] = terms[0]
        theirs_ref[:, :, i * lanes : (i + 2) * lanes] = terms[1]


def feed_forward(place, low, high, weights, units):
    count, group_rows, width = low.shape
    rows = group_rows // 2
    whole = pl.BlockSpec(memory_space=pltpu.VMEM)
    remote = pl.BlockSpec(memory_space=pl.ANY)
    return pl.pallas_call(
        ff_kernel,
        out_shape=(jax.ShapeDtypeStruct((Z, rows, width), jnp.bfloat16),) * 2,
        in_specs=[pl.BlockSpec(memory_space=pltpu.SMEM), remote, remote, whole],
        out_specs=(whole, whole),
        scratch_shapes=[
            pltpu.VMEM((2, Z, rows, width), jnp.bfloat16),
            pltpu.VMEM((2 * count * rows, units), jnp.bfloat16),
            pltpu.SemaphoreType.DMA((2 * count,)),
        ],
        compiler_params=pltpu.CompilerParams(vmem_limit_bytes=12 << 20),
        cost_estimate=pl.CostEstimate(
            flops=5 * 10**9, transcendentals=10**6, bytes_accessed=16 * 10**6
        ),
        name="feed_forward",
    )(place, in_hbm(low), in_hbm(high), weights)


def angles_of(cached_len):
    half = HEAD_DIM // 2
    frequency = ROPE_BASE ** (-jnp.arange(half).astype(jnp.float32) * 2.0 / HEAD_DIM)
    positions = (cached_len[:, None] + jnp.arange(S_NEW)[None, :]).reshape(-1)
    angles = frequency[:, None] * positions.astype(jnp.float32)[None, :]
    return jnp.cos(angles), jnp.sin(angles)


def per_device(
    hidden_in, attn_gain, w_qkv, w_out, mlp_gain, w_gate, w_up, w_down, cache_kv, cached_len
):
    head_count = lax.axis_size("head")
    head_index = lax.axis_index("head")
    q_width = HEADS * HEAD_DIM
    kv_width = KV_HEADS * HEAD_DIM
    q_dev = q_width // head_count
    split_count = head_count // KV_HEADS
    part_index = head_index % split_count
    kv_head = head_index // split_count
    units = w_gate.shape[1]
    half_z = Z // 2
    row_count, width = hidden_in.shape

    src = sources()
    own = cache_kv[:, 0]
    other = exchange(own)
    columns = jnp.concatenate(
        [
            lax.dynamic_slice_in_dim(w_qkv, head_index * q_dev, q_dev, 1),
            lax.dynamic_slice_in_dim(w_qkv, q_width + kv_head * HEAD_DIM, HEAD_DIM, 1),
            lax.dynamic_slice_in_dim(w_qkv, q_width + kv_width + kv_head * HEAD_DIM, HEAD_DIM, 1),
        ],
        axis=1,
    )
    spread = jnp.broadcast_to(columns[None], (lax.axis_size("tok"), *columns.shape))
    spread, x_own = lax.optimization_barrier((spread, hidden_in))
    group_w = lax.all_to_all(spread, "tok", 0, 0, tiled=True).reshape(width, columns.shape[1])
    x_same = [x_own] + [along_z(x_own, d) for d in range(1, Z)]
    out_cols = width // head_count
    out_pair = lax.all_gather(
        jnp.concatenate(
            [
                lax.dynamic_slice_in_dim(w_out, block * out_cols, out_cols, 1)
                for block in (head_index, (head_index + half_z * 2) % head_count)
            ],
            axis=1,
        ),
        "tok", axis=0, tiled=True,
    )
    x_others = exchange(jnp.stack(x_same))
    ff_part, group_w, other, *_ = lax.optimization_barrier(
        (jnp.concatenate([w_gate.T, w_up.T, w_down], axis=0), group_w, other, *x_same)
    )
    ff_weights = lax.all_gather(ff_part, "tok", axis=0)
    cosine, sine = angles_of(cached_len)
    qt_0, qt_1, kv_0, kv_1, cache_new, rows = prepare(
        cached_len, part_index.reshape(1), src, attn_gain[None], cosine, sine, group_w,
        x_same, x_others, own, other,
    )
    out_pair, qt_0 = lax.optimization_barrier((out_pair, qt_0))
    att_0 = attention(cached_len[:1], qt_0, kv_0)
    out_part = out_pair[:, :out_cols]
    out_far = [along_z(out_part, 1), along_z(out_part, Z - 1)]
    att_0, out_part, out_pair, *out_far = lax.optimization_barrier(
        (att_0, out_part, out_pair, *out_far)
    )
    out_same = jnp.stack([out_part, out_far[0], out_pair[:, out_cols:], out_far[1]])
    out_pieces = (out_same, exchange(out_same))
    far_0 = [along_z(att_0, d) for d in range(1, Z)]
    att_1 = attention(cached_len[1:], qt_1, kv_1)
    att_1, att_0, *far_0 = lax.optimization_barrier((att_1, att_0, *far_0))
    same_0 = jnp.stack([att_0] + far_0)
    pieces_0 = (same_0, exchange(same_0))
    far_1 = [along_z(att_1, d) for d in range(1, Z)]
    gain = mlp_gain[None]
    residual_0, normed_0 = project_out(src, gain, out_pieces, rows, pieces_0, 0)
    att_1, residual_0, ff_weights, *far_1 = lax.optimization_barrier(
        (att_1, residual_0, ff_weights, *far_1)
    )
    same_1 = jnp.stack([att_1] + far_1)
    pieces_1 = (same_1, exchange(same_1))
    residual_1, normed_1 = project_out(src, gain, out_pieces, rows, pieces_1, 1)
    half_count = head_count // 2
    low = normed_0.reshape(half_count, row_count, width)
    high = normed_1.reshape(half_count, row_count, width)
    z = head_index // 2
    core = head_index % 2
    own_0 = lax.dynamic_index_in_dim(
        residual_0.reshape(half_count, row_count, width), head_index % half_count, 0, keepdims=False
    )
    own_1 = lax.dynamic_index_in_dim(
        residual_1.reshape(half_count, row_count, width), head_index % half_count, 0, keepdims=False
    )
    residual = jnp.where(head_index < half_count, own_0, own_1)
    outs = []
    for chunk in range(2):
        place = jnp.stack([core, jnp.int32(chunk)]).astype(jnp.int32)
        mine, theirs = feed_forward(place, low, high, ff_weights, units)
        pair = (mine.astype(jnp.float32) + exchange(theirs).astype(jnp.float32)).astype(
            jnp.bfloat16
        )
        rows_here = row_count // 2
        total = residual[chunk * rows_here : (chunk + 1) * rows_here].astype(jnp.float32)
        total = total + lax.dynamic_index_in_dim(pair, z, 0, keepdims=False).astype(jnp.float32)
        for d in range(1, Z):
            sent = lax.dynamic_index_in_dim(pair, (z + d) % Z, 0, keepdims=False)
            total = total + along_z(sent, d).astype(jnp.float32)
        outs.append(total.astype(jnp.bfloat16))
    return (jnp.concatenate(outs), cache_new[:, None])


def solution(mesh):
    return jax.shard_map(
        per_device,
        mesh=mesh,
        in_specs=(
            P(("tok", "head"), None),
            P(),
            P("tok", None),
            P("tok", None),
            P(),
            P("tok", "head"),
            P("tok", "head"),
            P("head", "tok"),
            P("tok", "head", None, None),
            P("tok"),
        ),
        out_specs=(P(("tok", "head"), None), P("tok", "head", None, None)),
        check_vma=False,
    )
```

```python
import jax
import jax.numpy as jnp
from jax import lax
from jax.experimental import pallas as pl
from jax.experimental.pallas import tpu as pltpu
from jax.sharding import PartitionSpec as P

HEADS = 32
KV_HEADS = 4
HEAD_DIM = 64
S_NEW = 512
ROPE_BASE = 10000.0

KEYS = 512
ALIGN = 16
WINDOW = S_NEW + ALIGN
LOG2_E = 1.4426950408889634
VROWS = HEAD_DIM + 16


Z = 4
FF_PAIR = 128


def mean_norm(values, gain):
    widened = values.astype(jnp.float32)
    spread = jnp.mean(widened * widened, axis=-1, keepdims=True)
    return (widened * lax.rsqrt(spread + 1e-05) * gain).astype(jnp.bfloat16)


def contract(left_rows, right_rows):
    return jnp.dot(left_rows, right_rows, preferred_element_type=jnp.float32)


def in_hbm(array):
    return pltpu.with_memory_space_constraint(array, pltpu.HBM)


def exchange(array):
    return lax.ppermute(array, "head", [(i, i ^ 1) for i in range(lax.axis_size("head"))])


def along_z(array, distance):
    count = lax.axis_size("head")
    return lax.ppermute(array, "head", [(i, (i + 2 * distance) % count) for i in range(count)])


def gather_head(array):
    same_core = jnp.stack([array] + [along_z(array, d) for d in range(1, Z)])
    return same_core, exchange(same_core)


def sources():
    head_index = lax.axis_index("head")
    z, core = head_index // 2, head_index % 2
    chips = (z - jnp.arange(Z)) % Z * 2
    return jnp.concatenate([chips + core, chips + 1 - core]).astype(jnp.int32)


def attend(length, kv_ref, qt_ref, acc_ref, top_ref, out_ref):
    lanes = kv_ref.shape[1]
    acc_ref[...] = jnp.zeros(acc_ref.shape, jnp.float32)
    top_ref[...] = jnp.full(top_ref.shape, -1e30, jnp.float32)

    def step(index, masked, here):
        at = pl.multiple_of(index * KEYS, KEYS)
        block = kv_ref[pl.ds(at, KEYS)].astype(jnp.float32)
        on_key = lax.broadcasted_iota(jnp.int32, (KEYS, lanes), 1) < HEAD_DIM
        values = jnp.where(on_key, 1.0, block).T[HEAD_DIM - 16 :].astype(jnp.bfloat16)
        keys = jnp.where(on_key, block, pltpu.roll(block, HEAD_DIM, 1)).astype(jnp.bfloat16)
        scores = contract(keys, qt_ref[:, here])
        if masked:
            key = lax.broadcasted_iota(jnp.int32, scores.shape, 0) + (index * KEYS - length)
            query = lax.broadcasted_iota(jnp.int32, scores.shape, 1)
            scores = jnp.where(key <= query, scores, -jnp.inf)
        old_top = top_ref[:, here]
        top = jnp.maximum(jnp.max(scores, axis=0, keepdims=True), old_top)
        exps = jnp.exp2(scores - top).astype(jnp.bfloat16)
        acc_ref[:, here] = contract(values, exps) + acc_ref[:, here] * jnp.exp2(old_top - top)
        top_ref[:, here] = top

    def last(index, carry):
        def one_head(h, inner):
            step(index, True, pl.ds(pl.multiple_of(h * S_NEW, S_NEW), S_NEW))
            return inner

        return lax.fori_loop(0, qt_ref.shape[1] // S_NEW, one_head, carry)

    def full(index, carry):
        step(index, False, slice(None))
        return carry

    tail = length // KEYS
    lax.fori_loop(tail, (length + S_NEW + KEYS - 1) // KEYS, last, 0)
    lax.fori_loop(0, tail, full, 0)
    for pair in range(qt_ref.shape[1] // (2 * S_NEW)):
        sides = []
        for h in (2 * pair, 2 * pair + 1):
            here = slice(h * S_NEW, (h + 1) * S_NEW)
            sides.append(acc_ref[16:, here] / acc_ref[:1, here])
        out_ref[:, pair * lanes : (pair + 1) * lanes] = (
            jnp.concatenate(sides, axis=0).T.astype(jnp.bfloat16)
        )


def prepare_kernel(
    lens_ref, part_ref, src_ref, gain_ref, cos_ref, sin_ref, w_ref, x_0, x_1, x_2, x_3, x_others,
    own_hbm, other_hbm, qt_hbm, kv_hbm, cache_hbm, rows_hbm, x_ref, kv_ref, new_ref, qt_ref, x_sems, load_sems, store_sems,
):
    req_count, block_pos, lanes = own_hbm.shape
    heads_dev = qt_ref.shape[2] // S_NEW
    half = HEAD_DIM // 2
    x_pieces = [x_0, x_1, x_2, x_3] + [x_others.at[i] for i in range(Z)]
    piece_rows = x_0.shape[0]
    own_at = pl.multiple_of(part_ref[0] * block_pos, ALIGN)
    other_at = pl.multiple_of((1 - part_ref[0]) * block_pos, ALIGN)

    def x_load(i):
        at = pl.multiple_of(src_ref[i] * piece_rows, piece_rows)
        return pltpu.make_async_copy(x_pieces[i], x_ref.at[pl.ds(at, piece_rows)], x_sems.at[i])

    def loads(r):
        return (
            pltpu.make_async_copy(
                own_hbm.at[r], kv_ref.at[r, pl.ds(own_at, block_pos)], load_sems.at[r, 0]
            ),
            pltpu.make_async_copy(
                other_hbm.at[r], kv_ref.at[r, pl.ds(other_at, block_pos)], load_sems.at[r, 1]
            ),
        )

    def stores(r):
        return (
            pltpu.make_async_copy(
                kv_ref.at[r, pl.ds(own_at, block_pos)], cache_hbm.at[r], store_sems.at[r, 0]
            ),
            pltpu.make_async_copy(kv_ref.at[r], kv_hbm.at[r], store_sems.at[r, 1]),
            pltpu.make_async_copy(qt_ref.at[r], qt_hbm.at[r], store_sems.at[r, 2]),
        )

    for i in range(2 * Z):
        x_load(i).start()
    for r in range(req_count):
        for copy in loads(r):
            copy.start()
    for i in range(2 * Z):
        x_load(i).wait()
    keep = pltpu.make_async_copy(x_ref, rows_hbm, store_sems.at[req_count, 0])
    keep.start()

    q_lanes = heads_dev * HEAD_DIM
    gain = gain_ref[...]
    def project(r, carry):
        here = pl.ds(pl.multiple_of(r * S_NEW, S_NEW), S_NEW)
        cosine = cos_ref[:, here]
        sine = sin_ref[:, here]

        def turn(block, scale):
            first = block[:half]
            second = block[half:]
            return jnp.concatenate(
                [
                    (first * cosine - second * sine) * scale,
                    (second * cosine + first * sine) * scale,
                ],
                axis=0,
            )

        normed = mean_norm(x_ref[here], gain)
        projected = contract(normed, w_ref[...])
        for pair in range(heads_dev // 2):
            flipped = projected[:, pair * lanes : (pair + 1) * lanes].T
            for one in range(2):
                rows = turn(flipped[one * HEAD_DIM : (one + 1) * HEAD_DIM], HEAD_DIM**-0.5)
                rows = rows.astype(jnp.bfloat16).astype(jnp.float32) * LOG2_E
                upper = rows.astype(jnp.bfloat16)
                lower = (rows - upper.astype(jnp.float32)).astype(jnp.bfloat16)
                at = (2 * pair + one) * S_NEW
                qt_ref[r, :HEAD_DIM, at : at + S_NEW] = upper
                qt_ref[r, HEAD_DIM:, at : at + S_NEW] = lower
        flipped = projected[:, q_lanes:].T
        fresh = jnp.concatenate([turn(flipped[:HEAD_DIM], 1.0), flipped[HEAD_DIM:]], axis=0)
        new_ref[r] = fresh.T.astype(jnp.bfloat16)

        length = lens_ref[r]
        for copy in loads(r):
            copy.wait()
        shift = length % ALIGN
        window_at = pl.multiple_of(length - shift, ALIGN)
        row = lax.broadcasted_iota(jnp.int32, (WINDOW, S_NEW), 0)
        col = lax.broadcasted_iota(jnp.int32, (WINDOW, S_NEW), 1)
        pick = (row - shift == col).astype(jnp.float32).astype(jnp.bfloat16)
        moved = contract(pick, new_ref[r])
        row = lax.broadcasted_iota(jnp.int32, (WINDOW, lanes), 0)
        inside = (row >= shift) & (row < shift + S_NEW)
        old = kv_ref[r, pl.ds(window_at, WINDOW)].astype(jnp.float32)
        kv_ref[r, pl.ds(window_at, WINDOW)] = jnp.where(inside, moved, old).astype(jnp.bfloat16)
        for copy in stores(r):
            copy.start()
        return carry

    lax.fori_loop(0, req_count, project, 0)
    for r in range(req_count):
        for copy in stores(r):
            copy.wait()
    keep.wait()


def prepare(lens, part, src, gain, cosine, sine, w, x_same, x_others, own, other):
    req_count, block_pos, lanes = own.shape
    piece_rows, width = x_same[0].shape
    rows = piece_rows * 2 * Z
    heads_dev = (w.shape[1] - lanes) // HEAD_DIM
    positions = 2 * block_pos + ALIGN
    whole = pl.BlockSpec(memory_space=pltpu.VMEM)
    scalar = pl.BlockSpec(memory_space=pltpu.SMEM)
    remote = pl.BlockSpec(memory_space=pl.ANY)
    return pl.pallas_call(
        prepare_kernel,
        out_shape=(
            pltpu.HBM((req_count, lanes, heads_dev * S_NEW), jnp.bfloat16),
            pltpu.HBM((req_count, positions, lanes), jnp.bfloat16),
            pltpu.HBM(own.shape, jnp.bfloat16),
            pltpu.HBM((rows, width), jnp.bfloat16),
        ),
        in_specs=[scalar] * 3 + [whole] * 4 + [remote] * (Z + 3),
        out_specs=(pl.BlockSpec(memory_space=pltpu.HBM),) * 4,
        scratch_shapes=[
            pltpu.VMEM((rows, width), jnp.bfloat16),
            pltpu.VMEM((req_count, positions, lanes), jnp.bfloat16),
            pltpu.VMEM((req_count, S_NEW, lanes), jnp.bfloat16),
            pltpu.VMEM((req_count, lanes, heads_dev * S_NEW), jnp.bfloat16),
            pltpu.SemaphoreType.DMA((2 * Z,)),
            pltpu.SemaphoreType.DMA((req_count, 2)),
            pltpu.SemaphoreType.DMA((req_count + 1, 3)),
        ],
        compiler_params=pltpu.CompilerParams(vmem_limit_bytes=22 << 20),
        cost_estimate=pl.CostEstimate(
            flops=4 * 10**9, transcendentals=10**6, bytes_accessed=20 * 10**6
        ),
        name="prepare",
    )(lens, part, src, gain, cosine, sine, w, *x_same, x_others, in_hbm(own), other)


def attention_kernel(which_ref, qt_hbm, kv_hbm, out_ref, qt_ref, kv_ref, acc_ref, top_ref, sems):
    loads = (
        pltpu.make_async_copy(qt_hbm.at[which_ref[1]], qt_ref, sems.at[0]),
        pltpu.make_async_copy(kv_hbm.at[which_ref[1]], kv_ref, sems.at[1]),
    )
    for copy in loads:
        copy.start()
    for copy in loads:
        copy.wait()
    attend(which_ref[0], kv_ref, qt_ref, acc_ref, top_ref, out_ref)


def attention(lens, request, qt, kv):
    columns = qt.shape[2]
    remote = pl.BlockSpec(memory_space=pltpu.HBM)
    return pl.pallas_call(
        attention_kernel,
        out_shape=jax.ShapeDtypeStruct((S_NEW, columns // S_NEW * HEAD_DIM), jnp.bfloat16),
        in_specs=[pl.BlockSpec(memory_space=pltpu.SMEM), remote, remote],
        out_specs=pl.BlockSpec(memory_space=pltpu.VMEM),
        scratch_shapes=[
            pltpu.VMEM(qt.shape[1:], jnp.bfloat16),
            pltpu.VMEM(kv.shape[1:], jnp.bfloat16),
            pltpu.VMEM((VROWS, columns), jnp.float32),
            pltpu.VMEM((1, columns), jnp.float32),
            pltpu.SemaphoreType.DMA((2,)),
        ],
        compiler_params=pltpu.CompilerParams(vmem_limit_bytes=16 << 20),
        cost_estimate=pl.CostEstimate(
            flops=4 * 10**10, transcendentals=10**8, bytes_accessed=100 * 10**6
        ),
        name="attention",
    )(jnp.stack([lens[request], jnp.int32(request)]), in_hbm(qt), in_hbm(kv))


def out_kernel(
    src_ref, request_ref, gain_ref, rows_hbm, pair_0, near_0, far_0, pair_1, near_1, far_1, a_same,
    a_others, residual_hbm, normed_hbm, att_ref, w_ref, sum_ref, rows_ref, normed_ref, row_sem, out_sems, w_sems,
):
    cols = near_0.shape[1]
    sources = [
        (pair.at[:, pl.ds(0, cols)], near, pair.at[:, pl.ds(cols, cols)], far)
        for pair, near, far in ((pair_0, near_0, far_0), (pair_1, near_1, far_1))
    ]

    def w_load(side, i, source=near_0):
        return pltpu.make_async_copy(source, w_ref.at[side, i], w_sems.at[side, i])

    full_rows = rows_ref.shape[0]
    at = pl.multiple_of(request_ref[0] * full_rows, full_rows)
    load = pltpu.make_async_copy(rows_hbm.at[pl.ds(at, full_rows)], rows_ref, row_sem)
    for i in range(Z):
        w_load(0, i, sources[0][i]).start()
        w_load(1, i, sources[1][i]).start()
    load.start()
    for i in range(Z):
        att_ref[src_ref[i]] = a_same[i]
        att_ref[src_ref[Z + i]] = a_others[i]

    def columns(i, carry):
        attended = jnp.concatenate([att_ref[j] for j in range(2 * Z)], axis=1)
        w_load(0, i).wait()
        w_load(1, i).wait()
        sum_ref[src_ref[i]] = contract(attended, w_ref[0, i])
        sum_ref[src_ref[Z + i]] = contract(attended, w_ref[1, i])
        return carry

    lax.fori_loop(0, Z, columns, 0)
    load.wait()
    total = jnp.concatenate([sum_ref[i] for i in range(2 * Z)], axis=1)
    rows_ref[...] = (rows_ref[...].astype(jnp.float32) + total).astype(jnp.bfloat16)
    keep = pltpu.make_async_copy(rows_ref, residual_hbm, out_sems.at[0])
    keep.start()
    normed_ref[...] = mean_norm(rows_ref[...], gain_ref[...])
    give = pltpu.make_async_copy(normed_ref, normed_hbm, out_sems.at[1])
    give.start()
    keep.wait()
    give.wait()


def project_out(src, gain, weights, rows, pieces, request):
    piece_rows, piece_width = pieces[0].shape[1:]
    width = rows.shape[1]
    cols = weights[1].shape[1]
    scalar = pl.BlockSpec(memory_space=pltpu.SMEM)
    whole = pl.BlockSpec(memory_space=pltpu.VMEM)
    remote = pl.BlockSpec(memory_space=pltpu.HBM)
    return pl.pallas_call(
        out_kernel,
        out_shape=(pltpu.HBM((piece_rows, width), jnp.bfloat16),) * 2,
        in_specs=[scalar, scalar, whole] + [remote] * 7 + [whole] * 2,
        out_specs=(pl.BlockSpec(memory_space=pltpu.HBM),) * 2,
        scratch_shapes=[
            pltpu.VMEM((2 * Z, piece_rows, piece_width), jnp.bfloat16),
            pltpu.VMEM((2, Z, width, cols), jnp.bfloat16),
            pltpu.VMEM((2 * Z, piece_rows, cols), jnp.float32),
            pltpu.VMEM((piece_rows, width), jnp.bfloat16),
            pltpu.VMEM((piece_rows, width), jnp.bfloat16),
            pltpu.SemaphoreType.DMA,
            pltpu.SemaphoreType.DMA((2,)),
            pltpu.SemaphoreType.DMA((2, Z)),
        ],
        compiler_params=pltpu.CompilerParams(vmem_limit_bytes=27 << 20),
        cost_estimate=pl.CostEstimate(
            flops=4 * 10**9, transcendentals=0, bytes_accessed=16 * 10**6
        ),
        name="project_out",
    )(src, jnp.full((1,), request, jnp.int32), gain, in_hbm(rows), *map(in_hbm, weights), *pieces)


def ff_kernel(
    place_ref, low_hbm, high_hbm, w_ref, mine_ref, theirs_ref, x_ref, hidden_ref, x_sems
):
    shards, height, lanes = w_ref.shape
    width = x_ref.shape[3]
    units = hidden_ref.shape[1]
    rows = x_ref.shape[2]
    count = low_hbm.shape[0]
    row_at = pl.multiple_of(place_ref[1] * rows, rows)
    x_loads = []
    for i in range(2 * count):
        side = lax.rem(place_ref[0] + i % 2, 2)
        x_loads.append(
            pltpu.make_async_copy(
                (low_hbm, high_hbm)[i // count].at[i % count, pl.ds(row_at, rows)],
                x_ref.at[side, i // 2],
                x_sems.at[i],
            )
        )
    for copy in x_loads:
        copy.start()
    for copy in x_loads:
        copy.wait()
    x = x_ref[...].reshape(2 * Z * rows, width)
    for i in range(0, units, FF_PAIR):
        size = min(FF_PAIR, units - i)
        both = lax.dot_general(
            x,
            jnp.concatenate(
                [
                    jnp.concatenate([w_ref[j, at : at + size] for j in range(shards)], axis=1)
                    for at in (i, units + i)
                ],
                axis=0,
            ),
            (((1,), (1,)), ((), ())),
            preferred_element_type=jnp.float32,
        )
        hidden_ref[:, i : i + size] = (jax.nn.silu(both[:, :size]) * both[:, size:]).astype(
            jnp.bfloat16
        )
    hidden = hidden_ref[...]
    for i in range(0, shards, 2):
        down = jnp.concatenate([w_ref[i, 2 * units :], w_ref[i + 1, 2 * units :]], axis=1)
        terms = contract(hidden, down).astype(jnp.bfloat16).reshape(2, Z, rows, 2 * lanes)
        mine_ref[:, :, i * lanes : (i + 2) * lanes] = terms[0]
        theirs_ref[:, :, i * lanes : (i + 2) * lanes] = terms[1]


def feed_forward(place, low, high, weights, units):
    count, group_rows, width = low.shape
    rows = group_rows // 2
    whole = pl.BlockSpec(memory_space=pltpu.VMEM)
    remote = pl.BlockSpec(memory_space=pl.ANY)
    return pl.pallas_call(
        ff_kernel,
        out_shape=(jax.ShapeDtypeStruct((Z, rows, width), jnp.bfloat16),) * 2,
        in_specs=[pl.BlockSpec(memory_space=pltpu.SMEM), remote, remote, whole],
        out_specs=(whole, whole),
        scratch_shapes=[
            pltpu.VMEM((2, Z, rows, width), jnp.bfloat16),
            pltpu.VMEM((2 * count * rows, units), jnp.bfloat16),
            pltpu.SemaphoreType.DMA((2 * count,)),
        ],
        compiler_params=pltpu.CompilerParams(vmem_limit_bytes=12 << 20),
        cost_estimate=pl.CostEstimate(
            flops=5 * 10**9, transcendentals=10**6, bytes_accessed=16 * 10**6
        ),
        name="feed_forward",
    )(place, in_hbm(low), in_hbm(high), weights)


def angles_of(cached_len):
    half = HEAD_DIM // 2
    frequency = ROPE_BASE ** (-jnp.arange(half).astype(jnp.float32) * 2.0 / HEAD_DIM)
    positions = (cached_len[:, None] + jnp.arange(S_NEW)[None, :]).reshape(-1)
    angles = frequency[:, None] * positions.astype(jnp.float32)[None, :]
    return jnp.cos(angles), jnp.sin(angles)


def per_device(
    hidden_in, attn_gain, w_qkv, w_out, mlp_gain, w_gate, w_up, w_down, cache_kv, cached_len
):
    head_count = lax.axis_size("head")
    head_index = lax.axis_index("head")
    q_width = HEADS * HEAD_DIM
    kv_width = KV_HEADS * HEAD_DIM
    q_dev = q_width // head_count
    split_count = head_count // KV_HEADS
    part_index = head_index % split_count
    kv_head = head_index // split_count
    units = w_gate.shape[1]
    half_z = Z // 2
    row_count, width = hidden_in.shape

    src = sources()
    own = cache_kv[:, 0]
    other = exchange(own)
    columns = jnp.concatenate(
        [
            lax.dynamic_slice_in_dim(w_qkv, head_index * q_dev, q_dev, 1),
            lax.dynamic_slice_in_dim(w_qkv, q_width + kv_head * HEAD_DIM, HEAD_DIM, 1),
            lax.dynamic_slice_in_dim(w_qkv, q_width + kv_width + kv_head * HEAD_DIM, HEAD_DIM, 1),
        ],
        axis=1,
    )
    spread = jnp.broadcast_to(columns[None], (lax.axis_size("tok"), *columns.shape))
    spread, x_own = lax.optimization_barrier((spread, hidden_in))
    group_w = lax.all_to_all(spread, "tok", 0, 0, tiled=True).reshape(width, columns.shape[1])
    x_same = [x_own] + [along_z(x_own, d) for d in range(1, Z)]
    out_cols = width // head_count
    out_pair = lax.all_gather(
        jnp.concatenate(
            [
                lax.dynamic_slice_in_dim(w_out, block * out_cols, out_cols, 1)
                for block in (head_index, (head_index + half_z * 2) % head_count)
            ],
            axis=1,
        ),
        "tok", axis=0, tiled=True,
    )
    x_others = exchange(jnp.stack(x_same))
    ff_part, group_w, other, *_ = lax.optimization_barrier(
        (jnp.concatenate([w_gate.T, w_up.T, w_down], axis=0), group_w, other, *x_same)
    )
    ff_weights = lax.all_gather(ff_part, "tok", axis=0)
    cosine, sine = angles_of(cached_len)
    qt, kv, cache_new, rows = prepare(
        cached_len, part_index.reshape(1), src, attn_gain[None], cosine, sine, group_w,
        x_same, x_others, own, other,
    )
    out_pair, qt = lax.optimization_barrier((out_pair, qt))
    att_0 = attention(cached_len, 0, qt, kv)
    pair_other = exchange(out_pair)
    out_part = out_pair[:, :out_cols]
    out_far = [along_z(out_part, 1), along_z(out_part, Z - 1)]
    att_0, qt, pair_other, *out_far = lax.optimization_barrier((att_0, qt, pair_other, *out_far))
    out_pieces = (out_pair, *out_far, pair_other, *[exchange(piece) for piece in out_far])
    far_0 = [along_z(att_0, d) for d in range(1, Z)]
    att_1 = attention(cached_len, 1, qt, kv)
    att_1, att_0, *far_0 = lax.optimization_barrier((att_1, att_0, *far_0))
    same_0 = jnp.stack([att_0] + far_0)
    pieces_0 = (same_0, exchange(same_0))
    far_1 = [along_z(att_1, d) for d in range(1, Z)]
    gain = mlp_gain[None]
    residual_0, normed_0 = project_out(src, gain, out_pieces, rows, pieces_0, 0)
    att_1, residual_0, ff_weights, *far_1 = lax.optimization_barrier(
        (att_1, residual_0, ff_weights, *far_1)
    )
    same_1 = jnp.stack([att_1] + far_1)
    pieces_1 = (same_1, exchange(same_1))
    residual_1, normed_1 = project_out(src, gain, out_pieces, rows, pieces_1, 1)
    half_count = head_count // 2
    low = normed_0.reshape(half_count, row_count, width)
    high = normed_1.reshape(half_count, row_count, width)
    z = head_index // 2
    core = head_index % 2
    own_0 = lax.dynamic_index_in_dim(
        residual_0.reshape(half_count, row_count, width), head_index % half_count, 0, keepdims=False
    )
    own_1 = lax.dynamic_index_in_dim(
        residual_1.reshape(half_count, row_count, width), head_index % half_count, 0, keepdims=False
    )
    residual = jnp.where(head_index < half_count, own_0, own_1)
    outs = []
    for chunk in range(2):
        place = jnp.stack([core, jnp.int32(chunk)]).astype(jnp.int32)
        mine, theirs = feed_forward(place, low, high, ff_weights, units)
        pair = (mine.astype(jnp.float32) + exchange(theirs).astype(jnp.float32)).astype(
            jnp.bfloat16
        )
        rows_here = row_count // 2
        total = residual[chunk * rows_here : (chunk + 1) * rows_here].astype(jnp.float32)
        total = total + lax.dynamic_index_in_dim(pair, z, 0, keepdims=False).astype(jnp.float32)
        for d in range(1, Z):
            sent = lax.dynamic_index_in_dim(pair, (z + d) % Z, 0, keepdims=False)
            total = total + along_z(sent, d).astype(jnp.float32)
        outs.append(total.astype(jnp.bfloat16))
    return (jnp.concatenate(outs), cache_new[:, None])


def solution(mesh):
    return jax.shard_map(
        per_device,
        mesh=mesh,
        in_specs=(
            P(("tok", "head"), None),
            P(),
            P("tok", None),
            P("tok", None),
            P(),
            P("tok", "head"),
            P("tok", "head"),
            P("head", "tok"),
            P("tok", "head", None, None),
            P("tok"),
        ),
        out_specs=(P(("tok", "head"), None), P("tok", "head", None, None)),
        check_vma=False,
    )
```

```python
import jax
import jax.numpy as jnp
from jax import lax
from jax.experimental import pallas as pl
from jax.experimental.pallas import tpu as pltpu
from jax.sharding import PartitionSpec as P

HEADS = 32
KV_HEADS = 4
HEAD_DIM = 64
S_NEW = 512
ROPE_BASE = 10000.0

KEYS = 512
ALIGN = 16
WINDOW = S_NEW + ALIGN
LOG2_E = 1.4426950408889634
VROWS = HEAD_DIM + 16


Z = 4
FF_PAIR = 128


def mean_norm(values, gain):
    widened = values.astype(jnp.float32)
    spread = jnp.mean(widened * widened, axis=-1, keepdims=True)
    return (widened * lax.rsqrt(spread + 1e-05) * gain).astype(jnp.bfloat16)


def contract(left_rows, right_rows):
    return jnp.dot(left_rows, right_rows, preferred_element_type=jnp.float32)


def in_hbm(array):
    return pltpu.with_memory_space_constraint(array, pltpu.HBM)


def exchange(array):
    return lax.ppermute(array, "head", [(i, i ^ 1) for i in range(lax.axis_size("head"))])


def along_z(array, distance):
    count = lax.axis_size("head")
    return lax.ppermute(array, "head", [(i, (i + 2 * distance) % count) for i in range(count)])


def gather_head(array):
    same_core = jnp.stack([array] + [along_z(array, d) for d in range(1, Z)])
    return same_core, exchange(same_core)


def sources():
    head_index = lax.axis_index("head")
    z, core = head_index // 2, head_index % 2
    chips = (z - jnp.arange(Z)) % Z * 2
    return jnp.concatenate([chips + core, chips + 1 - core]).astype(jnp.int32)


def attend(length, kv_ref, qt_ref, acc_ref, top_ref, out_ref):
    lanes = kv_ref.shape[1]
    acc_ref[...] = jnp.zeros(acc_ref.shape, jnp.float32)
    top_ref[...] = jnp.full(top_ref.shape, -1e30, jnp.float32)

    def step(index, masked, here):
        at = pl.multiple_of(index * KEYS, KEYS)
        block = kv_ref[pl.ds(at, KEYS)].astype(jnp.float32)
        on_key = lax.broadcasted_iota(jnp.int32, (KEYS, lanes), 1) < HEAD_DIM
        values = jnp.where(on_key, 1.0, block).T[HEAD_DIM - 16 :].astype(jnp.bfloat16)
        keys = jnp.where(on_key, block, pltpu.roll(block, HEAD_DIM, 1)).astype(jnp.bfloat16)
        scores = contract(keys, qt_ref[:, here])
        if masked:
            key = lax.broadcasted_iota(jnp.int32, scores.shape, 0) + (index * KEYS - length)
            query = lax.broadcasted_iota(jnp.int32, scores.shape, 1)
            scores = jnp.where(key <= query, scores, -jnp.inf)
        old_top = top_ref[:, here]
        top = jnp.maximum(jnp.max(scores, axis=0, keepdims=True), old_top)
        exps = jnp.exp2(scores - top).astype(jnp.bfloat16)
        acc_ref[:, here] = contract(values, exps) + acc_ref[:, here] * jnp.exp2(old_top - top)
        top_ref[:, here] = top

    def last(index, carry):
        def one_head(h, inner):
            step(index, True, pl.ds(pl.multiple_of(h * S_NEW, S_NEW), S_NEW))
            return inner

        return lax.fori_loop(0, qt_ref.shape[1] // S_NEW, one_head, carry)

    def full(index, carry):
        step(index, False, slice(None))
        return carry

    tail = length // KEYS
    lax.fori_loop(tail, (length + S_NEW + KEYS - 1) // KEYS, last, 0)
    lax.fori_loop(0, tail, full, 0)
    for pair in range(qt_ref.shape[1] // (2 * S_NEW)):
        sides = []
        for h in (2 * pair, 2 * pair + 1):
            here = slice(h * S_NEW, (h + 1) * S_NEW)
            sides.append(acc_ref[16:, here] / acc_ref[:1, here])
        out_ref[:, pair * lanes : (pair + 1) * lanes] = (
            jnp.concatenate(sides, axis=0).T.astype(jnp.bfloat16)
        )


def prepare_kernel(
    lens_ref, part_ref, src_ref, gain_ref, cos_ref, sin_ref, w_ref, x_0, x_1, x_2, x_3, x_4, x_5, x_6, x_7,
    own_hbm, other_hbm, qt_hbm, kv_hbm, cache_hbm, rows_hbm, x_ref, kv_ref, new_ref, qt_ref, x_sems, load_sems, store_sems,
):
    req_count, block_pos, lanes = own_hbm.shape
    heads_dev = qt_ref.shape[2] // S_NEW
    half = HEAD_DIM // 2
    x_pieces = [x_0, x_1, x_2, x_3, x_4, x_5, x_6, x_7]
    piece_rows = x_0.shape[0]
    own_at = pl.multiple_of(part_ref[0] * block_pos, ALIGN)
    other_at = pl.multiple_of((1 - part_ref[0]) * block_pos, ALIGN)

    def x_load(i):
        at = pl.multiple_of(src_ref[i] * piece_rows, piece_rows)
        return pltpu.make_async_copy(x_pieces[i], x_ref.at[pl.ds(at, piece_rows)], x_sems.at[i])

    def loads(r):
        return (
            pltpu.make_async_copy(
                own_hbm.at[r], kv_ref.at[r, pl.ds(own_at, block_pos)], load_sems.at[r, 0]
            ),
            pltpu.make_async_copy(
                other_hbm.at[r], kv_ref.at[r, pl.ds(other_at, block_pos)], load_sems.at[r, 1]
            ),
        )

    def stores(r):
        return (
            pltpu.make_async_copy(
                kv_ref.at[r, pl.ds(own_at, block_pos)], cache_hbm.at[r], store_sems.at[r, 0]
            ),
            pltpu.make_async_copy(kv_ref.at[r], kv_hbm.at[r], store_sems.at[r, 1]),
            pltpu.make_async_copy(qt_ref.at[r], qt_hbm.at[r], store_sems.at[r, 2]),
        )

    for i in range(2 * Z):
        x_load(i).start()
    for r in range(req_count):
        for copy in loads(r):
            copy.start()
    for i in range(2 * Z):
        x_load(i).wait()
    keep = pltpu.make_async_copy(x_ref, rows_hbm, store_sems.at[req_count, 0])
    keep.start()

    q_lanes = heads_dev * HEAD_DIM
    gain = gain_ref[...]
    def project(r, carry):
        here = pl.ds(pl.multiple_of(r * S_NEW, S_NEW), S_NEW)
        cosine = cos_ref[:, here]
        sine = sin_ref[:, here]

        def turn(block, scale):
            first = block[:half]
            second = block[half:]
            return jnp.concatenate(
                [
                    (first * cosine - second * sine) * scale,
                    (second * cosine + first * sine) * scale,
                ],
                axis=0,
            )

        normed = mean_norm(x_ref[here], gain)
        projected = contract(normed, w_ref[...])
        for pair in range(heads_dev // 2):
            flipped = projected[:, pair * lanes : (pair + 1) * lanes].T
            for one in range(2):
                rows = turn(flipped[one * HEAD_DIM : (one + 1) * HEAD_DIM], HEAD_DIM**-0.5)
                rows = rows.astype(jnp.bfloat16).astype(jnp.float32) * LOG2_E
                upper = rows.astype(jnp.bfloat16)
                lower = (rows - upper.astype(jnp.float32)).astype(jnp.bfloat16)
                at = (2 * pair + one) * S_NEW
                qt_ref[r, :HEAD_DIM, at : at + S_NEW] = upper
                qt_ref[r, HEAD_DIM:, at : at + S_NEW] = lower
        flipped = projected[:, q_lanes:].T
        fresh = jnp.concatenate([turn(flipped[:HEAD_DIM], 1.0), flipped[HEAD_DIM:]], axis=0)
        new_ref[r] = fresh.T.astype(jnp.bfloat16)

        length = lens_ref[r]
        for copy in loads(r):
            copy.wait()
        shift = length % ALIGN
        window_at = pl.multiple_of(length - shift, ALIGN)
        row = lax.broadcasted_iota(jnp.int32, (WINDOW, S_NEW), 0)
        col = lax.broadcasted_iota(jnp.int32, (WINDOW, S_NEW), 1)
        pick = (row - shift == col).astype(jnp.float32).astype(jnp.bfloat16)
        moved = contract(pick, new_ref[r])
        row = lax.broadcasted_iota(jnp.int32, (WINDOW, lanes), 0)
        inside = (row >= shift) & (row < shift + S_NEW)
        old = kv_ref[r, pl.ds(window_at, WINDOW)].astype(jnp.float32)
        kv_ref[r, pl.ds(window_at, WINDOW)] = jnp.where(inside, moved, old).astype(jnp.bfloat16)
        for copy in stores(r):
            copy.start()
        return carry

    lax.fori_loop(0, req_count, project, 0)
    for r in range(req_count):
        for copy in stores(r):
            copy.wait()
    keep.wait()


def prepare(lens, part, src, gain, cosine, sine, w, x_same, x_others, own, other):
    req_count, block_pos, lanes = own.shape
    piece_rows, width = x_same[0].shape
    rows = piece_rows * 2 * Z
    heads_dev = (w.shape[1] - lanes) // HEAD_DIM
    positions = 2 * block_pos + ALIGN
    whole = pl.BlockSpec(memory_space=pltpu.VMEM)
    scalar = pl.BlockSpec(memory_space=pltpu.SMEM)
    remote = pl.BlockSpec(memory_space=pl.ANY)
    return pl.pallas_call(
        prepare_kernel,
        out_shape=(
            pltpu.HBM((req_count, lanes, heads_dev * S_NEW), jnp.bfloat16),
            pltpu.HBM((req_count, positions, lanes), jnp.bfloat16),
            pltpu.HBM(own.shape, jnp.bfloat16),
            pltpu.HBM((rows, width), jnp.bfloat16),
        ),
        in_specs=[scalar] * 3 + [whole] * 4 + [remote] * (2 * Z + 2),
        out_specs=(pl.BlockSpec(memory_space=pltpu.HBM),) * 4,
        scratch_shapes=[
            pltpu.VMEM((rows, width), jnp.bfloat16),
            pltpu.VMEM((req_count, positions, lanes), jnp.bfloat16),
            pltpu.VMEM((req_count, S_NEW, lanes), jnp.bfloat16),
            pltpu.VMEM((req_count, lanes, heads_dev * S_NEW), jnp.bfloat16),
            pltpu.SemaphoreType.DMA((2 * Z,)),
            pltpu.SemaphoreType.DMA((req_count, 2)),
            pltpu.SemaphoreType.DMA((req_count + 1, 3)),
        ],
        compiler_params=pltpu.CompilerParams(vmem_limit_bytes=22 << 20),
        cost_estimate=pl.CostEstimate(
            flops=4 * 10**9, transcendentals=10**6, bytes_accessed=20 * 10**6
        ),
        name="prepare",
    )(lens, part, src, gain, cosine, sine, w, *x_same, *x_others, in_hbm(own), other)


def attention_kernel(which_ref, qt_hbm, kv_hbm, out_ref, qt_ref, kv_ref, acc_ref, top_ref, sems):
    loads = (
        pltpu.make_async_copy(qt_hbm.at[which_ref[1]], qt_ref, sems.at[0]),
        pltpu.make_async_copy(kv_hbm.at[which_ref[1]], kv_ref, sems.at[1]),
    )
    for copy in loads:
        copy.start()
    for copy in loads:
        copy.wait()
    attend(which_ref[0], kv_ref, qt_ref, acc_ref, top_ref, out_ref)


def attention(lens, request, qt, kv):
    columns = qt.shape[2]
    remote = pl.BlockSpec(memory_space=pltpu.HBM)
    return pl.pallas_call(
        attention_kernel,
        out_shape=jax.ShapeDtypeStruct((S_NEW, columns // S_NEW * HEAD_DIM), jnp.bfloat16),
        in_specs=[pl.BlockSpec(memory_space=pltpu.SMEM), remote, remote],
        out_specs=pl.BlockSpec(memory_space=pltpu.VMEM),
        scratch_shapes=[
            pltpu.VMEM(qt.shape[1:], jnp.bfloat16),
            pltpu.VMEM(kv.shape[1:], jnp.bfloat16),
            pltpu.VMEM((VROWS, columns), jnp.float32),
            pltpu.VMEM((1, columns), jnp.float32),
            pltpu.SemaphoreType.DMA((2,)),
        ],
        compiler_params=pltpu.CompilerParams(vmem_limit_bytes=16 << 20),
        cost_estimate=pl.CostEstimate(
            flops=4 * 10**10, transcendentals=10**8, bytes_accessed=100 * 10**6
        ),
        name="attention",
    )(jnp.stack([lens[request], jnp.int32(request)]), in_hbm(qt), in_hbm(kv))


def out_kernel(
    src_ref, request_ref, gain_ref, rows_hbm, pair_0, near_0, far_0, pair_1, near_1, far_1, a_same,
    a_others, residual_hbm, normed_hbm, att_ref, w_ref, sum_ref, rows_ref, normed_ref, row_sem, out_sems, w_sems,
):
    cols = near_0.shape[1]
    sources = [
        (pair.at[:, pl.ds(0, cols)], near, pair.at[:, pl.ds(cols, cols)], far)
        for pair, near, far in ((pair_0, near_0, far_0), (pair_1, near_1, far_1))
    ]

    def w_load(side, i, source=near_0):
        return pltpu.make_async_copy(source, w_ref.at[side, i], w_sems.at[side, i])

    full_rows = rows_ref.shape[0]
    at = pl.multiple_of(request_ref[0] * full_rows, full_rows)
    load = pltpu.make_async_copy(rows_hbm.at[pl.ds(at, full_rows)], rows_ref, row_sem)
    for i in range(Z):
        w_load(0, i, sources[0][i]).start()
        w_load(1, i, sources[1][i]).start()
    load.start()
    for i in range(Z):
        att_ref[src_ref[i]] = a_same[i]
        att_ref[src_ref[Z + i]] = a_others[i]

    def columns(i, carry):
        attended = jnp.concatenate([att_ref[j] for j in range(2 * Z)], axis=1)
        w_load(0, i).wait()
        w_load(1, i).wait()
        sum_ref[src_ref[i]] = contract(attended, w_ref[0, i])
        sum_ref[src_ref[Z + i]] = contract(attended, w_ref[1, i])
        return carry

    lax.fori_loop(0, Z, columns, 0)
    load.wait()
    total = jnp.concatenate([sum_ref[i] for i in range(2 * Z)], axis=1)
    rows_ref[...] = (rows_ref[...].astype(jnp.float32) + total).astype(jnp.bfloat16)
    keep = pltpu.make_async_copy(rows_ref, residual_hbm, out_sems.at[0])
    keep.start()
    normed_ref[...] = mean_norm(rows_ref[...], gain_ref[...])
    give = pltpu.make_async_copy(normed_ref, normed_hbm, out_sems.at[1])
    give.start()
    keep.wait()
    give.wait()


def project_out(src, gain, weights, rows, pieces, request):
    piece_rows, piece_width = pieces[0].shape[1:]
    width = rows.shape[1]
    cols = weights[1].shape[1]
    scalar = pl.BlockSpec(memory_space=pltpu.SMEM)
    whole = pl.BlockSpec(memory_space=pltpu.VMEM)
    remote = pl.BlockSpec(memory_space=pltpu.HBM)
    return pl.pallas_call(
        out_kernel,
        out_shape=(pltpu.HBM((piece_rows, width), jnp.bfloat16),) * 2,
        in_specs=[scalar, scalar, whole] + [remote] * 7 + [whole] * 2,
        out_specs=(pl.BlockSpec(memory_space=pltpu.HBM),) * 2,
        scratch_shapes=[
            pltpu.VMEM((2 * Z, piece_rows, piece_width), jnp.bfloat16),
            pltpu.VMEM((2, Z, width, cols), jnp.bfloat16),
            pltpu.VMEM((2 * Z, piece_rows, cols), jnp.float32),
            pltpu.VMEM((piece_rows, width), jnp.bfloat16),
            pltpu.VMEM((piece_rows, width), jnp.bfloat16),
            pltpu.SemaphoreType.DMA,
            pltpu.SemaphoreType.DMA((2,)),
            pltpu.SemaphoreType.DMA((2, Z)),
        ],
        compiler_params=pltpu.CompilerParams(vmem_limit_bytes=27 << 20),
        cost_estimate=pl.CostEstimate(
            flops=4 * 10**9, transcendentals=0, bytes_accessed=16 * 10**6
        ),
        name="project_out",
    )(src, jnp.full((1,), request, jnp.int32), gain, in_hbm(rows), *map(in_hbm, weights), *pieces)


def ff_kernel(
    place_ref, low_hbm, high_hbm, w_ref, mine_ref, theirs_ref, x_ref, hidden_ref, x_sems
):
    shards, height, lanes = w_ref.shape
    width = x_ref.shape[3]
    units = hidden_ref.shape[1]
    rows = x_ref.shape[2]
    count = low_hbm.shape[0]
    row_at = pl.multiple_of(place_ref[1] * rows, rows)
    x_loads = []
    for i in range(2 * count):
        side = lax.rem(place_ref[0] + i % 2, 2)
        x_loads.append(
            pltpu.make_async_copy(
                (low_hbm, high_hbm)[i // count].at[i % count, pl.ds(row_at, rows)],
                x_ref.at[side, i // 2],
                x_sems.at[i],
            )
        )
    for copy in x_loads:
        copy.start()
    for copy in x_loads:
        copy.wait()
    x = x_ref[...].reshape(2 * Z * rows, width)
    for i in range(0, units, FF_PAIR):
        size = min(FF_PAIR, units - i)
        both = lax.dot_general(
            x,
            jnp.concatenate(
                [
                    jnp.concatenate([w_ref[j, at : at + size] for j in range(shards)], axis=1)
                    for at in (i, units + i)
                ],
                axis=0,
            ),
            (((1,), (1,)), ((), ())),
            preferred_element_type=jnp.float32,
        )
        hidden_ref[:, i : i + size] = (jax.nn.silu(both[:, :size]) * both[:, size:]).astype(
            jnp.bfloat16
        )
    hidden = hidden_ref[...]
    for i in range(0, shards, 2):
        down = jnp.concatenate([w_ref[i, 2 * units :], w_ref[i + 1, 2 * units :]], axis=1)
        terms = contract(hidden, down).astype(jnp.bfloat16).reshape(2, Z, rows, 2 * lanes)
        mine_ref[:, :, i * lanes : (i + 2) * lanes] = terms[0]
        theirs_ref[:, :, i * lanes : (i + 2) * lanes] = terms[1]


def feed_forward(place, low, high, weights, units):
    count, group_rows, width = low.shape
    rows = group_rows // 2
    whole = pl.BlockSpec(memory_space=pltpu.VMEM)
    remote = pl.BlockSpec(memory_space=pl.ANY)
    return pl.pallas_call(
        ff_kernel,
        out_shape=(jax.ShapeDtypeStruct((Z, rows, width), jnp.bfloat16),) * 2,
        in_specs=[pl.BlockSpec(memory_space=pltpu.SMEM), remote, remote, whole],
        out_specs=(whole, whole),
        scratch_shapes=[
            pltpu.VMEM((2, Z, rows, width), jnp.bfloat16),
            pltpu.VMEM((2 * count * rows, units), jnp.bfloat16),
            pltpu.SemaphoreType.DMA((2 * count,)),
        ],
        compiler_params=pltpu.CompilerParams(vmem_limit_bytes=12 << 20),
        cost_estimate=pl.CostEstimate(
            flops=5 * 10**9, transcendentals=10**6, bytes_accessed=16 * 10**6
        ),
        name="feed_forward",
    )(place, in_hbm(low), in_hbm(high), weights)


def angles_of(cached_len):
    half = HEAD_DIM // 2
    frequency = ROPE_BASE ** (-jnp.arange(half).astype(jnp.float32) * 2.0 / HEAD_DIM)
    positions = (cached_len[:, None] + jnp.arange(S_NEW)[None, :]).reshape(-1)
    angles = frequency[:, None] * positions.astype(jnp.float32)[None, :]
    return jnp.cos(angles), jnp.sin(angles)


def per_device(
    hidden_in, attn_gain, w_qkv, w_out, mlp_gain, w_gate, w_up, w_down, cache_kv, cached_len
):
    head_count = lax.axis_size("head")
    head_index = lax.axis_index("head")
    q_width = HEADS * HEAD_DIM
    kv_width = KV_HEADS * HEAD_DIM
    q_dev = q_width // head_count
    split_count = head_count // KV_HEADS
    part_index = head_index % split_count
    kv_head = head_index // split_count
    units = w_gate.shape[1]
    half_z = Z // 2
    row_count, width = hidden_in.shape

    src = sources()
    own = cache_kv[:, 0]
    other = exchange(own)
    columns = jnp.concatenate(
        [
            lax.dynamic_slice_in_dim(w_qkv, head_index * q_dev, q_dev, 1),
            lax.dynamic_slice_in_dim(w_qkv, q_width + kv_head * HEAD_DIM, HEAD_DIM, 1),
            lax.dynamic_slice_in_dim(w_qkv, q_width + kv_width + kv_head * HEAD_DIM, HEAD_DIM, 1),
        ],
        axis=1,
    )
    spread = jnp.broadcast_to(columns[None], (lax.axis_size("tok"), *columns.shape))
    spread, x_own = lax.optimization_barrier((spread, hidden_in))
    group_w = lax.all_to_all(spread, "tok", 0, 0, tiled=True).reshape(width, columns.shape[1])
    x_same = [x_own] + [along_z(x_own, d) for d in range(1, Z)]
    out_cols = width // head_count
    out_pair = lax.all_gather(
        jnp.concatenate(
            [
                lax.dynamic_slice_in_dim(w_out, block * out_cols, out_cols, 1)
                for block in (head_index, (head_index + half_z * 2) % head_count)
            ],
            axis=1,
        ),
        "tok", axis=0, tiled=True,
    )
    x_others = [exchange(x_same[d]) if d != half_z else None for d in range(Z)]
    early = [x_others[d] for d in range(Z) if d != half_z]
    ff_part, group_w, other, x_same[half_z], *early = lax.optimization_barrier(
        (
            jnp.concatenate([w_gate.T, w_up.T, w_down], axis=0),
            group_w, other, x_same[half_z], *early,
        )
    )
    x_others = early[:half_z] + [exchange(x_same[half_z])] + early[half_z:]
    ff_weights = lax.all_gather(ff_part, "tok", axis=0)
    cosine, sine = angles_of(cached_len)
    qt, kv, cache_new, rows = prepare(
        cached_len, part_index.reshape(1), src, attn_gain[None], cosine, sine, group_w,
        x_same, x_others, own, other,
    )
    out_pair, qt = lax.optimization_barrier((out_pair, qt))
    att_0 = attention(cached_len, 0, qt, kv)
    pair_other = exchange(out_pair)
    out_part = out_pair[:, :out_cols]
    out_far = [along_z(out_part, 1), along_z(out_part, Z - 1)]
    att_0, qt, pair_other, *out_far = lax.optimization_barrier((att_0, qt, pair_other, *out_far))
    out_pieces = (out_pair, *out_far, pair_other, *[exchange(piece) for piece in out_far])
    far_0 = [along_z(att_0, d) for d in range(1, Z)]
    att_1 = attention(cached_len, 1, qt, kv)
    att_1, att_0, *far_0 = lax.optimization_barrier((att_1, att_0, *far_0))
    same_0 = jnp.stack([att_0] + far_0)
    pieces_0 = (same_0, exchange(same_0))
    far_1 = [along_z(att_1, d) for d in range(1, Z)]
    gain = mlp_gain[None]
    residual_0, normed_0 = project_out(src, gain, out_pieces, rows, pieces_0, 0)
    att_1, residual_0, ff_weights, *far_1 = lax.optimization_barrier(
        (att_1, residual_0, ff_weights, *far_1)
    )
    same_1 = jnp.stack([att_1] + far_1)
    pieces_1 = (same_1, exchange(same_1))
    residual_1, normed_1 = project_out(src, gain, out_pieces, rows, pieces_1, 1)
    half_count = head_count // 2
    low = normed_0.reshape(half_count, row_count, width)
    high = normed_1.reshape(half_count, row_count, width)
    z = head_index // 2
    core = head_index % 2
    own_0 = lax.dynamic_index_in_dim(
        residual_0.reshape(half_count, row_count, width), head_index % half_count, 0, keepdims=False
    )
    own_1 = lax.dynamic_index_in_dim(
        residual_1.reshape(half_count, row_count, width), head_index % half_count, 0, keepdims=False
    )
    residual = jnp.where(head_index < half_count, own_0, own_1)
    outs = []
    for chunk in range(2):
        place = jnp.stack([core, jnp.int32(chunk)]).astype(jnp.int32)
        mine, theirs = feed_forward(place, low, high, ff_weights, units)
        pair = (mine.astype(jnp.float32) + exchange(theirs).astype(jnp.float32)).astype(
            jnp.bfloat16
        )
        rows_here = row_count // 2
        total = residual[chunk * rows_here : (chunk + 1) * rows_here].astype(jnp.float32)
        total = total + lax.dynamic_index_in_dim(pair, z, 0, keepdims=False).astype(jnp.float32)
        for d in range(1, Z):
            sent = lax.dynamic_index_in_dim(pair, (z + d) % Z, 0, keepdims=False)
            total = total + along_z(sent, d).astype(jnp.float32)
        outs.append(total.astype(jnp.bfloat16))
    return (jnp.concatenate(outs), cache_new[:, None])


def solution(mesh):
    return jax.shard_map(
        per_device,
        mesh=mesh,
        in_specs=(
            P(("tok", "head"), None),
            P(),
            P("tok", None),
            P("tok", None),
            P(),
            P("tok", "head"),
            P("tok", "head"),
            P("head", "tok"),
            P("tok", "head", None, None),
            P("tok"),
        ),
        out_specs=(P(("tok", "head"), None), P("tok", "head", None, None)),
        check_vma=False,
    )
```

```python
import jax
import jax.numpy as jnp
from jax import lax
from jax.experimental import pallas as pl
from jax.experimental.pallas import tpu as pltpu
from jax.sharding import PartitionSpec as P

HEADS = 32
KV_HEADS = 4
HEAD_DIM = 64
S_NEW = 512
ROPE_BASE = 10000.0

KEYS = 512
ALIGN = 16
WINDOW = S_NEW + ALIGN
LOG2_E = 1.4426950408889634
VROWS = HEAD_DIM + 16


Z = 4
FF_PAIR = 128


def mean_norm(values, gain):
    widened = values.astype(jnp.float32)
    spread = jnp.mean(widened * widened, axis=-1, keepdims=True)
    return (widened * lax.rsqrt(spread + 1e-05) * gain).astype(jnp.bfloat16)


def contract(left_rows, right_rows):
    return jnp.dot(left_rows, right_rows, preferred_element_type=jnp.float32)


def in_hbm(array):
    return pltpu.with_memory_space_constraint(array, pltpu.HBM)


def exchange(array):
    return lax.ppermute(array, "head", [(i, i ^ 1) for i in range(lax.axis_size("head"))])


def along_z(array, distance):
    count = lax.axis_size("head")
    return lax.ppermute(array, "head", [(i, (i + 2 * distance) % count) for i in range(count)])


def gather_head(array):
    same_core = jnp.stack([array] + [along_z(array, d) for d in range(1, Z)])
    return same_core, exchange(same_core)


def sources():
    head_index = lax.axis_index("head")
    z, core = head_index // 2, head_index % 2
    chips = (z - jnp.arange(Z)) % Z * 2
    return jnp.concatenate([chips + core, chips + 1 - core]).astype(jnp.int32)


def attend(length, kv_ref, qt_ref, acc_ref, top_ref, out_ref):
    lanes = kv_ref.shape[1]
    acc_ref[...] = jnp.zeros(acc_ref.shape, jnp.float32)
    top_ref[...] = jnp.full(top_ref.shape, -1e30, jnp.float32)

    def step(index, masked, here):
        at = pl.multiple_of(index * KEYS, KEYS)
        block = kv_ref[pl.ds(at, KEYS)].astype(jnp.float32)
        on_key = lax.broadcasted_iota(jnp.int32, (KEYS, lanes), 1) < HEAD_DIM
        values = jnp.where(on_key, 1.0, block).T[HEAD_DIM - 16 :].astype(jnp.bfloat16)
        keys = jnp.where(on_key, block, pltpu.roll(block, HEAD_DIM, 1)).astype(jnp.bfloat16)
        scores = contract(keys, qt_ref[:, here])
        if masked:
            key = lax.broadcasted_iota(jnp.int32, scores.shape, 0) + (index * KEYS - length)
            query = lax.broadcasted_iota(jnp.int32, scores.shape, 1)
            scores = jnp.where(key <= query, scores, -jnp.inf)
        old_top = top_ref[:, here]
        top = jnp.maximum(jnp.max(scores, axis=0, keepdims=True), old_top)
        exps = jnp.exp2(scores - top).astype(jnp.bfloat16)
        acc_ref[:, here] = contract(values, exps) + acc_ref[:, here] * jnp.exp2(old_top - top)
        top_ref[:, here] = top

    def last(index, carry):
        def one_head(h, inner):
            step(index, True, pl.ds(pl.multiple_of(h * S_NEW, S_NEW), S_NEW))
            return inner

        return lax.fori_loop(0, qt_ref.shape[1] // S_NEW, one_head, carry)

    def full(index, carry):
        step(index, False, slice(None))
        return carry

    tail = length // KEYS
    lax.fori_loop(tail, (length + S_NEW + KEYS - 1) // KEYS, last, 0)
    lax.fori_loop(0, tail, full, 0)
    for pair in range(qt_ref.shape[1] // (2 * S_NEW)):
        sides = []
        for h in (2 * pair, 2 * pair + 1):
            here = slice(h * S_NEW, (h + 1) * S_NEW)
            sides.append(acc_ref[16:, here] / acc_ref[:1, here])
        out_ref[:, pair * lanes : (pair + 1) * lanes] = (
            jnp.concatenate(sides, axis=0).T.astype(jnp.bfloat16)
        )


def prepare_kernel(
    lens_ref, part_ref, src_ref, gain_ref, cos_ref, sin_ref, w_ref, x_0, x_1, x_2, x_3, x_others,
    own_hbm, other_hbm, qt_hbm, kv_hbm, cache_hbm, rows_hbm, x_ref, kv_ref, new_ref, qt_ref, x_sems, load_sems, store_sems,
):
    req_count, block_pos, lanes = own_hbm.shape
    heads_dev = qt_ref.shape[2] // S_NEW
    half = HEAD_DIM // 2
    x_pieces = [x_0, x_1, x_2, x_3] + [x_others.at[i] for i in range(Z)]
    piece_rows = x_0.shape[0]
    own_at = pl.multiple_of(part_ref[0] * block_pos, ALIGN)
    other_at = pl.multiple_of((1 - part_ref[0]) * block_pos, ALIGN)

    def x_load(i):
        at = pl.multiple_of(src_ref[i] * piece_rows, piece_rows)
        return pltpu.make_async_copy(x_pieces[i], x_ref.at[pl.ds(at, piece_rows)], x_sems.at[i])

    def loads(r):
        return (
            pltpu.make_async_copy(
                own_hbm.at[r], kv_ref.at[r, pl.ds(own_at, block_pos)], load_sems.at[r, 0]
            ),
            pltpu.make_async_copy(
                other_hbm.at[r], kv_ref.at[r, pl.ds(other_at, block_pos)], load_sems.at[r, 1]
            ),
        )

    def stores(r):
        return (
            pltpu.make_async_copy(
                kv_ref.at[r, pl.ds(own_at, block_pos)], cache_hbm.at[r], store_sems.at[r, 0]
            ),
            pltpu.make_async_copy(kv_ref.at[r], kv_hbm.at[r], store_sems.at[r, 1]),
            pltpu.make_async_copy(qt_ref.at[r], qt_hbm.at[r], store_sems.at[r, 2]),
        )

    for i in range(2 * Z):
        x_load(i).start()
    for r in range(req_count):
        for copy in loads(r):
            copy.start()
    for i in range(2 * Z):
        x_load(i).wait()
    keep = pltpu.make_async_copy(x_ref, rows_hbm, store_sems.at[req_count, 0])
    keep.start()

    q_lanes = heads_dev * HEAD_DIM
    gain = gain_ref[...]
    def project(r, carry):
        here = pl.ds(pl.multiple_of(r * S_NEW, S_NEW), S_NEW)
        cosine = cos_ref[:, here]
        sine = sin_ref[:, here]

        def turn(block, scale):
            first = block[:half]
            second = block[half:]
            return jnp.concatenate(
                [
                    (first * cosine - second * sine) * scale,
                    (second * cosine + first * sine) * scale,
                ],
                axis=0,
            )

        normed = mean_norm(x_ref[here], gain)
        projected = contract(normed, w_ref[...])
        for pair in range(heads_dev // 2):
            flipped = projected[:, pair * lanes : (pair + 1) * lanes].T
            for one in range(2):
                rows = turn(flipped[one * HEAD_DIM : (one + 1) * HEAD_DIM], HEAD_DIM**-0.5)
                rows = rows.astype(jnp.bfloat16).astype(jnp.float32) * LOG2_E
                upper = rows.astype(jnp.bfloat16)
                lower = (rows - upper.astype(jnp.float32)).astype(jnp.bfloat16)
                at = (2 * pair + one) * S_NEW
                qt_ref[r, :HEAD_DIM, at : at + S_NEW] = upper
                qt_ref[r, HEAD_DIM:, at : at + S_NEW] = lower
        flipped = projected[:, q_lanes:].T
        fresh = jnp.concatenate([turn(flipped[:HEAD_DIM], 1.0), flipped[HEAD_DIM:]], axis=0)
        new_ref[r] = fresh.T.astype(jnp.bfloat16)

        length = lens_ref[r]
        for copy in loads(r):
            copy.wait()
        shift = length % ALIGN
        window_at = pl.multiple_of(length - shift, ALIGN)
        row = lax.broadcasted_iota(jnp.int32, (WINDOW, S_NEW), 0)
        col = lax.broadcasted_iota(jnp.int32, (WINDOW, S_NEW), 1)
        pick = (row - shift == col).astype(jnp.float32).astype(jnp.bfloat16)
        moved = contract(pick, new_ref[r])
        row = lax.broadcasted_iota(jnp.int32, (WINDOW, lanes), 0)
        inside = (row >= shift) & (row < shift + S_NEW)
        old = kv_ref[r, pl.ds(window_at, WINDOW)].astype(jnp.float32)
        kv_ref[r, pl.ds(window_at, WINDOW)] = jnp.where(inside, moved, old).astype(jnp.bfloat16)
        for copy in stores(r):
            copy.start()
        return carry

    lax.fori_loop(0, req_count, project, 0)
    for r in range(req_count):
        for copy in stores(r):
            copy.wait()
    keep.wait()


def prepare(lens, part, src, gain, cosine, sine, w, x_same, x_others, own, other):
    req_count, block_pos, lanes = own.shape
    piece_rows, width = x_same[0].shape
    rows = piece_rows * 2 * Z
    heads_dev = (w.shape[1] - lanes) // HEAD_DIM
    positions = 2 * block_pos + ALIGN
    whole = pl.BlockSpec(memory_space=pltpu.VMEM)
    scalar = pl.BlockSpec(memory_space=pltpu.SMEM)
    remote = pl.BlockSpec(memory_space=pl.ANY)
    return pl.pallas_call(
        prepare_kernel,
        out_shape=(
            pltpu.HBM((req_count, lanes, heads_dev * S_NEW), jnp.bfloat16),
            pltpu.HBM((req_count, positions, lanes), jnp.bfloat16),
            pltpu.HBM(own.shape, jnp.bfloat16),
            pltpu.HBM((rows, width), jnp.bfloat16),
        ),
        in_specs=[scalar] * 3 + [whole] * 4 + [remote] * (Z + 3),
        out_specs=(pl.BlockSpec(memory_space=pltpu.HBM),) * 4,
        scratch_shapes=[
            pltpu.VMEM((rows, width), jnp.bfloat16),
            pltpu.VMEM((req_count, positions, lanes), jnp.bfloat16),
            pltpu.VMEM((req_count, S_NEW, lanes), jnp.bfloat16),
            pltpu.VMEM((req_count, lanes, heads_dev * S_NEW), jnp.bfloat16),
            pltpu.SemaphoreType.DMA((2 * Z,)),
            pltpu.SemaphoreType.DMA((req_count, 2)),
            pltpu.SemaphoreType.DMA((req_count + 1, 3)),
        ],
        compiler_params=pltpu.CompilerParams(vmem_limit_bytes=22 << 20),
        cost_estimate=pl.CostEstimate(
            flops=4 * 10**9, transcendentals=10**6, bytes_accessed=20 * 10**6
        ),
        name="prepare",
    )(lens, part, src, gain, cosine, sine, w, *x_same, x_others, in_hbm(own), other)


def attention_kernel(which_ref, qt_hbm, kv_hbm, out_ref, qt_ref, kv_ref, acc_ref, top_ref, sems):
    loads = (
        pltpu.make_async_copy(qt_hbm.at[which_ref[1]], qt_ref, sems.at[0]),
        pltpu.make_async_copy(kv_hbm.at[which_ref[1]], kv_ref, sems.at[1]),
    )
    for copy in loads:
        copy.start()
    for copy in loads:
        copy.wait()
    attend(which_ref[0], kv_ref, qt_ref, acc_ref, top_ref, out_ref)


def attention(lens, request, qt, kv):
    columns = qt.shape[2]
    remote = pl.BlockSpec(memory_space=pltpu.HBM)
    return pl.pallas_call(
        attention_kernel,
        out_shape=jax.ShapeDtypeStruct((S_NEW, columns // S_NEW * HEAD_DIM), jnp.bfloat16),
        in_specs=[pl.BlockSpec(memory_space=pltpu.SMEM), remote, remote],
        out_specs=pl.BlockSpec(memory_space=pltpu.VMEM),
        scratch_shapes=[
            pltpu.VMEM(qt.shape[1:], jnp.bfloat16),
            pltpu.VMEM(kv.shape[1:], jnp.bfloat16),
            pltpu.VMEM((VROWS, columns), jnp.float32),
            pltpu.VMEM((1, columns), jnp.float32),
            pltpu.SemaphoreType.DMA((2,)),
        ],
        compiler_params=pltpu.CompilerParams(vmem_limit_bytes=16 << 20),
        cost_estimate=pl.CostEstimate(
            flops=4 * 10**10, transcendentals=10**8, bytes_accessed=100 * 10**6
        ),
        name="attention",
    )(jnp.stack([lens[request], jnp.int32(request)]), in_hbm(qt), in_hbm(kv))


def out_kernel(
    src_ref, request_ref, gain_ref, rows_hbm, pair_0, near_0, far_0, pair_1, near_1, far_1, a_same,
    a_others, residual_hbm, normed_hbm, att_ref, w_ref, sum_ref, rows_ref, normed_ref, row_sem, out_sems, w_sems,
):
    cols = near_0.shape[1]
    sources = [
        (pair.at[:, pl.ds(0, cols)], near, pair.at[:, pl.ds(cols, cols)], far)
        for pair, near, far in ((pair_0, near_0, far_0), (pair_1, near_1, far_1))
    ]

    def w_load(side, i, source=near_0):
        return pltpu.make_async_copy(source, w_ref.at[side, i], w_sems.at[side, i])

    full_rows = rows_ref.shape[0]
    at = pl.multiple_of(request_ref[0] * full_rows, full_rows)
    load = pltpu.make_async_copy(rows_hbm.at[pl.ds(at, full_rows)], rows_ref, row_sem)
    for i in range(Z):
        w_load(0, i, sources[0][i]).start()
        w_load(1, i, sources[1][i]).start()
    load.start()
    for i in range(Z):
        att_ref[src_ref[i]] = a_same[i]
        att_ref[src_ref[Z + i]] = a_others[i]

    def columns(i, carry):
        attended = jnp.concatenate([att_ref[j] for j in range(2 * Z)], axis=1)
        w_load(0, i).wait()
        w_load(1, i).wait()
        sum_ref[src_ref[i]] = contract(attended, w_ref[0, i])
        sum_ref[src_ref[Z + i]] = contract(attended, w_ref[1, i])
        return carry

    lax.fori_loop(0, Z, columns, 0)
    load.wait()
    total = jnp.concatenate([sum_ref[i] for i in range(2 * Z)], axis=1)
    rows_ref[...] = (rows_ref[...].astype(jnp.float32) + total).astype(jnp.bfloat16)
    keep = pltpu.make_async_copy(rows_ref, residual_hbm, out_sems.at[0])
    keep.start()
    normed_ref[...] = mean_norm(rows_ref[...], gain_ref[...])
    give = pltpu.make_async_copy(normed_ref, normed_hbm, out_sems.at[1])
    give.start()
    keep.wait()
    give.wait()


def project_out(src, gain, weights, rows, pieces, request):
    piece_rows, piece_width = pieces[0].shape[1:]
    width = rows.shape[1]
    cols = weights[1].shape[1]
    scalar = pl.BlockSpec(memory_space=pltpu.SMEM)
    whole = pl.BlockSpec(memory_space=pltpu.VMEM)
    remote = pl.BlockSpec(memory_space=pltpu.HBM)
    return pl.pallas_call(
        out_kernel,
        out_shape=(pltpu.HBM((piece_rows, width), jnp.bfloat16),) * 2,
        in_specs=[scalar, scalar, whole] + [remote] * 7 + [whole] * 2,
        out_specs=(pl.BlockSpec(memory_space=pltpu.HBM),) * 2,
        scratch_shapes=[
            pltpu.VMEM((2 * Z, piece_rows, piece_width), jnp.bfloat16),
            pltpu.VMEM((2, Z, width, cols), jnp.bfloat16),
            pltpu.VMEM((2 * Z, piece_rows, cols), jnp.float32),
            pltpu.VMEM((piece_rows, width), jnp.bfloat16),
            pltpu.VMEM((piece_rows, width), jnp.bfloat16),
            pltpu.SemaphoreType.DMA,
            pltpu.SemaphoreType.DMA((2,)),
            pltpu.SemaphoreType.DMA((2, Z)),
        ],
        compiler_params=pltpu.CompilerParams(vmem_limit_bytes=27 << 20),
        cost_estimate=pl.CostEstimate(
            flops=4 * 10**9, transcendentals=0, bytes_accessed=16 * 10**6
        ),
        name="project_out",
    )(src, jnp.full((1,), request, jnp.int32), gain, in_hbm(rows), *map(in_hbm, weights), *pieces)


def ff_kernel(
    place_ref, low_hbm, high_hbm, w_ref, mine_ref, theirs_ref, x_ref, hidden_ref, x_sems
):
    shards, height, lanes = w_ref.shape
    width = x_ref.shape[3]
    units = hidden_ref.shape[1]
    rows = x_ref.shape[2]
    count = low_hbm.shape[0]
    row_at = pl.multiple_of(place_ref[1] * rows, rows)
    x_loads = []
    for i in range(2 * count):
        side = lax.rem(place_ref[0] + i % 2, 2)
        x_loads.append(
            pltpu.make_async_copy(
                (low_hbm, high_hbm)[i // count].at[i % count, pl.ds(row_at, rows)],
                x_ref.at[side, i // 2],
                x_sems.at[i],
            )
        )
    for copy in x_loads:
        copy.start()
    for copy in x_loads:
        copy.wait()
    x = x_ref[...].reshape(2 * Z * rows, width)
    for i in range(0, units, FF_PAIR):
        size = min(FF_PAIR, units - i)
        both = lax.dot_general(
            x,
            jnp.concatenate(
                [
                    jnp.concatenate([w_ref[j, at : at + size] for j in range(shards)], axis=1)
                    for at in (i, units + i)
                ],
                axis=0,
            ),
            (((1,), (1,)), ((), ())),
            preferred_element_type=jnp.float32,
        )
        hidden_ref[:, i : i + size] = (jax.nn.silu(both[:, :size]) * both[:, size:]).astype(
            jnp.bfloat16
        )
    hidden = hidden_ref[...]
    for i in range(0, shards, 2):
        down = jnp.concatenate([w_ref[i, 2 * units :], w_ref[i + 1, 2 * units :]], axis=1)
        terms = contract(hidden, down).astype(jnp.bfloat16).reshape(2, Z, rows, 2 * lanes)
        mine_ref[:, :, i * lanes : (i + 2) * lanes] = terms[0]
        theirs_ref[:, :, i * lanes : (i + 2) * lanes] = terms[1]


def feed_forward(place, low, high, weights, units):
    count, group_rows, width = low.shape
    rows = group_rows // 2
    whole = pl.BlockSpec(memory_space=pltpu.VMEM)
    remote = pl.BlockSpec(memory_space=pl.ANY)
    return pl.pallas_call(
        ff_kernel,
        out_shape=(jax.ShapeDtypeStruct((Z, rows, width), jnp.bfloat16),) * 2,
        in_specs=[pl.BlockSpec(memory_space=pltpu.SMEM), remote, remote, whole],
        out_specs=(whole, whole),
        scratch_shapes=[
            pltpu.VMEM((2, Z, rows, width), jnp.bfloat16),
            pltpu.VMEM((2 * count * rows, units), jnp.bfloat16),
            pltpu.SemaphoreType.DMA((2 * count,)),
        ],
        compiler_params=pltpu.CompilerParams(vmem_limit_bytes=12 << 20),
        cost_estimate=pl.CostEstimate(
            flops=5 * 10**9, transcendentals=10**6, bytes_accessed=16 * 10**6
        ),
        name="feed_forward",
    )(place, in_hbm(low), in_hbm(high), weights)


def angles_of(cached_len):
    half = HEAD_DIM // 2
    frequency = ROPE_BASE ** (-jnp.arange(half).astype(jnp.float32) * 2.0 / HEAD_DIM)
    positions = (cached_len[:, None] + jnp.arange(S_NEW)[None, :]).reshape(-1)
    angles = frequency[:, None] * positions.astype(jnp.float32)[None, :]
    return jnp.cos(angles), jnp.sin(angles)


def per_device(
    hidden_in, attn_gain, w_qkv, w_out, mlp_gain, w_gate, w_up, w_down, cache_kv, cached_len
):
    head_count = lax.axis_size("head")
    head_index = lax.axis_index("head")
    q_width = HEADS * HEAD_DIM
    kv_width = KV_HEADS * HEAD_DIM
    q_dev = q_width // head_count
    split_count = head_count // KV_HEADS
    part_index = head_index % split_count
    kv_head = head_index // split_count
    units = w_gate.shape[1]
    half_z = Z // 2
    row_count, width = hidden_in.shape

    src = sources()
    own = cache_kv[:, 0]
    other = exchange(own)
    columns = jnp.concatenate(
        [
            lax.dynamic_slice_in_dim(w_qkv, head_index * q_dev, q_dev, 1),
            lax.dynamic_slice_in_dim(w_qkv, q_width + kv_head * HEAD_DIM, HEAD_DIM, 1),
            lax.dynamic_slice_in_dim(w_qkv, q_width + kv_width + kv_head * HEAD_DIM, HEAD_DIM, 1),
        ],
        axis=1,
    )
    spread = jnp.broadcast_to(columns[None], (lax.axis_size("tok"), *columns.shape))
    spread, x_own = lax.optimization_barrier((spread, hidden_in))
    group_w = lax.all_to_all(spread, "tok", 0, 0, tiled=True).reshape(width, columns.shape[1])
    x_same = [x_own] + [along_z(x_own, d) for d in range(1, Z)]
    out_cols = width // head_count
    out_pair = lax.all_gather(
        jnp.concatenate(
            [
                lax.dynamic_slice_in_dim(w_out, block * out_cols, out_cols, 1)
                for block in (head_index, (head_index + half_z * 2) % head_count)
            ],
            axis=1,
        ),
        "tok", axis=0, tiled=True,
    )
    x_others = exchange(jnp.stack(x_same))
    ff_part, group_w, other, *_ = lax.optimization_barrier(
        (jnp.concatenate([w_gate.T, w_up.T, w_down], axis=0), group_w, other, *x_same)
    )
    ff_weights = lax.all_gather(ff_part, "tok", axis=0)
    cosine, sine = angles_of(cached_len)
    qt, kv, cache_new, rows = prepare(
        cached_len, part_index.reshape(1), src, attn_gain[None], cosine, sine, group_w,
        x_same, x_others, own, other,
    )
    out_pair, qt = lax.optimization_barrier((out_pair, qt))
    att_0 = attention(cached_len, 0, qt, kv)
    pair_other = exchange(out_pair)
    out_part = out_pair[:, :out_cols]
    out_far = [along_z(out_part, 1), along_z(out_part, Z - 1)]
    att_0, qt, pair_other, *out_far = lax.optimization_barrier((att_0, qt, pair_other, *out_far))
    out_pieces = (out_pair, *out_far, pair_other, *[exchange(piece) for piece in out_far])
    far_0 = [along_z(att_0, d) for d in range(1, Z)]
    att_1 = attention(cached_len, 1, qt, kv)
    att_1, att_0, *far_0 = lax.optimization_barrier((att_1, att_0, *far_0))
    same_0 = jnp.stack([att_0] + far_0)
    pieces_0 = (same_0, exchange(same_0))
    far_1 = [along_z(att_1, d) for d in range(1, Z)]
    gain = mlp_gain[None]
    residual_0, normed_0 = project_out(src, gain, out_pieces, rows, pieces_0, 0)
    att_1, residual_0, ff_weights, *far_1 = lax.optimization_barrier(
        (att_1, residual_0, ff_weights, *far_1)
    )
    same_1 = jnp.stack([att_1] + far_1)
    pieces_1 = (same_1, exchange(same_1))
    residual_1, normed_1 = project_out(src, gain, out_pieces, rows, pieces_1, 1)
    half_count = head_count // 2
    low = normed_0.reshape(half_count, row_count, width)
    high = normed_1.reshape(half_count, row_count, width)
    z = head_index // 2
    core = head_index % 2
    own_0 = lax.dynamic_index_in_dim(
        residual_0.reshape(half_count, row_count, width), head_index % half_count, 0, keepdims=False
    )
    own_1 = lax.dynamic_index_in_dim(
        residual_1.reshape(half_count, row_count, width), head_index % half_count, 0, keepdims=False
    )
    residual = jnp.where(head_index < half_count, own_0, own_1)
    outs = []
    for chunk in range(2):
        place = jnp.stack([core, jnp.int32(chunk)]).astype(jnp.int32)
        mine, theirs = feed_forward(place, low, high, ff_weights, units)
        theirs = exchange(theirs)

        def pair(chip):
            ours, others = (
                lax.dynamic_index_in_dim(part, chip % Z, 0, keepdims=False).astype(jnp.float32)
                for part in (mine, theirs)
            )
            return (ours + others).astype(jnp.bfloat16)

        rows_here = row_count // 2
        total = residual[chunk * rows_here : (chunk + 1) * rows_here].astype(jnp.float32)
        total = total + pair(z).astype(jnp.float32)
        for d in range(1, Z):
            total = total + along_z(pair(z + d), d).astype(jnp.float32)
        outs.append(total.astype(jnp.bfloat16))
    return (jnp.concatenate(outs), cache_new[:, None])


def solution(mesh):
    return jax.shard_map(
        per_device,
        mesh=mesh,
        in_specs=(
            P(("tok", "head"), None),
            P(),
            P("tok", None),
            P("tok", None),
            P(),
            P("tok", "head"),
            P("tok", "head"),
            P("head", "tok"),
            P("tok", "head", None, None),
            P("tok"),
        ),
        out_specs=(P(("tok", "head"), None), P("tok", "head", None, None)),
        check_vma=False,
    )
```
